32 devices in a mesh: scene: 8 (over y, x, core), seq: 4 (over z).
Axes of the slice: x: 2, y: 2, z: 4, core: 2. Of those that a mesh axis runs over, the one named last changes fastest.
Arguments:
- tokens: bfloat16 [24576, 1024], P(('scene', 'seq')), may hold values from -6 to 6
- image_count: int32 [8], P('scene'), may hold values from 576 to 2304, as said below
- norm_params: float32 [1024, 4], P('scene'), may hold values from -1.5 to 1.5, as said below
- w_qkv: float32 [1024, 3072], P('scene'), may hold values from -0.1875 to 0.1875
- w_proj: float32 [1024, 1024], P('scene'), may hold values from -6 to 6
- w_fc1: float32 [1024, 4096], P('scene'), may hold values from -0.1875 to 0.1875
- w_fc2: float32 [4096, 1024], P('scene'), may hold values from -0.09375 to 0.09375
- w_unpatch: float32 [1024, 128], P('scene'), may hold values from -0.1875 to 0.1875
- w_dec1: float32 [32, 64], replicated, may hold values from -0.375 to 0.375
- b_dec1: float32 [64], replicated, may hold values from -3 to 3
- w_dec2: float32 [64, 4], replicated, may hold values from -0.75 to 0.75
- cot_out: bfloat16 [24576, 1024], P(('scene', 'seq')), may hold values from -6 to 6
- cot_dec: bfloat16 [2048, 16], P(('scene', 'seq')), may hold values from -6 to 6
Outputs:
- block_out: bfloat16 [24576, 1024], P(('scene', 'seq'))
- decoded: float32 [2048, 16], P(('scene', 'seq'))
- grad_tokens: bfloat16 [24576, 1024], P(('scene', 'seq'))
- grad_norm_one: float32 [1024, 2], P('scene')
- grad_norm_two: float32 [1024, 2], P('scene')
- grad_qkv: float32 [1024, 3072], P('scene')
- grad_proj: float32 [1024, 1024], P('scene')
- grad_fc1: float32 [1024, 4096], P('scene')
- grad_fc2: float32 [4096, 1024], P('scene')
- grad_unpatch: float32 [1024, 128], P('scene')
- grad_dec1: float32 [32, 64], replicated
- grad_bdec1: float32 [64], replicated
- grad_dec2: float32 [64, 4], replicated
The draws below stay inside these ranges and needn't reach their ends.
Inputs may be any that keep to these rules, and one draw needn't show every extreme that they name: `image_count`: each scene has either 576 or 2304 image tokens, and some scene has each. `norm_params`: columns 0 and 2 are gains, columns 1 and 3 biases.
All inputs are finite; a program needn't handle non-finite values.
Results may differ from the reference program's by a relative error of at most 0.028.
The reference program's roundings to bfloat16 on the way count: a program that leaves them out, or rounds other values in their place, can miss the bound.
Values may be sent and summed in bfloat16 or wider, within the bound.
No kernel may reach another device: no remote copies, remote signals or barrier semaphores. Data moves between devices by JAX's collectives and lax.ppermute only.
A program may use at most 256 MiB of HBM per device.

```python
import jax
import jax.numpy as jnp
from jax import lax

D = 1024
H = 16
HD = 64
FF = 4096
TF = 32
PP = 4
DH = 64
OUT = 4
TG = 16
IMG_DEV = 576
TRI = 768
TOK_DEV = 768
CAP = 3072
IMG_BIG = 2304
IMG_SMALL = 576
SCENES = 8
TOKENS = 24576
POINTS = 2048


def draw_image_count(key, part):
    big_roll = jax.random.randint(jax.random.fold_in(key, 11), (SCENES,), 0, 11)
    big_pick = jax.random.randint(jax.random.fold_in(key, 12), (), 0, SCENES)
    small_step = jax.random.randint(jax.random.fold_in(key, 13), (), 1, SCENES)
    small_pick = (big_pick + small_step) % SCENES
    slots = jnp.arange(SCENES, dtype=jnp.int32)
    is_big = ((big_roll < 8) | (slots == big_pick)) & (slots != small_pick)
    return jnp.where(is_big, IMG_BIG, IMG_SMALL).astype(jnp.int32)


def draw_norm_params(key, part):
    gain_draw = jax.random.uniform(jax.random.fold_in(key, 21), (D, 2), jnp.float32, 0.6, 1.4)
    shift_draw = jnp.clip(0.5 * jax.random.normal(jax.random.fold_in(key, 22), (D, 2), jnp.float32), -1.5, 1.5)
    return jnp.stack([gain_draw[:, 0], shift_draw[:, 0], gain_draw[:, 1], shift_draw[:, 1]], axis=1)


def strengthened(values, key, source, target, parts, factor):
    def block_of(dim):
        return (jnp.arange(values.shape[dim]) // (values.shape[dim] // parts)).reshape((-1,) + (1,) * (values.ndim - 1 - dim))

    near = jax.random.permutation(key, parts)[block_of(target)]
    far = (block_of(target) + parts // 2) % parts
    return jnp.where((block_of(source) == near) | (block_of(source) == far), factor * values, values)


def levels(stream_key, shape, split, smallest, largest):
    level = 1.0
    for dim, blocks in split:
        draws = jax.random.uniform(jax.random.fold_in(jax.random.fold_in(stream_key, 6), dim), (blocks,), jnp.float32, smallest / len(split), largest / len(split))
        level = level * jnp.repeat(jnp.exp(draws), shape[dim] // blocks).reshape((-1,) + (1,) * (len(shape) - 1 - dim))
    return level


def normal_values(stream_key, shape, scale, bound, split=(), kind=jnp.bfloat16):
    values = jax.random.normal(stream_key, shape, jnp.float32) * scale
    if len(split) > 0:
        values = levels(stream_key, shape, split, -0.22, 0.18) * values
    return jnp.clip(values, min=-bound, max=bound).astype(kind)


def bell_draw_with(rng, extent, scale, bound, pieces, heavy, kind=jnp.bfloat16):
    values = scale * jax.random.normal(rng, extent, jnp.float32)
    if pieces:
        values = values * levels(rng, extent, pieces, -0.22, 0.18)
    return jnp.clip(strengthened(values, jax.random.fold_in(rng, 3), *heavy), -bound, bound).astype(kind)


def setup_inputs(seed: int = 0) -> dict:
    splits = jax.random.split(jax.random.key(seed), 14)
    tokens = bell_draw_with(splits[0], (TOKENS, D), 1.0, 6.0, ((0, 32),), (0, 1, 32, 2.75))
    image_count = draw_image_count(jax.random.fold_in(splits[13], 71), 0)
    norm_params = draw_norm_params(jax.random.fold_in(splits[13], 71), 0)
    w_qkv = normal_values(splits[3], (D, 3 * D), D ** -0.5, 0.1875, ((0, 8),), jnp.float32)
    w_proj = normal_values(splits[4], (D, D), (4 * D // CAP) ** -0.5, 6.0, ((0, 8),), jnp.float32)
    w_fc1 = normal_values(splits[5], (D, FF), D ** -0.5, 0.1875, ((0, 8),), jnp.float32)
    w_fc2 = normal_values(splits[6], (FF, D), FF ** -0.5, 0.09375, ((0, 8),), jnp.float32)
    w_unpatch = normal_values(splits[7], (D, PP * TF), D ** -0.5, 0.1875, ((0, 8),), jnp.float32)
    w_dec1 = normal_values(splits[8], (TF, DH), (8 * TF) ** -0.5, 0.375, (), jnp.float32)
    b_dec1 = normal_values(splits[9], (DH,), 0.5, 3.0, (), jnp.float32)
    w_dec2 = normal_values(splits[10], (DH, OUT), DH ** -0.5, 0.75, (), jnp.float32)
    cot_out = normal_values(splits[11], (TOKENS, D), 1.0, 6.0, ((0, 32),))
    cot_dec = normal_values(splits[12], (POINTS, OUT * PP), 1.0, 6.0, ((0, 32),))
    return dict(tokens=tokens, image_count=image_count, norm_params=norm_params, w_qkv=w_qkv, w_proj=w_proj, w_fc1=w_fc1, w_fc2=w_fc2, w_unpatch=w_unpatch, w_dec1=w_dec1, b_dec1=b_dec1, w_dec2=w_dec2, cot_out=cot_out, cot_dec=cot_dec)


@jax.custom_vjp
def low(v):
    return lax.optimization_barrier(v.astype(jnp.bfloat16)).astype(jnp.float32)

@jax.custom_vjp
def low_back(v):
    return v

def low_keep(v):
    return (low(v), None)

def low_pass(kept, grad):
    return (grad,)

def back_keep(v):
    return (v, None)

def back_low(kept, grad):
    return (low(grad),)
low.defvjp(low_keep, low_pass)
low_back.defvjp(back_keep, back_low)

def matmul_hi(left, right):
    return jnp.dot(left, right, precision=lax.Precision.HIGHEST, preferred_element_type=jnp.float32)

def layer_norm(rows_in, gain, shift):
    center = rows_in - lax.optimization_barrier(jnp.mean(rows_in, axis=-1, keepdims=True))
    spread = lax.optimization_barrier(jnp.mean(center * center, axis=-1, keepdims=True))
    return center * lax.rsqrt(spread + 1e-05) * gain + shift

def gelu_exact(values_in):
    return jax.nn.gelu(values_in, approximate=False)

def split_heads(rows_in):
    return rows_in.reshape(rows_in.shape[0], H, HD).transpose(1, 0, 2)

def scene_forward(scene_in, image_total, norm_params, w_qkv, w_proj, w_fc1, w_fc2, w_unpatch, w_dec1, b_dec1, w_dec2):
    norm_low = low(norm_params)
    position = jnp.arange(CAP, dtype=jnp.int32) % TOK_DEV
    row_live = (position >= IMG_DEV) | (position < image_total // (CAP // TOK_DEV))
    normed_one = low(layer_norm(scene_in, norm_low[:, 0], norm_low[:, 1]))
    qkv_rows = low_back(low(matmul_hi(normed_one, low(w_qkv))))
    queries = split_heads(qkv_rows[:, :D])
    key_heads = split_heads(qkv_rows[:, D:2 * D])
    value_heads = split_heads(qkv_rows[:, 2 * D:])
    blocks = queries.reshape(H, CAP // TOK_DEV, TOK_DEV, HD).transpose(1, 0, 2, 3)

    def attend(block):
        scores = jnp.einsum('hqd,hkd->hqk', block, key_heads, precision=lax.Precision.HIGHEST)
        scores = low_back(scores * HD ** (-0.5))
        scores = jnp.where(row_live[None, None, :], scores, -1e+30)
        row_peak = lax.optimization_barrier(jnp.max(scores, axis=2, keepdims=True))
        exponent = jnp.exp(scores - row_peak)
        attn_probs = exponent / lax.optimization_barrier(jnp.sum(exponent, axis=2, keepdims=True))
        return jnp.einsum('hqk,hkd->hqd', low(attn_probs), value_heads, precision=lax.Precision.HIGHEST)
    mixed_rows = lax.map(jax.checkpoint(attend), blocks)
    mixed_rows = mixed_rows.transpose(1, 0, 2, 3).reshape(H, CAP, HD).transpose(1, 0, 2).reshape(CAP, D)
    mixed_rows = low_back(low(mixed_rows))
    middle = scene_in + low_back(matmul_hi(mixed_rows, low(w_proj)))
    normed_two = low(layer_norm(middle, norm_low[:, 2], norm_low[:, 3]))
    pre_act = low_back(matmul_hi(normed_two, low(w_fc1)))
    activated = low(gelu_exact(pre_act))
    result = jnp.where(row_live[:, None], middle + low_back(matmul_hi(activated, low(w_fc2))), 0.0)
    triplane = low(result.reshape(CAP // TOK_DEV, TOK_DEV, D)[:, IMG_DEV:, :].reshape(TRI, D))
    planes = low_back(low(matmul_hi(triplane, low(w_unpatch))))
    cell_count = TG * TG
    features = planes[:cell_count] + planes[cell_count:2 * cell_count] + planes[2 * cell_count:]
    features = features.reshape(cell_count * PP, TF)
    hidden = gelu_exact(matmul_hi(features, w_dec1) + b_dec1)
    decoded = matmul_hi(hidden, w_dec2).reshape(cell_count, PP, OUT).transpose(0, 2, 1).reshape(cell_count, OUT * PP)
    return (result, decoded)

def reference(tokens, image_count, norm_params, w_qkv, w_proj, w_fc1, w_fc2, w_unpatch, w_dec1, b_dec1, w_dec2, cot_out, cot_dec):
    params = (norm_params, w_qkv, w_proj, w_fc1, w_fc2, w_unpatch, w_dec1, b_dec1, w_dec2)
    scene_rows = tokens.astype(jnp.float32).reshape(SCENES, CAP, D)
    scene_cots = cot_out.astype(jnp.float32).reshape(SCENES, CAP, D)
    cell_cots = cot_dec.astype(jnp.float32).reshape(SCENES, TG * TG, OUT * PP)

    def one_scene(totals, inputs):
        scene_in, image_total, row_cot, cell_cot = inputs

        def scene_fn(rows_arg, *weights):
            return scene_forward(rows_arg, image_total, *weights)
        (result, decoded), pull = jax.vjp(scene_fn, scene_in, *params)
        grads = pull((row_cot, cell_cot))
        totals = tuple((running + fresh for running, fresh in zip(totals, grads[1:])))
        return (totals, (result, decoded, grads[0]))
    zeros = tuple((jnp.zeros(weight.shape, jnp.float32) for weight in params))
    totals, (results, decodes, row_grads) = lax.scan(one_scene, zeros, (scene_rows, image_count, scene_cots, cell_cots))
    return (results.reshape(TOKENS, D).astype(jnp.bfloat16), decodes.reshape(POINTS, OUT * PP), row_grads.reshape(TOKENS, D).astype(jnp.bfloat16), totals[0][:, :2], totals[0][:, 2:], totals[1], totals[2], totals[3], totals[4], totals[5], totals[6], totals[7], totals[8])
```

```python
import functools

import jax
import jax.numpy as jnp
from jax import lax
from jax.experimental import pallas as pl
from jax.experimental.pallas import tpu as pltpu
from jax.sharding import PartitionSpec as P

H = 16
TF = 32
PP = 4
OUT = 4
TG = 16
IMG_DEV = 576

EPS = 1e-05
NEG_FILL = -1e30
LOG2E = 1.4426950408889634
VMEM_BYTES = 60 * 2**20

NT = (((1,), (1,)), ((), ()))
NN = (((1,), (0,)), ((), ()))
TN = (((0,), (0,)), ((), ()))


def mxu(left, right, dims):
    return lax.dot_general(left, right, dims, preferred_element_type=jnp.float32)


def exact(left, right, dims):
    return lax.dot_general(
        left, right, dims, precision=lax.Precision.HIGHEST, preferred_element_type=jnp.float32
    )


def gelu_parts(v):
    a = jnp.abs(v) * 0.7071067811865476
    t = 1.0 / (1.0 + 0.3275911 * a)
    poly = t * (
        0.254829592
        + t * (-0.284496736 + t * (1.421413741 + t * (-1.453152027 + t * 1.061405429)))
    )
    e = jnp.exp(-a * a)
    tail = 0.5 * poly * e
    cdf = jnp.where(v >= 0.0, 1.0 - tail, tail)
    return v * cdf, cdf + v * (e * 0.3989422804014327)


def pair_keys(block, bias, head, half):
    lane = lax.broadcasted_iota(jnp.int32, block.shape, 1)
    mine = (lane < half) if head == 0 else (lane >= half)
    flag = half if head == 0 else 0
    zero = jnp.zeros_like(block)
    return jnp.where(mine, block, jnp.where(lane == flag, bias, zero))


def pair_queries(block, head, half):
    lane = lax.broadcasted_iota(jnp.int32, block.shape, 1)
    mine = (lane < half) if head == 0 else (lane >= half)
    flag = half if head == 0 else 0
    zero = jnp.zeros_like(block)
    return jnp.where(mine, block, jnp.where(lane == flag, jnp.ones_like(block), zero))


def pair_mask(block, head, half):
    lane = lax.broadcasted_iota(jnp.int32, block.shape, 1)
    mine = (lane < half) if head == 0 else (lane >= half)
    return jnp.where(mine, block, jnp.zeros_like(block))


def attn_fwd_kernel(*refs, n, scale):
    q_ref, bias_ref = refs[0], refs[1]
    k_refs, v_refs = refs[2 : 2 + n], refs[2 + n : 2 + 2 * n]
    o_ref, lse_ref, s_buf, k_buf, vt_buf, acc_buf = refs[2 + 2 * n :]
    tq = q_ref.shape[0]
    tk = k_refs[0].shape[0]
    half = q_ref.shape[1] // 2
    ext = half + 16
    q = q_ref[...]
    qs = [pair_queries(q, h, half) for h in range(2)]
    bias = bias_ref[...]
    ones = jnp.ones((16, tk), jnp.bfloat16)
    for i in range(n):
        kb = k_refs[i][...]
        vt = v_refs[i][...].T
        for h in range(2):
            k_buf[i, h] = pair_keys(kb, bias, h, half)
            vt_buf[i, h, :half] = vt[h * half : h * half + half]
            vt_buf[i, h, half:] = ones

    def score(j, slot, peak):
        out = []
        for h in range(2):
            s = mxu(k_buf[j, h], qs[h], NT)
            s_buf[slot, h] = s
            out.append(jnp.maximum(peak[h], jnp.max(s, axis=0, keepdims=True)))
        return out

    def mix(j, slot, before, peak):
        for h in range(2):
            fade = jnp.exp2((before[h] - peak[h]) * scale)
            p = jnp.exp2((s_buf[slot, h] - peak[h]) * scale).astype(jnp.bfloat16)
            acc_buf[h] = acc_buf[h] * fade + mxu(vt_buf[j, h], p, NN)

    start = [jnp.full((1, tq), -3e38, jnp.float32)] * 2
    acc_buf[...] = jnp.zeros(acc_buf.shape, jnp.float32)
    first = score(0, 0, start)

    def body(j, carry):
        before, peak = carry
        fresh = score(j, lax.rem(j, 2), peak)
        mix(j - 1, lax.rem(j - 1, 2), before, peak)
        return (peak, fresh)

    before, peak = lax.fori_loop(1, n, body, (start, first))
    mix(n - 1, (n - 1) % 2, before, peak)
    outs = []
    for h in range(2):
        acc = acc_buf[h]
        total = acc[half : half + 1]
        outs.append(acc[:half] / total)
        lse_ref[h : h + 1, :] = peak[h] * scale + jnp.log2(total)
    o_ref[...] = jnp.concatenate(outs, axis=0).T.astype(jnp.bfloat16)


def attn_fwd(q_rows, kv_rows, bias, head_dim):
    n = len(kv_rows)
    tq, width = q_rows.shape[0], kv_rows[0].shape[1] // 2
    tk = kv_rows[0].shape[0]
    lanes = 2 * head_dim
    pairs = width // lanes
    scale = head_dim**-0.5 * LOG2E
    block = lambda rows, off: pl.BlockSpec((rows, lanes), lambda h: (0, h + off))
    flops = 4 * tq * tk * n * width
    return pl.pallas_call(
        functools.partial(attn_fwd_kernel, n=n, scale=scale),
        grid=(pairs,),
        in_specs=[block(tq, 0), pl.BlockSpec((tk, lanes), lambda h: (0, 0))]
        + [block(tk, 0)] * n
        + [block(tk, pairs)] * n,
        out_specs=(block(tq, 0), pl.BlockSpec((None, 2, tq), lambda h: (h, 0, 0))),
        out_shape=(
            jax.ShapeDtypeStruct((tq, width), jnp.bfloat16),
            jax.ShapeDtypeStruct((pairs, 2, tq), jnp.float32),
        ),
        scratch_shapes=[
            pltpu.VMEM((2, 2, tk, tq), jnp.float32),
            pltpu.VMEM((n, 2, tk, lanes), jnp.bfloat16),
            pltpu.VMEM((n, 2, head_dim + 16, tk), jnp.bfloat16),
            pltpu.VMEM((2, head_dim + 16, tq), jnp.float32),
        ],
        compiler_params=pltpu.CompilerParams(vmem_limit_bytes=VMEM_BYTES),
        cost_estimate=pl.CostEstimate(
            flops=flops * 4, bytes_accessed=2 * width * (2 * tq + 2 * n * tk), transcendentals=0
        ),
        name="attn_fwd",
    )(q_rows, bias, *kv_rows, *kv_rows)


def attn_bwd_kernel(
    q_ref, k_ref, v_ref, do_ref, lse_ref, del_ref, bias_ref,
    dq_ref, dk_ref, dv_ref,
    s_buf, dp_buf, qm, km, dom, kt, qt, dot, dqa, dka, dva, *, tk, tq, scale, post
):
    nq = q_ref.shape[0] // tq
    nk = k_ref.shape[0] // tk
    half = q_ref.shape[1] // 2
    for i in range(nk):
        rows = slice(i * tk, i * tk + tk)
        for h in range(2):
            km[h, rows] = pair_keys(k_ref[rows, :], bias_ref[...], h, half)
    for h in range(2):
        qm[h] = pair_queries(q_ref[...], h, half)
        dom[h] = pair_mask(do_ref[...], h, half)
    kt[...] = k_ref[...].T
    qt[...] = q_ref[...].T
    dot[...] = do_ref[...].T
    for acc in (dqa, dka, dva):
        acc[...] = jnp.zeros(acc.shape, jnp.float32)

    def place(t):
        if isinstance(t, int):
            return t // nq * tk, t % nq * tq, t % 2
        return (
            pl.multiple_of(lax.div(t, nq) * tk, tk),
            pl.multiple_of(lax.rem(t, nq) * tq, tq),
            lax.rem(t, 2),
        )

    def score(t):
        k0, q0, slot = place(t)
        ks, qs = pl.ds(k0, tk), pl.ds(q0, tq)
        vv = v_ref[ks, :]
        for h in range(2):
            s_buf[slot, h] = mxu(km[h, ks, :], qm[h, qs, :], NT)
            dp_buf[slot, h] = mxu(vv, dom[h, qs, :], NT)

    def grads(t):
        k0, q0, slot = place(t)
        ks, qs = pl.ds(k0, tk), pl.ds(q0, tq)
        for h in range(2):
            p = jnp.exp2(s_buf[slot, h] * scale - lse_ref[h : h + 1, qs])
            ds = (p * (dp_buf[slot, h] - del_ref[h : h + 1, qs])).astype(jnp.bfloat16)
            pb = p.astype(jnp.bfloat16)
            r = slice(half * h, half * h + half)
            dqa[r, qs] += mxu(kt[r, ks], ds, NN)
            dva[r, ks] += mxu(dot[r, qs], pb, NT)
            dka[r, ks] += mxu(qt[r, qs], ds, NT)

    score(0)

    def body(t, carry):
        score(t)
        grads(t - 1)
        return carry

    lax.fori_loop(1, nq * nk, body, 0)
    grads(nq * nk - 1)
    dq_ref[...] = (dqa[...] * post).T.astype(jnp.bfloat16)
    dk_ref[...] = (dka[...] * post).T.astype(jnp.bfloat16)
    dv_ref[...] = dva[...].T.astype(jnp.bfloat16)


def attn_bwd(q, k, v, do, lse, delta, bias, head_dim):
    rows, width = q.shape
    tk = bias.shape[0]
    tq = tk
    lanes = 2 * head_dim
    pairs = width // lanes
    block = pl.BlockSpec((rows, lanes), lambda h: (0, h))
    stat = pl.BlockSpec((None, 2, rows), lambda h: (h, 0, 0))
    return pl.pallas_call(
        functools.partial(
            attn_bwd_kernel, tk=tk, tq=tq, scale=head_dim**-0.5 * LOG2E, post=head_dim**-0.5
        ),
        grid=(pairs,),
        in_specs=[block] * 4 + [stat] * 2 + [pl.BlockSpec((tk, lanes), lambda h: (0, 0))],
        out_specs=(block,) * 3,
        out_shape=(jax.ShapeDtypeStruct((rows, width), jnp.bfloat16),) * 3,
        scratch_shapes=[
            pltpu.VMEM((2, 2, tk, tq), jnp.float32),
            pltpu.VMEM((2, 2, tk, tq), jnp.float32),
            pltpu.VMEM((2, rows, lanes), jnp.bfloat16),
            pltpu.VMEM((2, rows, lanes), jnp.bfloat16),
            pltpu.VMEM((2, rows, lanes), jnp.bfloat16),
            pltpu.VMEM((lanes, rows), jnp.bfloat16),
            pltpu.VMEM((lanes, rows), jnp.bfloat16),
            pltpu.VMEM((lanes, rows), jnp.bfloat16),
            pltpu.VMEM((lanes, rows), jnp.float32),
            pltpu.VMEM((lanes, rows), jnp.float32),
            pltpu.VMEM((lanes, rows), jnp.float32),
        ],
        compiler_params=pltpu.CompilerParams(vmem_limit_bytes=VMEM_BYTES),
        cost_estimate=pl.CostEstimate(
            flops=10 * rows * rows * width * 4, bytes_accessed=14 * rows * width, transcendentals=0
        ),
        name="attn_bwd",
    )(q, k, v, do, lse, delta, bias)


def fc1_kernel(x_ref, w_ref, act_ref, slope_ref):
    act, slope = gelu_parts(mxu(x_ref[...], w_ref[...], NN))
    act_ref[...] = act.astype(jnp.bfloat16)
    slope_ref[...] = slope.astype(jnp.bfloat16)


def fc1_gelu(x, w):
    rows, depth = x.shape
    cols = w.shape[1]
    tile = 512
    spec = pl.BlockSpec((rows, tile), lambda i: (0, i))
    return pl.pallas_call(
        fc1_kernel,
        grid=(cols // tile,),
        in_specs=[
            pl.BlockSpec((rows, depth), lambda i: (0, 0)),
            pl.BlockSpec((depth, tile), lambda i: (0, i)),
        ],
        out_specs=(spec, spec),
        out_shape=(jax.ShapeDtypeStruct((rows, cols), jnp.bfloat16),) * 2,
        compiler_params=pltpu.CompilerParams(vmem_limit_bytes=VMEM_BYTES),
        cost_estimate=pl.CostEstimate(
            flops=2 * rows * cols * depth,
            bytes_accessed=2 * (rows * depth + depth * cols + 2 * rows * cols),
            transcendentals=0,
        ),
        name="fc1_gelu",
    )(x, w)


def normalize(v):
    center = v - jnp.mean(v, axis=-1, keepdims=True)
    spread = jnp.mean(center * center, axis=-1, keepdims=True)
    inv = lax.rsqrt(spread + EPS)
    return center * inv, inv


def norm_back(g, u, inv, gain):
    q = g * gain
    back = inv * (
        q - jnp.mean(q, axis=-1, keepdims=True) - u * jnp.mean(q * u, axis=-1, keepdims=True)
    )
    return back, jnp.sum(g * u, axis=0), jnp.sum(g, axis=0)


def per_device(
    tokens,
    image_count,
    norm_params,
    w_qkv,
    w_proj,
    w_fc1,
    w_fc2,
    w_unpatch,
    w_dec1,
    b_dec1,
    w_dec2,
    cot_out,
    cot_dec,
):
    seq_count = lax.axis_size("seq")
    rank = lax.axis_index("seq")
    scene_rank = lax.axis_index("scene")
    tok_rows, width = tokens.shape
    head_dim = width // H
    cols = width // seq_count
    cells = TG * TG
    bf16, f32 = jnp.bfloat16, jnp.float32
    live_image = image_count[0] // seq_count
    pos = jnp.arange(tok_rows, dtype=jnp.int32)
    row_live = (pos >= IMG_DEV) | (pos < live_image)
    bias = jnp.broadcast_to(
        jnp.where(row_live, 0.0, NEG_FILL).astype(bf16)[:, None], (tok_rows, 2 * head_dim)
    )

    def hop(x, step):
        return lax.ppermute(
            x, "seq", [(i, i + step) for i in range(seq_count) if 0 <= i + step < seq_count]
        )

    def turn(x, step):
        return lax.ppermute(x, "seq", [(i, (i + step) % seq_count) for i in range(seq_count)])

    def slot_of(chunk):
        return jnp.where(chunk <= rank, rank - chunk, chunk)

    ups, downs = [tokens], [tokens]
    for _ in range(seq_count - 1):
        ups.append(hop(ups[-1], 1))
        downs.append(hop(downs[-1], -1))
    slots = [tokens]
    for d in range(1, seq_count):
        pick = ups[d]
        for r in range(d):
            pick = jnp.where(rank == r, downs[d - r], pick)
        slots.append(pick)

    def gather(w):
        return lax.all_gather(w.astype(bf16), "scene", axis=0, tiled=True)

    small = gather(
        jnp.concatenate(
            [w_unpatch, norm_params, jnp.zeros((w_unpatch.shape[0], 124), f32)], axis=1
        )
    )
    unpatch_w = small[:, : PP * TF]
    norm_full = small[:, PP * TF : PP * TF + 4].astype(f32)
    gain_one, shift_one, gain_two, shift_two = (norm_full[:, i] for i in range(4))
    qkv_w = gather(w_qkv)
    proj_w = gather(w_proj)
    fc1_w = gather(w_fc1)
    fc2_w = gather(w_fc2)
    cot_cells = lax.all_gather(cot_dec, "seq", axis=0, tiled=True)

    def own_cols(base):
        return lax.dynamic_slice_in_dim(qkv_w, base * width + rank * cols, cols, 1)

    own_w = [own_cols(i) for i in range(3)]
    a1 = []
    kv_rows, head_q, head_k, head_v = [], [], [], []
    for d in range(seq_count):
        u, _ = normalize(slots[d].astype(f32))
        a = (u * gain_one + shift_one).astype(bf16)
        a1.append(a)
        if d == 0:
            q_rows = mxu(a, qkv_w[:, :width], NN).astype(bf16)
        kv = mxu(a, qkv_w[:, width:], NN).astype(bf16)
        kv_rows.append(kv)
        if d == 0:
            head_q.append(lax.dynamic_slice_in_dim(q_rows, rank * cols, cols, 1))
        else:
            head_q.append(mxu(a, own_w[0], NN).astype(bf16))
        head_k.append(lax.dynamic_slice_in_dim(kv, rank * cols, cols, 1))
        head_v.append(lax.dynamic_slice_in_dim(kv, width + rank * cols, cols, 1))
    mixed, lse = attn_fwd(q_rows, kv_rows, bias, head_dim)
    lse = lse.reshape(H, tok_rows)

    inputs_f = tokens.astype(f32)
    middle = inputs_f + mxu(mixed, proj_w, NN)
    u_two, inv_two = normalize(middle)
    a2 = (u_two * gain_two + shift_two).astype(bf16)
    act, slope = fc1_gelu(a2, fc1_w)
    result = jnp.where(row_live[:, None], middle + mxu(act, fc2_w, NN), 0.0)
    block_out = result.astype(bf16)

    triplane = block_out[IMG_DEV:]
    planes = mxu(triplane, unpatch_w, NN).astype(bf16)
    all_planes = lax.all_gather(planes, "seq", axis=0, tiled=True).astype(f32)
    feat = all_planes[:cells] + all_planes[cells : 2 * cells] + all_planes[2 * cells :]
    dh = w_dec1.shape[1]
    eye = jnp.eye(PP, dtype=f32)
    dec1 = jnp.einsum("fh,pq->pfqh", w_dec1, eye).reshape(PP * TF, PP * dh)
    dec2 = jnp.einsum("ho,pq->phoq", w_dec2, eye).reshape(PP * dh, OUT * PP)
    hidden_pre = exact(feat, dec1, NN) + jnp.tile(b_dec1, PP)
    zdec, zslope = gelu_parts(hidden_pre)
    decoded_all = exact(zdec, dec2, NN)
    cells_dev = cells // seq_count
    decoded = lax.dynamic_slice_in_dim(decoded_all, rank * cells_dev, cells_dev, 0)
    cot_f = cot_cells.astype(f32)
    grad_hidden = exact(cot_f, dec2, NT) * zslope
    gfeat = exact(grad_hidden, dec1, NT).astype(bf16)
    grad_w2 = jnp.einsum(
        "phop->ho", exact(zdec, cot_f, TN).reshape(PP, dh, OUT, PP)
    )
    grad_b1 = jnp.sum(jnp.sum(grad_hidden, axis=0).reshape(PP, dh), axis=0)
    grad_w1 = jnp.einsum(
        "pfph->fh", exact(feat, grad_hidden, TN).reshape(PP, TF, PP, dh)
    )
    tri_rows = tok_rows - IMG_DEV
    plane_grad = lax.dynamic_slice_in_dim(
        jnp.concatenate([gfeat] * 4, axis=0), lax.rem(rank * tri_rows, cells), tri_rows, 0
    )
    grad_unpatch = mxu(triplane, plane_grad, TN)
    grad_tri = mxu(plane_grad, unpatch_w, NT)

    grad_result = jnp.where(row_live[:, None], cot_out.astype(f32), 0.0)
    grad_result = jnp.concatenate([grad_result[:IMG_DEV], grad_result[IMG_DEV:] + grad_tri], axis=0)
    branch = grad_result.astype(bf16)
    grad_pre = (mxu(branch, fc2_w, NT) * slope.astype(f32)).astype(bf16)
    back_two, gain_grad_two, shift_grad_two = norm_back(
        mxu(grad_pre, fc1_w, NT), u_two, inv_two, gain_two
    )
    grad_mid = grad_result + back_two
    mid_grad = grad_mid.astype(bf16)
    grad_mixed = mxu(mid_grad, proj_w, NT).astype(bf16)

    head_of = (jnp.arange(width) // head_dim)[None, :] == jnp.arange(H)[:, None]
    delta = exact(
        head_of.astype(f32), grad_mixed.astype(f32) * mixed.astype(f32), NT
    )
    heads_dev = H // seq_count
    stats = jnp.concatenate(
        [lse.reshape(seq_count, heads_dev, tok_rows), delta.reshape(seq_count, heads_dev, tok_rows)],
        axis=1,
    )

    def piece(x, chunk, size, axis):
        return lax.dynamic_slice_in_dim(x, chunk * size, size, axis)

    do_all = jnp.zeros((seq_count * tok_rows, cols), bf16)
    stat_all = jnp.zeros((2 * heads_dev, seq_count * tok_rows), f32)
    for d in range(seq_count):
        to = lax.rem(rank + d, seq_count)
        got = piece(grad_mixed, to, cols, 1)
        got_stat = lax.dynamic_index_in_dim(stats, to, 0, keepdims=False)
        if d:
            got, got_stat = turn(got, d), turn(got_stat, d)
        at = slot_of(lax.rem(rank - d + seq_count, seq_count)) * tok_rows
        do_all = lax.dynamic_update_slice_in_dim(do_all, got, at, 0)
        stat_all = lax.dynamic_update_slice_in_dim(stat_all, got_stat, at, 1)
    pairs_dev = heads_dev // 2
    dq, dk, dv = attn_bwd(
        jnp.concatenate(head_q, axis=0),
        jnp.concatenate(head_k, axis=0),
        jnp.concatenate(head_v, axis=0),
        do_all,
        stat_all[:heads_dev].reshape(pairs_dev, 2, seq_count * tok_rows),
        stat_all[heads_dev:].reshape(pairs_dev, 2, seq_count * tok_rows),
        bias,
        head_dim,
    )
    head_grads = jnp.concatenate([dq, dk, dv], axis=1)

    row_grads = jnp.zeros((3, tok_rows, width), bf16)
    for d in range(seq_count):
        to = lax.rem(rank + d, seq_count)
        got = piece(head_grads, slot_of(to), tok_rows, 0)
        if d:
            got = turn(got, d)
        source = lax.rem(rank - d + seq_count, seq_count)
        row_grads = lax.dynamic_update_slice(
            row_grads,
            got.reshape(tok_rows, 3, cols).transpose(1, 0, 2),
            (0, 0, source * cols),
        )
    grad_in = sum(
        mxu(row_grads[i], qkv_w[:, i * width : (i + 1) * width], NT) for i in range(3)
    )
    u_one, inv_one = normalize(inputs_f)
    back_one, gain_grad_one, shift_grad_one = norm_back(grad_in, u_one, inv_one, gain_one)
    grad_tokens = (grad_mid + back_one).astype(bf16)

    def over_scene(g):
        return lax.psum_scatter(g.astype(bf16), "scene", scatter_dimension=0, tiled=True)

    def over_seq(part):
        size = part.shape[1] // seq_count
        total = piece(part, rank, size, 1).astype(f32)
        for d in range(1, seq_count):
            to = lax.rem(rank + d, seq_count)
            total = total + turn(piece(part, to, size, 1), d).astype(f32)
        return over_cols(total.astype(bf16))

    def over_cols(mine):
        size = mine.shape[1]
        out = jnp.zeros((mine.shape[0], size * seq_count), f32)
        for d in range(seq_count):
            got = turn(mine, d) if d else mine
            source = lax.rem(rank - d + seq_count, seq_count)
            out = lax.dynamic_update_slice_in_dim(out, got.astype(f32), source * size, 1)
        return out

    fc2_part = over_scene(mxu(act, branch, TN))
    fc1_part = over_scene(mxu(a2, grad_pre, TN))
    proj_part = over_scene(
        jnp.concatenate([mxu(mixed, mid_grad, TN).astype(bf16), grad_unpatch.astype(bf16)], axis=1)
    )
    grad_fc2 = over_seq(fc2_part)
    grad_fc1 = over_seq(fc1_part)
    grad_proj_all = over_seq(
        jnp.pad(proj_part, ((0, 0), (0, 128 * seq_count - PP * TF)))
    )
    grad_proj = grad_proj_all[:, :width]
    grad_unp = grad_proj_all[:, width : width + PP * TF]
    own_qkv = mxu(jnp.concatenate(a1, axis=0), head_grads, TN)
    qkv_all = over_cols(over_scene(own_qkv))
    shard = qkv_all.shape[0]
    grad_qkv = (
        qkv_all.reshape(shard, seq_count, 3, cols).transpose(0, 2, 1, 3).reshape(shard, 3 * width)
    )

    def own_rows(total):
        return lax.dynamic_slice_in_dim(total, scene_rank * shard, shard, 1).T

    norm_one = lax.psum(jnp.stack([gain_grad_one, shift_grad_one]), ("scene", "seq"))
    norm_two = lax.psum(jnp.stack([gain_grad_two, shift_grad_two]), ("scene", "seq"))
    dec_grads = lax.psum((grad_w1, grad_b1, grad_w2), "scene")
    return (
        block_out,
        decoded,
        grad_tokens,
        own_rows(norm_one),
        own_rows(norm_two),
        grad_qkv,
        grad_proj,
        grad_fc1,
        grad_fc2,
        grad_unp,
        dec_grads[0],
        dec_grads[1],
        dec_grads[2],
    )


def solution(mesh):
    rows = P(("scene", "seq"), None)
    shard = P("scene", None)
    in_specs = (
        rows, P("scene"), shard, shard, shard, shard, shard, shard, P(), P(), P(), rows, rows
    )
    out_specs = (rows,) * 3 + (shard,) * 7 + (P(),) * 3
    return jax.shard_map(
        per_device, mesh=mesh, in_specs=in_specs, out_specs=out_specs, check_vma=False
    )
```

```python
import functools

import jax
import jax.numpy as jnp
from jax import lax
from jax.experimental import pallas as pl
from jax.experimental.pallas import tpu as pltpu
from jax.sharding import PartitionSpec as P

H = 16
TF = 32
PP = 4
OUT = 4
TG = 16
IMG_DEV = 576

EPS = 1e-05
NEG_FILL = -1e30
LOG2E = 1.4426950408889634
VMEM_BYTES = 60 * 2**20

NT = (((1,), (1,)), ((), ()))
NN = (((1,), (0,)), ((), ()))
TN = (((0,), (0,)), ((), ()))


def mxu(left, right, dims):
    return lax.dot_general(left, right, dims, preferred_element_type=jnp.float32)


def exact(left, right, dims):
    return lax.dot_general(
        left, right, dims, precision=lax.Precision.HIGHEST, preferred_element_type=jnp.float32
    )


def gelu_parts(v):
    a = jnp.abs(v) * 0.7071067811865476
    t = 1.0 / (1.0 + 0.3275911 * a)
    poly = t * (
        0.254829592
        + t * (-0.284496736 + t * (1.421413741 + t * (-1.453152027 + t * 1.061405429)))
    )
    e = jnp.exp(-a * a)
    tail = 0.5 * poly * e
    cdf = jnp.where(v >= 0.0, 1.0 - tail, tail)
    return v * cdf, cdf + v * (e * 0.3989422804014327)


def pair_keys(block, bias, head, half):
    lane = lax.broadcasted_iota(jnp.int32, block.shape, 1)
    mine = (lane < half) if head == 0 else (lane >= half)
    flag = half if head == 0 else 0
    zero = jnp.zeros_like(block)
    return jnp.where(mine, block, jnp.where(lane == flag, bias, zero))


def pair_queries(block, head, half):
    lane = lax.broadcasted_iota(jnp.int32, block.shape, 1)
    mine = (lane < half) if head == 0 else (lane >= half)
    flag = half if head == 0 else 0
    zero = jnp.zeros_like(block)
    return jnp.where(mine, block, jnp.where(lane == flag, jnp.ones_like(block), zero))


def pair_mask(block, head, half):
    lane = lax.broadcasted_iota(jnp.int32, block.shape, 1)
    mine = (lane < half) if head == 0 else (lane >= half)
    return jnp.where(mine, block, jnp.zeros_like(block))


def attn_fwd_kernel(*refs, first, last, sub, scale):
    q_ref, k_ref, v_ref, bias_ref = refs[:4]
    refs = refs[4:]
    if not first:
        acc_in, peak_in = refs[:2]
        refs = refs[2:]
    out_a, out_b, s_buf, k_buf, vt_buf, acc_buf = refs
    tq, lanes = q_ref.shape
    n = k_ref.shape[0] // sub
    half = lanes // 2
    q = q_ref[...]
    qs = [pair_queries(q, h, half) for h in range(2)]
    ones = jnp.ones((16, sub), jnp.bfloat16)
    for i in range(n):
        rows = slice(i * sub, i * sub + sub)
        kb, bias = k_ref[rows, :], bias_ref[rows, :]
        vt = v_ref[rows, :].T
        for h in range(2):
            k_buf[i, h] = pair_keys(kb, bias, h, half)
            vt_buf[i, h, :half] = vt[h * half : h * half + half]
            vt_buf[i, h, half:] = ones

    def score(j, peak):
        out = []
        for h in range(2):
            s = mxu(k_buf[j, h], qs[h], NT)
            s_buf[j % 2, h] = s
            out.append(jnp.maximum(peak[h], jnp.max(s, axis=0, keepdims=True)))
        return out

    def mix(j, before, peak):
        for h in range(2):
            p = jnp.exp2((s_buf[j % 2, h] - peak[h]) * scale).astype(jnp.bfloat16)
            part = mxu(vt_buf[j, h], p, NN)
            if first and j == 0:
                acc_buf[h] = part
            else:
                fade = jnp.exp2((before[h] - peak[h]) * scale)
                old = acc_in[h] if j == 0 else acc_buf[h]
                acc_buf[h] = old * fade + part

    if first:
        before = [jnp.full((1, tq), -3e38, jnp.float32)] * 2
    else:
        before = [peak_in[h : h + 1, :] for h in range(2)]
    peak = score(0, before)
    for j in range(1, n):
        fresh = score(j, peak)
        mix(j - 1, before, peak)
        before, peak = peak, fresh
    mix(n - 1, before, peak)
    if last:
        outs = []
        for h in range(2):
            acc = acc_buf[h]
            total = acc[half : half + 1]
            outs.append(acc[:half] / total)
            out_b[h : h + 1, :] = peak[h] * scale + jnp.log2(total)
        out_a[...] = jnp.concatenate(outs, axis=0).T.astype(jnp.bfloat16)
    else:
        for h in range(2):
            out_a[h] = acc_buf[h]
            out_b[h : h + 1, :] = peak[h]


def attn_fwd(q_rows, kv_rows, bias, state, last, head_dim):
    lanes = 2 * head_dim
    tq, tk = q_rows.shape[0], kv_rows.shape[0]
    pairs = kv_rows.shape[1] // (3 * lanes)
    width = pairs * lanes
    ext = head_dim + 16
    sub = 256
    first = state is None
    block = lambda rows, off: pl.BlockSpec((rows, lanes), lambda h: (0, 3 * h + off))
    stat = pl.BlockSpec((None, 2, tq), lambda h: (h, 0, 0))
    carry = pl.BlockSpec((None, 2, ext, tq), lambda h: (h, 0, 0, 0))
    stat_shape = jax.ShapeDtypeStruct((pairs, 2, tq), jnp.float32)
    if last:
        out_specs = (pl.BlockSpec((tq, lanes), lambda h: (0, h)), stat)
        out_shape = (jax.ShapeDtypeStruct((tq, width), jnp.bfloat16), stat_shape)
    else:
        out_specs = (carry, stat)
        out_shape = (jax.ShapeDtypeStruct((pairs, 2, ext, tq), jnp.float32), stat_shape)
    return pl.pallas_call(
        functools.partial(
            attn_fwd_kernel, first=first, last=last, sub=sub, scale=head_dim**-0.5 * LOG2E
        ),
        grid=(pairs,),
        in_specs=[block(tq, 0), block(tk, 1), block(tk, 2), pl.BlockSpec((tk, lanes), lambda h: (0, 0))]
        + ([] if first else [carry, stat]),
        out_specs=out_specs,
        out_shape=out_shape,
        scratch_shapes=[
            pltpu.VMEM((2, 2, sub, tq), jnp.float32),
            pltpu.VMEM((tk // sub, 2, sub, lanes), jnp.bfloat16),
            pltpu.VMEM((tk // sub, 2, ext, sub), jnp.bfloat16),
            pltpu.VMEM((2, ext, tq), jnp.float32),
        ],
        compiler_params=pltpu.CompilerParams(vmem_limit_bytes=VMEM_BYTES),
        cost_estimate=pl.CostEstimate(
            flops=16 * tq * tk * width, bytes_accessed=2 * width * (2 * tq + 2 * tk), transcendentals=0
        ),
        name="attn_fwd",
    )(q_rows, kv_rows, kv_rows, bias, *(() if first else state))


def attn_bwd_kernel(
    q_ref, k_ref, v_ref, do_ref, lse_ref, del_ref, bias_ref,
    out_ref,
    s_buf, dp_buf, qm, km, dom, kt, qt, dot, dqa, dka, dva, *, tk, tq, scale, post
):
    nq = q_ref.shape[0] // tq
    nk = k_ref.shape[0] // tk
    half = q_ref.shape[1] // 2
    for i in range(nk):
        rows = slice(i * tk, i * tk + tk)
        for h in range(2):
            km[h, rows] = pair_keys(k_ref[rows, :], bias_ref[...], h, half)
    for h in range(2):
        qm[h] = pair_queries(q_ref[...], h, half)
        dom[h] = pair_mask(do_ref[...], h, half)
    kt[...] = k_ref[...].T
    qt[...] = q_ref[...].T
    dot[...] = do_ref[...].T
    for acc in (dqa, dka, dva):
        acc[...] = jnp.zeros(acc.shape, jnp.float32)

    def place(t):
        if isinstance(t, int):
            return t // nq * tk, t % nq * tq, t % 2
        return (
            pl.multiple_of(lax.div(t, nq) * tk, tk),
            pl.multiple_of(lax.rem(t, nq) * tq, tq),
            lax.rem(t, 2),
        )

    def score(t):
        k0, q0, slot = place(t)
        ks, qs = pl.ds(k0, tk), pl.ds(q0, tq)
        vv = v_ref[ks, :]
        for h in range(2):
            s_buf[slot, h] = mxu(km[h, ks, :], qm[h, qs, :], NT)
            dp_buf[slot, h] = mxu(vv, dom[h, qs, :], NT)

    def grads(t):
        k0, q0, slot = place(t)
        ks, qs = pl.ds(k0, tk), pl.ds(q0, tq)
        for h in range(2):
            p = jnp.exp2(s_buf[slot, h] * scale - lse_ref[h : h + 1, qs])
            ds = (p * (dp_buf[slot, h] - del_ref[h : h + 1, qs])).astype(jnp.bfloat16)
            pb = p.astype(jnp.bfloat16)
            r = slice(half * h, half * h + half)
            dqa[r, qs] += mxu(kt[r, ks], ds, NN)
            dva[r, ks] += mxu(dot[r, qs], pb, NT)
            dka[r, ks] += mxu(qt[r, qs], ds, NT)

    score(0)

    def body(t, carry):
        score(t)
        grads(t - 1)
        return carry

    lax.fori_loop(1, nq * nk, body, 0)
    grads(nq * nk - 1)
    lanes = 2 * half
    out_ref[:, :lanes] = (dqa[...] * post).T.astype(jnp.bfloat16)
    out_ref[:, lanes : 2 * lanes] = (dka[...] * post).T.astype(jnp.bfloat16)
    out_ref[:, 2 * lanes :] = dva[...].T.astype(jnp.bfloat16)


def attn_bwd(qkv, do, lse, delta, bias, pair, head_dim):
    rows = qkv.shape[0]
    tk = bias.shape[0]
    tq = tk
    lanes = 2 * head_dim
    block = lambda at: pl.BlockSpec((rows, lanes), lambda h: (0, at))
    stat = pl.BlockSpec((None, 2, rows), lambda h: (pair, 0, 0))
    return pl.pallas_call(
        functools.partial(
            attn_bwd_kernel, tk=tk, tq=tq, scale=head_dim**-0.5 * LOG2E, post=head_dim**-0.5
        ),
        grid=(1,),
        in_specs=[block(3 * pair), block(3 * pair + 1), block(3 * pair + 2), block(pair)]
        + [stat] * 2
        + [pl.BlockSpec((tk, lanes), lambda h: (0, 0))],
        out_specs=pl.BlockSpec((rows, 3 * lanes), lambda h: (0, 0)),
        out_shape=jax.ShapeDtypeStruct((rows, 3 * lanes), jnp.bfloat16),
        scratch_shapes=[
            pltpu.VMEM((2, 2, tk, tq), jnp.float32),
            pltpu.VMEM((2, 2, tk, tq), jnp.float32),
            pltpu.VMEM((2, rows, lanes), jnp.bfloat16),
            pltpu.VMEM((2, rows, lanes), jnp.bfloat16),
            pltpu.VMEM((2, rows, lanes), jnp.bfloat16),
            pltpu.VMEM((lanes, rows), jnp.bfloat16),
            pltpu.VMEM((lanes, rows), jnp.bfloat16),
            pltpu.VMEM((lanes, rows), jnp.bfloat16),
            pltpu.VMEM((lanes, rows), jnp.float32),
            pltpu.VMEM((lanes, rows), jnp.float32),
            pltpu.VMEM((lanes, rows), jnp.float32),
        ],
        compiler_params=pltpu.CompilerParams(vmem_limit_bytes=VMEM_BYTES),
        cost_estimate=pl.CostEstimate(
            flops=40 * rows * rows * lanes, bytes_accessed=14 * rows * lanes, transcendentals=0
        ),
        name="attn_bwd",
    )(qkv, qkv, qkv, do, lse, delta, bias)


def fc1_kernel(x_ref, w_ref, act_ref, slope_ref):
    act, slope = gelu_parts(mxu(x_ref[...], w_ref[...], NN))
    act_ref[...] = act.astype(jnp.bfloat16)
    slope_ref[...] = slope.astype(jnp.bfloat16)


def fc1_gelu(x, w):
    rows, depth = x.shape
    cols = w.shape[1]
    tile = 512
    spec = pl.BlockSpec((rows, tile), lambda i: (0, i))
    return pl.pallas_call(
        fc1_kernel,
        grid=(cols // tile,),
        in_specs=[
            pl.BlockSpec((rows, depth), lambda i: (0, 0)),
            pl.BlockSpec((depth, tile), lambda i: (0, i)),
        ],
        out_specs=(spec, spec),
        out_shape=(jax.ShapeDtypeStruct((rows, cols), jnp.bfloat16),) * 2,
        compiler_params=pltpu.CompilerParams(vmem_limit_bytes=VMEM_BYTES),
        cost_estimate=pl.CostEstimate(
            flops=2 * rows * cols * depth,
            bytes_accessed=2 * (rows * depth + depth * cols + 2 * rows * cols),
            transcendentals=0,
        ),
        name="fc1_gelu",
    )(x, w)


def normalize(v):
    center = v - jnp.mean(v, axis=-1, keepdims=True)
    spread = jnp.mean(center * center, axis=-1, keepdims=True)
    inv = lax.rsqrt(spread + EPS)
    return center * inv, inv


def norm_back(g, u, inv, gain):
    q = g * gain
    back = inv * (
        q - jnp.mean(q, axis=-1, keepdims=True) - u * jnp.mean(q * u, axis=-1, keepdims=True)
    )
    return back, jnp.sum(g * u, axis=0), jnp.sum(g, axis=0)


def per_device(
    tokens,
    image_count,
    norm_params,
    w_qkv,
    w_proj,
    w_fc1,
    w_fc2,
    w_unpatch,
    w_dec1,
    b_dec1,
    w_dec2,
    cot_out,
    cot_dec,
):
    seq_count = lax.axis_size("seq")
    rank = lax.axis_index("seq")
    scene_rank = lax.axis_index("scene")
    tok_rows, width = tokens.shape
    head_dim = width // H
    cols = width // seq_count
    cells = TG * TG
    bf16, f32 = jnp.bfloat16, jnp.float32
    live_image = image_count[0] // seq_count
    pos = jnp.arange(tok_rows, dtype=jnp.int32)
    row_live = (pos >= IMG_DEV) | (pos < live_image)
    bias = jnp.broadcast_to(
        jnp.where(row_live, 0.0, NEG_FILL).astype(bf16)[:, None], (tok_rows, 2 * head_dim)
    )

    def hop(x, step):
        return lax.ppermute(
            x, "seq", [(i, i + step) for i in range(seq_count) if 0 <= i + step < seq_count]
        )

    def turn(x, step):
        return lax.ppermute(x, "seq", [(i, (i + step) % seq_count) for i in range(seq_count)])

    def ahead(d):
        return lax.rem(rank + d, seq_count)

    def behind(d):
        return lax.rem(rank - d + seq_count, seq_count)

    def slot_of(chunk):
        return jnp.where(chunk <= rank, rank - chunk, chunk)

    def piece(x, chunk, size, axis):
        return lax.dynamic_slice_in_dim(x, chunk * size, size, axis)

    cot_row = jnp.pad(cot_dec.reshape(1, -1), ((0, 15), (0, width - cot_dec.size)))
    parcel = jnp.concatenate([tokens, cot_row], axis=0)
    ups, downs = [parcel], [parcel]

    def move_on():
        ups.append(hop(ups[-1], 1))
        downs.append(hop(downs[-1], -1))

    move_on()
    move_on()

    def slot(d):
        pick = ups[d]
        for r in range(d):
            pick = jnp.where(rank == r, downs[d - r], pick)
        return pick

    lanes = 2 * head_dim
    pairs = width // lanes
    shard = w_qkv.shape[0]
    scene_count = width // shard

    def gather(w):
        return lax.all_gather(w.astype(bf16), "scene", axis=0, tiled=True)

    pair_order = w_qkv.astype(bf16).reshape(shard, 3, pairs, lanes).transpose(0, 2, 1, 3)
    first_w = lax.all_gather(
        jnp.concatenate(
            [
                pair_order.reshape(shard, 3 * width),
                w_unpatch.astype(bf16),
                jnp.pad(norm_params.astype(bf16), ((0, 0), (0, 124))),
            ],
            axis=1,
        ),
        "scene",
        axis=0,
        tiled=True,
    )
    qkv_w = first_w[:, : 3 * width]
    unpatch_w = first_w[:, 3 * width : 3 * width + PP * TF]
    norm_full = first_w[:, 3 * width + PP * TF : 3 * width + PP * TF + 4].astype(f32)
    gain_one, shift_one, gain_two, shift_two = (norm_full[:, i] for i in range(4))
    proj_w = gather(w_proj)
    fc1_w = gather(w_fc1)
    fc2_w = gather(w_fc2)

    a1, own, slots = [], [], []
    state = None
    for d in range(seq_count):
        slots.append(slot(d))
        u, _ = normalize(slots[d][:tok_rows].astype(f32))
        a = (u * gain_one + shift_one).astype(bf16)
        a1.append(a)
        qkv = mxu(a, qkv_w, NN).astype(bf16)
        own.append(piece(qkv, rank, 3 * cols, 1))
        if d == 0:
            q_rows = qkv
        state = attn_fwd(q_rows, qkv, bias, state, d == seq_count - 1, head_dim)
        if d + 2 < seq_count:
            ups[d + 2], downs[d + 2], state = lax.optimization_barrier(
                (ups[d + 2], downs[d + 2], state)
            )
            if d + 3 < seq_count:
                move_on()
    mixed, lse = state
    lse = lse.reshape(H, tok_rows)

    inputs_f = tokens.astype(f32)
    middle = inputs_f + mxu(mixed, proj_w, NN)
    u_two, inv_two = normalize(middle)
    a2 = (u_two * gain_two + shift_two).astype(bf16)
    act, slope = fc1_gelu(a2, fc1_w)
    triplane = (middle[IMG_DEV:] + mxu(act[IMG_DEV:], fc2_w, NN)).astype(bf16)
    tri_rows = tok_rows - IMG_DEV
    planes = mxu(triplane, unpatch_w, NN).astype(bf16)
    all_planes = jnp.zeros((seq_count * tri_rows, PP * TF), bf16)
    for d in range(seq_count):
        got = turn(planes, d) if d else planes
        all_planes = lax.dynamic_update_slice_in_dim(all_planes, got, behind(d) * tri_rows, 0)
    image_live = pos[:IMG_DEV] < live_image
    image_out = jnp.where(
        image_live[:, None], middle[:IMG_DEV] + mxu(act[:IMG_DEV], fc2_w, NN), 0.0
    ).astype(bf16)
    image_out, all_planes = lax.optimization_barrier((image_out, all_planes))
    block_out = jnp.concatenate([image_out, triplane], axis=0)

    cot_rows = jnp.zeros((seq_count, width), bf16)
    for d in range(seq_count):
        chunk = jnp.where(rank >= d, rank - d, d)
        cot_rows = lax.dynamic_update_slice_in_dim(
            cot_rows, slots[d][tok_rows : tok_rows + 1], chunk, 0
        )
    cot_cells = cot_rows[:, : cot_dec.size].reshape(cells, OUT * PP)
    planes_f = all_planes.astype(f32)
    feat = planes_f[:cells] + planes_f[cells : 2 * cells] + planes_f[2 * cells :]
    dh = w_dec1.shape[1]
    eye = jnp.eye(PP, dtype=f32)
    dec1 = jnp.einsum("fh,pq->pfqh", w_dec1, eye).reshape(PP * TF, PP * dh)
    dec2 = jnp.einsum("ho,pq->phoq", w_dec2, eye).reshape(PP * dh, OUT * PP)
    hidden_pre = exact(feat, dec1, NN) + jnp.tile(b_dec1, PP)
    zdec, zslope = gelu_parts(hidden_pre)
    decoded_all = exact(zdec, dec2, NN)
    cells_dev = cells // seq_count
    decoded = lax.dynamic_slice_in_dim(decoded_all, rank * cells_dev, cells_dev, 0)
    cot_f = cot_cells.astype(f32)
    grad_hidden = exact(cot_f, dec2, NT) * zslope
    gfeat = exact(grad_hidden, dec1, NT).astype(bf16)
    grad_w2 = jnp.einsum(
        "phop->ho", exact(zdec, cot_f, TN).reshape(PP, dh, OUT, PP)
    )
    grad_b1 = jnp.sum(jnp.sum(grad_hidden, axis=0).reshape(PP, dh), axis=0)
    grad_w1 = jnp.einsum(
        "pfph->fh", exact(feat, grad_hidden, TN).reshape(PP, TF, PP, dh)
    )
    plane_grad = lax.dynamic_slice_in_dim(
        jnp.concatenate([gfeat] * 4, axis=0), lax.rem(rank * tri_rows, cells), tri_rows, 0
    )
    grad_unpatch = mxu(triplane, plane_grad, TN)
    grad_tri = mxu(plane_grad, unpatch_w, NT)

    grad_result = jnp.where(row_live[:, None], cot_out.astype(f32), 0.0)
    grad_result = jnp.concatenate([grad_result[:IMG_DEV], grad_result[IMG_DEV:] + grad_tri], axis=0)
    branch = grad_result.astype(bf16)
    fc2_grad = mxu(act, branch, TN).astype(bf16)
    grad_pre = (mxu(branch, fc2_w, NT) * slope.astype(f32)).astype(bf16)
    back_two, gain_grad_two, shift_grad_two = norm_back(
        mxu(grad_pre, fc1_w, NT), u_two, inv_two, gain_two
    )
    grad_mid = grad_result + back_two
    mid_grad = grad_mid.astype(bf16)
    grad_mixed = mxu(mid_grad, proj_w, NT).astype(bf16)
    head_of = (jnp.arange(width) // head_dim)[None, :] == jnp.arange(H)[:, None]
    delta = exact(
        head_of.astype(f32), grad_mixed.astype(f32) * mixed.astype(f32), NT
    )
    heads_dev = H // seq_count
    stats = jnp.concatenate(
        [lse.reshape(seq_count, heads_dev, tok_rows), delta.reshape(seq_count, heads_dev, tok_rows)],
        axis=1,
    )
    parts, rest = [], stats
    for _ in range(3):
        top = lax.reduce_precision(rest, 8, 7)
        parts.append(top.astype(bf16))
        rest = rest - top
    stat_cols = jnp.concatenate(parts, axis=1).reshape(seq_count, -1, cols)
    stat_rows = stat_cols.shape[1]
    pad_rows = -stat_rows % 16
    letter = jnp.concatenate(
        [grad_mixed]
        + [
            jnp.pad(
                stat_cols.transpose(1, 0, 2).reshape(stat_rows, width), ((0, pad_rows), (0, 0))
            )
        ],
        axis=0,
    )
    letter, late_a2, late_pre, late_mid = lax.optimization_barrier((letter, a2, grad_pre, mid_grad))
    norm_cols = jnp.stack([gain_grad_two, shift_grad_two], axis=1).astype(bf16)
    wide_grad = jnp.concatenate(
        [
            mxu(late_a2, late_pre, TN).astype(bf16),
            mxu(mixed, late_mid, TN).astype(bf16),
            grad_unpatch.astype(bf16),
            jnp.pad(norm_cols, ((0, 0), (0, 128 * seq_count - PP * TF - 2))),
        ],
        axis=1,
    )
    do_all = jnp.zeros((seq_count * tok_rows, cols), bf16)
    stat_all = jnp.zeros((3, 2 * heads_dev, seq_count * tok_rows), f32)
    for d in range(seq_count):
        got = piece(letter, ahead(d), cols, 1)
        if d:
            got = turn(got, d)
        at = slot_of(behind(d)) * tok_rows
        do_all = lax.dynamic_update_slice_in_dim(do_all, got[:tok_rows], at, 0)
        got_stat = got[tok_rows : tok_rows + stat_rows].reshape(3, 2 * heads_dev, tok_rows)
        stat_all = lax.dynamic_update_slice_in_dim(stat_all, got_stat.astype(f32), at, 2)
    stat_all = stat_all[0] + stat_all[1] + stat_all[2]
    pairs_dev = heads_dev // 2
    lse_all = stat_all[:heads_dev].reshape(pairs_dev, 2, seq_count * tok_rows)
    delta_all = stat_all[heads_dev:].reshape(pairs_dev, 2, seq_count * tok_rows)
    own_all = jnp.concatenate(own, axis=0)
    dec_grads = lax.psum((grad_w1, grad_b1, grad_w2), "scene")

    def over_scene(g):
        return lax.psum_scatter(g, "scene", scatter_dimension=0, tiled=True)

    fc2_part = over_scene(fc2_grad)
    wide_part = over_scene(wide_grad)
    (own_all, do_all, lse_all, delta_all, wide_grad, dec_grads) = lax.optimization_barrier(
        (own_all, do_all, lse_all, delta_all, wide_grad, dec_grads)
    )

    def sum_pieces(part):
        size = part.shape[1] // seq_count
        return [
            turn(piece(part, ahead(d), size, 1), d) if d else piece(part, rank, size, 1)
            for d in range(seq_count)
        ]

    def over_seq(pieces):
        return over_cols(sum(x.astype(f32) for x in pieces).astype(bf16))

    def over_cols(mine):
        size = mine.shape[1]
        out = jnp.zeros((mine.shape[0], size * seq_count), f32)
        for d in range(seq_count):
            got = turn(mine, d) if d else mine
            out = lax.dynamic_update_slice_in_dim(out, got.astype(f32), behind(d) * size, 1)
        return out

    def exchange(mine):
        pieces = [piece(mine, slot_of(ahead(d)), tok_rows, 0) for d in range(seq_count)]
        return [turn(x, d) if d else x for d, x in enumerate(pieces)]

    moved, head_grads = [], []
    for p in range(pairs_dev):
        mine = attn_bwd(own_all, do_all, lse_all, delta_all, bias, p, head_dim)
        if p:
            mine, moved[-1], head_grads[-1], fc2_pieces = lax.optimization_barrier(
                (mine, moved[-1], head_grads[-1], fc2_pieces)
            )
        else:
            own_all, mine, fc2_part = lax.optimization_barrier((own_all, mine, fc2_part))
            fc2_pieces = sum_pieces(fc2_part)
        head_grads.append(mine)
        moved.append(exchange(mine))
    row_grads = jnp.zeros((tok_rows, 3 * width), bf16)
    for p in range(pairs_dev):
        for d in range(seq_count):
            row_grads = lax.dynamic_update_slice_in_dim(
                row_grads, moved[p][d], behind(d) * 3 * cols + p * 3 * lanes, 1
            )
    a1_all = jnp.concatenate(a1, axis=0)
    own_qkv = jnp.concatenate(
        [mxu(a1_all, part, TN).astype(bf16) for part in head_grads], axis=1
    )
    got_qkv = lax.all_to_all(
        own_qkv.reshape(scene_count, shard, 3 * cols), "scene", 0, 0, tiled=True
    )
    qkv_part = jnp.sum(got_qkv.astype(f32), axis=0).astype(bf16)

    grad_in = mxu(row_grads, qkv_w, NT)
    u_one, inv_one = normalize(inputs_f)
    back_one, gain_grad_one, shift_grad_one = norm_back(grad_in, u_one, inv_one, gain_one)
    grad_tokens = (grad_mid + back_one).astype(bf16)

    grad_fc2 = over_seq(fc2_pieces)
    grad_wide = over_seq(sum_pieces(wide_part))
    hidden = w_fc1.shape[1]
    grad_fc1, grad_misc = grad_wide[:, :hidden], grad_wide[:, hidden:]
    grad_proj = grad_misc[:, :width]
    grad_unp = grad_misc[:, width : width + PP * TF]
    norm_two = grad_misc[:, width + PP * TF : width + PP * TF + 2]
    qkv_all = over_cols(qkv_part)
    grad_qkv = qkv_all.reshape(shard, pairs, 3, lanes).transpose(0, 2, 1, 3).reshape(shard, 3 * width)

    norm_one = lax.psum(jnp.stack([gain_grad_one, shift_grad_one]), "scene")
    norm_one = lax.psum(lax.dynamic_slice_in_dim(norm_one, scene_rank * shard, shard, 1), "seq").T
    return (
        block_out,
        decoded,
        grad_tokens,
        norm_one,
        norm_two,
        grad_qkv,
        grad_proj,
        grad_fc1,
        grad_fc2,
        grad_unp,
        dec_grads[0],
        dec_grads[1],
        dec_grads[2],
    )


def solution(mesh):
    rows = P(("scene", "seq"), None)
    shard = P("scene", None)
    in_specs = (
        rows, P("scene"), shard, shard, shard, shard, shard, shard, P(), P(), P(), rows, rows
    )
    out_specs = (rows,) * 3 + (shard,) * 7 + (P(),) * 3
    return jax.shard_map(
        per_device, mesh=mesh, in_specs=in_specs, out_specs=out_specs, check_vma=False
    )
```

```python
import functools

import jax
import jax.numpy as jnp
from jax import lax
from jax.experimental import pallas as pl
from jax.experimental.pallas import tpu as pltpu
from jax.sharding import PartitionSpec as P

H = 16
TF = 32
PP = 4
OUT = 4
TG = 16
IMG_DEV = 576

EPS = 1e-05
NEG_FILL = -1e30
LOG2E = 1.4426950408889634
VMEM_BYTES = 60 * 2**20

NT = (((1,), (1,)), ((), ()))
NN = (((1,), (0,)), ((), ()))
TN = (((0,), (0,)), ((), ()))


def mxu(left, right, dims):
    return lax.dot_general(left, right, dims, preferred_element_type=jnp.float32)


def exact(left, right, dims):
    return lax.dot_general(
        left, right, dims, precision=lax.Precision.HIGHEST, preferred_element_type=jnp.float32
    )


def gelu_parts(v):
    a = jnp.abs(v) * 0.7071067811865476
    t = 1.0 / (1.0 + 0.3275911 * a)
    poly = t * (
        0.254829592
        + t * (-0.284496736 + t * (1.421413741 + t * (-1.453152027 + t * 1.061405429)))
    )
    e = jnp.exp(-a * a)
    tail = 0.5 * poly * e
    cdf = jnp.where(v >= 0.0, 1.0 - tail, tail)
    return v * cdf, cdf + v * (e * 0.3989422804014327)


def pair_keys(block, bias, head, half):
    lane = lax.broadcasted_iota(jnp.int32, block.shape, 1)
    mine = (lane < half) if head == 0 else (lane >= half)
    flag = half if head == 0 else 0
    zero = jnp.zeros_like(block)
    return jnp.where(mine, block, jnp.where(lane == flag, bias, zero))


def pair_queries(block, head, half):
    lane = lax.broadcasted_iota(jnp.int32, block.shape, 1)
    mine = (lane < half) if head == 0 else (lane >= half)
    flag = half if head == 0 else 0
    zero = jnp.zeros_like(block)
    return jnp.where(mine, block, jnp.where(lane == flag, jnp.ones_like(block), zero))


def pair_mask(block, head, half):
    lane = lax.broadcasted_iota(jnp.int32, block.shape, 1)
    mine = (lane < half) if head == 0 else (lane >= half)
    return jnp.where(mine, block, jnp.zeros_like(block))


def attn_fwd_kernel(*refs, first, last, sub, scale):
    q_ref, k_ref, v_ref, bias_ref = refs[:4]
    refs = refs[4:]
    if not first:
        acc_in, peak_in = refs[:2]
        refs = refs[2:]
    out_a, out_b, s_buf, k_buf, vt_buf, acc_buf = refs
    tq, lanes = q_ref.shape
    n = k_ref.shape[0] // sub
    half = lanes // 2
    q = q_ref[...]
    qs = [pair_queries(q, h, half) for h in range(2)]
    ones = jnp.ones((16, sub), jnp.bfloat16)
    for i in range(n):
        rows = slice(i * sub, i * sub + sub)
        kb, bias = k_ref[rows, :], bias_ref[rows, :]
        vt = v_ref[rows, :].T
        for h in range(2):
            k_buf[i, h] = pair_keys(kb, bias, h, half)
            vt_buf[i, h, :half] = vt[h * half : h * half + half]
            vt_buf[i, h, half:] = ones

    def score(j, peak):
        out = []
        for h in range(2):
            s = mxu(k_buf[j, h], qs[h], NT)
            s_buf[j % 2, h] = s
            out.append(jnp.maximum(peak[h], jnp.max(s, axis=0, keepdims=True)))
        return out

    def mix(j, before, peak):
        for h in range(2):
            p = jnp.exp2((s_buf[j % 2, h] - peak[h]) * scale).astype(jnp.bfloat16)
            part = mxu(vt_buf[j, h], p, NN)
            if first and j == 0:
                acc_buf[h] = part
            else:
                fade = jnp.exp2((before[h] - peak[h]) * scale)
                old = acc_in[h] if j == 0 else acc_buf[h]
                acc_buf[h] = old * fade + part

    if first:
        before = [jnp.full((1, tq), -3e38, jnp.float32)] * 2
    else:
        before = [peak_in[h : h + 1, :] for h in range(2)]
    peak = score(0, before)
    for j in range(1, n):
        fresh = score(j, peak)
        mix(j - 1, before, peak)
        before, peak = peak, fresh
    mix(n - 1, before, peak)
    if last:
        outs = []
        for h in range(2):
            acc = acc_buf[h]
            total = acc[half : half + 1]
            outs.append(acc[:half] / total)
            out_b[h : h + 1, :] = peak[h] * scale + jnp.log2(total)
        out_a[...] = jnp.concatenate(outs, axis=0).T.astype(jnp.bfloat16)
    else:
        for h in range(2):
            out_a[h] = acc_buf[h]
            out_b[h : h + 1, :] = peak[h]


def attn_fwd(q_rows, kv_rows, bias, state, last, head_dim):
    lanes = 2 * head_dim
    tq, tk = q_rows.shape[0], kv_rows.shape[0]
    pairs = kv_rows.shape[1] // (3 * lanes)
    width = pairs * lanes
    ext = head_dim + 16
    sub = 256
    first = state is None
    block = lambda rows, off: pl.BlockSpec((rows, lanes), lambda h: (0, 3 * h + off))
    stat = pl.BlockSpec((None, 2, tq), lambda h: (h, 0, 0))
    carry = pl.BlockSpec((None, 2, ext, tq), lambda h: (h, 0, 0, 0))
    stat_shape = jax.ShapeDtypeStruct((pairs, 2, tq), jnp.float32)
    if last:
        out_specs = (pl.BlockSpec((tq, lanes), lambda h: (0, h)), stat)
        out_shape = (jax.ShapeDtypeStruct((tq, width), jnp.bfloat16), stat_shape)
    else:
        out_specs = (carry, stat)
        out_shape = (jax.ShapeDtypeStruct((pairs, 2, ext, tq), jnp.float32), stat_shape)
    return pl.pallas_call(
        functools.partial(
            attn_fwd_kernel, first=first, last=last, sub=sub, scale=head_dim**-0.5 * LOG2E
        ),
        grid=(pairs,),
        in_specs=[block(tq, 0), block(tk, 1), block(tk, 2), pl.BlockSpec((tk, lanes), lambda h: (0, 0))]
        + ([] if first else [carry, stat]),
        out_specs=out_specs,
        out_shape=out_shape,
        scratch_shapes=[
            pltpu.VMEM((2, 2, sub, tq), jnp.float32),
            pltpu.VMEM((tk // sub, 2, sub, lanes), jnp.bfloat16),
            pltpu.VMEM((tk // sub, 2, ext, sub), jnp.bfloat16),
            pltpu.VMEM((2, ext, tq), jnp.float32),
        ],
        compiler_params=pltpu.CompilerParams(vmem_limit_bytes=VMEM_BYTES),
        cost_estimate=pl.CostEstimate(
            flops=16 * tq * tk * width, bytes_accessed=2 * width * (2 * tq + 2 * tk), transcendentals=0
        ),
        name="attn_fwd",
    )(q_rows, kv_rows, kv_rows, bias, *(() if first else state))


def attn_bwd_kernel(*refs, tk, tq, scale, post):
    q_ref, k_ref, v_ref, bias_ref = refs[:4]
    letters = refs[4:-14]
    out_ref = refs[-14]
    s_buf, dp_buf, lse_ref, del_ref, qm, km, dom, kt, qt, dot, dqa, dka, dva = refs[-13:]
    nq = q_ref.shape[0] // tq
    nk = k_ref.shape[0] // tk
    half = q_ref.shape[1] // 2
    for i in range(nk):
        rows = slice(i * tk, i * tk + tk)
        for h in range(2):
            km[h, rows] = pair_keys(k_ref[rows, :], bias_ref[...], h, half)
    for h in range(2):
        qm[h] = pair_queries(q_ref[...], h, half)
    kt[...] = k_ref[...].T
    qt[...] = q_ref[...].T
    per_row = tk // (2 * half)
    for i, letter in enumerate(letters):
        rows = slice(i * tk, i * tk + tk)
        do = letter[:tk, :]
        dot[:, rows] = do.T
        for h in range(2):
            dom[h, rows] = pair_mask(do, h, half)
        count = 4 * per_row
        stat = letter[tk : tk + 3 * count, :].astype(jnp.float32)
        stat = stat[:count] + stat[count : 2 * count] + stat[2 * count :]
        for kind, buf in enumerate((lse_ref, del_ref)):
            for h in range(2):
                at = (kind * 2 + h) * per_row
                buf[h : h + 1, rows] = jnp.concatenate(
                    [stat[at + j : at + j + 1] for j in range(per_row)], axis=1
                )
    for acc in (dqa, dka, dva):
        acc[...] = jnp.zeros(acc.shape, jnp.float32)

    def place(t):
        if isinstance(t, int):
            return t // nq * tk, t % nq * tq, t % 2
        return (
            pl.multiple_of(lax.div(t, nq) * tk, tk),
            pl.multiple_of(lax.rem(t, nq) * tq, tq),
            lax.rem(t, 2),
        )

    def score(t):
        k0, q0, slot = place(t)
        ks, qs = pl.ds(k0, tk), pl.ds(q0, tq)
        vv = v_ref[ks, :]
        for h in range(2):
            s_buf[slot, h] = mxu(km[h, ks, :], qm[h, qs, :], NT)
            dp_buf[slot, h] = mxu(vv, dom[h, qs, :], NT)

    def grads(t):
        k0, q0, slot = place(t)
        ks, qs = pl.ds(k0, tk), pl.ds(q0, tq)
        for h in range(2):
            p = jnp.exp2(s_buf[slot, h] * scale - lse_ref[h : h + 1, qs])
            ds = (p * (dp_buf[slot, h] - del_ref[h : h + 1, qs])).astype(jnp.bfloat16)
            pb = p.astype(jnp.bfloat16)
            r = slice(half * h, half * h + half)
            dqa[r, qs] += mxu(kt[r, ks], ds, NN)
            dva[r, ks] += mxu(dot[r, qs], pb, NT)
            dka[r, ks] += mxu(qt[r, qs], ds, NT)

    score(0)

    def body(t, carry):
        score(t)
        grads(t - 1)
        return carry

    lax.fori_loop(1, nq * nk, body, 0)
    grads(nq * nk - 1)
    lanes = 2 * half
    out_ref[:, :lanes] = (dqa[...] * post).T.astype(jnp.bfloat16)
    out_ref[:, lanes : 2 * lanes] = (dka[...] * post).T.astype(jnp.bfloat16)
    out_ref[:, 2 * lanes :] = dva[...].T.astype(jnp.bfloat16)


def attn_bwd(qkv, letters, bias, pair, head_dim):
    rows = qkv.shape[0]
    tk = bias.shape[0]
    lanes = 2 * head_dim
    block = lambda at: pl.BlockSpec((rows, lanes), lambda h: (0, at))
    return pl.pallas_call(
        functools.partial(
            attn_bwd_kernel, tk=tk, tq=tk, scale=head_dim**-0.5 * LOG2E, post=head_dim**-0.5
        ),
        grid=(1,),
        in_specs=[block(3 * pair), block(3 * pair + 1), block(3 * pair + 2)]
        + [pl.BlockSpec((tk, lanes), lambda h: (0, 0))]
        + [pl.BlockSpec((letters[0].shape[0], lanes), lambda h: (0, pair))] * len(letters),
        out_specs=pl.BlockSpec((rows, 3 * lanes), lambda h: (0, 0)),
        out_shape=jax.ShapeDtypeStruct((rows, 3 * lanes), jnp.bfloat16),
        scratch_shapes=[
            pltpu.VMEM((2, 2, tk, tk), jnp.float32),
            pltpu.VMEM((2, 2, tk, tk), jnp.float32),
            pltpu.VMEM((2, rows), jnp.float32),
            pltpu.VMEM((2, rows), jnp.float32),
            pltpu.VMEM((2, rows, lanes), jnp.bfloat16),
            pltpu.VMEM((2, rows, lanes), jnp.bfloat16),
            pltpu.VMEM((2, rows, lanes), jnp.bfloat16),
            pltpu.VMEM((lanes, rows), jnp.bfloat16),
            pltpu.VMEM((lanes, rows), jnp.bfloat16),
            pltpu.VMEM((lanes, rows), jnp.bfloat16),
            pltpu.VMEM((lanes, rows), jnp.float32),
            pltpu.VMEM((lanes, rows), jnp.float32),
            pltpu.VMEM((lanes, rows), jnp.float32),
        ],
        compiler_params=pltpu.CompilerParams(vmem_limit_bytes=VMEM_BYTES),
        cost_estimate=pl.CostEstimate(
            flops=40 * rows * rows * lanes, bytes_accessed=14 * rows * lanes, transcendentals=0
        ),
        name="attn_bwd",
    )(qkv, qkv, qkv, bias, *letters)


def fc1_kernel(x_ref, w_ref, act_ref, slope_ref):
    act, slope = gelu_parts(mxu(x_ref[...], w_ref[...], NN))
    act_ref[...] = act.astype(jnp.bfloat16)
    slope_ref[...] = slope.astype(jnp.bfloat16)


def fc1_gelu(x, w):
    rows, depth = x.shape
    cols = w.shape[1]
    tile = 512
    spec = pl.BlockSpec((rows, tile), lambda i: (0, i))
    return pl.pallas_call(
        fc1_kernel,
        grid=(cols // tile,),
        in_specs=[
            pl.BlockSpec((rows, depth), lambda i: (0, 0)),
            pl.BlockSpec((depth, tile), lambda i: (0, i)),
        ],
        out_specs=(spec, spec),
        out_shape=(jax.ShapeDtypeStruct((rows, cols), jnp.bfloat16),) * 2,
        compiler_params=pltpu.CompilerParams(vmem_limit_bytes=VMEM_BYTES),
        cost_estimate=pl.CostEstimate(
            flops=2 * rows * cols * depth,
            bytes_accessed=2 * (rows * depth + depth * cols + 2 * rows * cols),
            transcendentals=0,
        ),
        name="fc1_gelu",
    )(x, w)


def normalize(v):
    center = v - jnp.mean(v, axis=-1, keepdims=True)
    spread = jnp.mean(center * center, axis=-1, keepdims=True)
    inv = lax.rsqrt(spread + EPS)
    return center * inv, inv


def norm_back(g, u, inv, gain):
    q = g * gain
    back = inv * (
        q - jnp.mean(q, axis=-1, keepdims=True) - u * jnp.mean(q * u, axis=-1, keepdims=True)
    )
    return back, jnp.sum(g * u, axis=0), jnp.sum(g, axis=0)


def per_device(
    tokens,
    image_count,
    norm_params,
    w_qkv,
    w_proj,
    w_fc1,
    w_fc2,
    w_unpatch,
    w_dec1,
    b_dec1,
    w_dec2,
    cot_out,
    cot_dec,
):
    seq_count = lax.axis_size("seq")
    rank = lax.axis_index("seq")
    scene_rank = lax.axis_index("scene")
    tok_rows, width = tokens.shape
    head_dim = width // H
    cols = width // seq_count
    cells = TG * TG
    bf16, f32 = jnp.bfloat16, jnp.float32
    live_image = image_count[0] // seq_count
    pos = jnp.arange(tok_rows, dtype=jnp.int32)
    row_live = (pos >= IMG_DEV) | (pos < live_image)
    bias = jnp.broadcast_to(
        jnp.where(row_live, 0.0, NEG_FILL).astype(bf16)[:, None], (tok_rows, 2 * head_dim)
    )

    def hop(x, step):
        return lax.ppermute(
            x, "seq", [(i, i + step) for i in range(seq_count) if 0 <= i + step < seq_count]
        )

    def turn(x, step):
        return lax.ppermute(x, "seq", [(i, (i + step) % seq_count) for i in range(seq_count)])

    def ahead(d):
        return lax.rem(rank + d, seq_count)

    def behind(d):
        return lax.rem(rank - d + seq_count, seq_count)

    def piece(x, chunk, size, axis):
        return lax.dynamic_slice_in_dim(x, chunk * size, size, axis)

    cot_row = jnp.pad(cot_dec.reshape(1, -1), ((0, 15), (0, width - cot_dec.size)))
    parcel = jnp.concatenate([tokens, cot_row], axis=0)
    ups, downs = [parcel], [parcel]

    def move_on():
        ups.append(hop(ups[-1], 1))
        downs.append(hop(downs[-1], -1))

    move_on()
    move_on()

    def slot(d):
        pick = ups[d]
        for r in range(d):
            pick = jnp.where(rank == r, downs[d - r], pick)
        return pick

    lanes = 2 * head_dim
    pairs = width // lanes
    shard = w_qkv.shape[0]
    scene_count = width // shard

    def gather(w):
        return lax.all_gather(w.astype(bf16), "scene", axis=0, tiled=True)

    pair_order = w_qkv.astype(bf16).reshape(shard, 3, pairs, lanes).transpose(0, 2, 1, 3)
    first_w = lax.all_gather(
        jnp.concatenate(
            [
                pair_order.reshape(shard, 3 * width),
                w_unpatch.astype(bf16),
                jnp.pad(norm_params.astype(bf16), ((0, 0), (0, 124))),
            ],
            axis=1,
        ),
        "scene",
        axis=0,
        tiled=True,
    )
    qkv_w = first_w[:, : 3 * width]
    unpatch_w = first_w[:, 3 * width : 3 * width + PP * TF]
    norm_full = first_w[:, 3 * width + PP * TF : 3 * width + PP * TF + 4].astype(f32)
    gain_one, shift_one, gain_two, shift_two = (norm_full[:, i] for i in range(4))
    proj_w = gather(w_proj)
    fc1_w = gather(w_fc1)
    fc2_w = gather(w_fc2)

    slots = []
    state = None
    a1_all = jnp.zeros((seq_count * tok_rows, width), bf16)
    own_all = jnp.zeros((seq_count * tok_rows, 3 * cols), bf16)
    for d in range(seq_count):
        slots.append(slot(d))
        u, _ = normalize(slots[d][:tok_rows].astype(f32))
        a = (u * gain_one + shift_one).astype(bf16)
        qkv = mxu(a, qkv_w, NN).astype(bf16)
        at = jnp.where(rank >= d, d, rank - d + seq_count) * tok_rows
        a1_all = lax.dynamic_update_slice_in_dim(a1_all, a, at, 0)
        own_all = lax.dynamic_update_slice_in_dim(own_all, piece(qkv, rank, 3 * cols, 1), at, 0)
        if d == 0:
            q_rows = qkv
        state = attn_fwd(q_rows, qkv, bias, state, d == seq_count - 1, head_dim)
        if d + 2 < seq_count:
            ups[d + 2], downs[d + 2], state = lax.optimization_barrier(
                (ups[d + 2], downs[d + 2], state)
            )
            if d + 3 < seq_count:
                move_on()
    mixed, lse = state
    lse = lse.reshape(H, tok_rows)

    inputs_f = tokens.astype(f32)
    middle = inputs_f + mxu(mixed, proj_w, NN)
    u_two, inv_two = normalize(middle)
    a2 = (u_two * gain_two + shift_two).astype(bf16)
    act, slope = fc1_gelu(a2, fc1_w)
    triplane = (middle[IMG_DEV:] + mxu(act[IMG_DEV:], fc2_w, NN)).astype(bf16)
    tri_rows = tok_rows - IMG_DEV
    planes = mxu(triplane, unpatch_w, NN).astype(bf16)
    all_planes = jnp.zeros((seq_count * tri_rows, PP * TF), bf16)
    for d in range(seq_count):
        got = turn(planes, d) if d else planes
        all_planes = lax.dynamic_update_slice_in_dim(all_planes, got, behind(d) * tri_rows, 0)
    image_live = pos[:IMG_DEV] < live_image
    image_out = jnp.where(
        image_live[:, None], middle[:IMG_DEV] + mxu(act[:IMG_DEV], fc2_w, NN), 0.0
    ).astype(bf16)
    image_out, all_planes = lax.optimization_barrier((image_out, all_planes))
    block_out = jnp.concatenate([image_out, triplane], axis=0)

    cot_rows = jnp.zeros((seq_count, width), bf16)
    for d in range(seq_count):
        chunk = jnp.where(rank >= d, rank - d, d)
        cot_rows = lax.dynamic_update_slice_in_dim(
            cot_rows, slots[d][tok_rows : tok_rows + 1], chunk, 0
        )
    cot_cells = cot_rows[:, : cot_dec.size].reshape(cells, OUT * PP)
    planes_f = all_planes.astype(f32)
    feat = planes_f[:cells] + planes_f[cells : 2 * cells] + planes_f[2 * cells :]
    dh = w_dec1.shape[1]
    eye = jnp.eye(PP, dtype=f32)
    dec1 = jnp.einsum("fh,pq->pfqh", w_dec1, eye).reshape(PP * TF, PP * dh)
    dec2 = jnp.einsum("ho,pq->phoq", w_dec2, eye).reshape(PP * dh, OUT * PP)
    hidden_pre = exact(feat, dec1, NN) + jnp.tile(b_dec1, PP)
    zdec, zslope = gelu_parts(hidden_pre)
    decoded_all = exact(zdec, dec2, NN)
    cells_dev = cells // seq_count
    decoded = lax.dynamic_slice_in_dim(decoded_all, rank * cells_dev, cells_dev, 0)
    cot_f = cot_cells.astype(f32)
    grad_hidden = exact(cot_f, dec2, NT) * zslope
    gfeat = exact(grad_hidden, dec1, NT).astype(bf16)
    grad_w2 = jnp.einsum(
        "phop->ho", exact(zdec, cot_f, TN).reshape(PP, dh, OUT, PP)
    )
    grad_b1 = jnp.sum(jnp.sum(grad_hidden, axis=0).reshape(PP, dh), axis=0)
    grad_w1 = jnp.einsum(
        "pfph->fh", exact(feat, grad_hidden, TN).reshape(PP, TF, PP, dh)
    )
    plane_grad = lax.dynamic_slice_in_dim(
        jnp.concatenate([gfeat] * 4, axis=0), lax.rem(rank * tri_rows, cells), tri_rows, 0
    )
    grad_unpatch = mxu(triplane, plane_grad, TN)
    grad_tri = mxu(plane_grad, unpatch_w, NT)

    grad_result = jnp.where(row_live[:, None], cot_out.astype(f32), 0.0)
    grad_result = jnp.concatenate([grad_result[:IMG_DEV], grad_result[IMG_DEV:] + grad_tri], axis=0)
    branch = grad_result.astype(bf16)
    fc2_grad = mxu(act, branch, TN).astype(bf16)
    grad_pre = (mxu(branch, fc2_w, NT) * slope.astype(f32)).astype(bf16)
    back_two, gain_grad_two, shift_grad_two = norm_back(
        mxu(grad_pre, fc1_w, NT), u_two, inv_two, gain_two
    )
    grad_mid = grad_result + back_two
    mid_grad = grad_mid.astype(bf16)
    grad_mixed = mxu(mid_grad, proj_w, NT).astype(bf16)
    head_of = (jnp.arange(width) // head_dim)[None, :] == jnp.arange(H)[:, None]
    delta = exact(
        head_of.astype(f32), grad_mixed.astype(f32) * mixed.astype(f32), NT
    )
    pairs_dev = pairs // seq_count
    parts, rest = [], jnp.stack([lse, delta])
    for _ in range(3):
        top = lax.reduce_precision(rest, 8, 7)
        parts.append(top.astype(bf16))
        rest = rest - top
    stats = jnp.stack(parts).reshape(3, 2, pairs, 2, tok_rows // lanes, lanes)
    stats = stats.transpose(0, 1, 3, 4, 2, 5).reshape(-1, width)
    letter = jnp.concatenate(
        [grad_mixed, jnp.pad(stats, ((0, -stats.shape[0] % 16), (0, 0)))], axis=0
    )
    letter, late_a2, late_pre, late_mid = lax.optimization_barrier((letter, a2, grad_pre, mid_grad))
    letters = [piece(letter, ahead(d), cols, 1) for d in range(seq_count)]
    letters = [turn(x, d) if d else x for d, x in enumerate(letters)]
    fc1_grad = mxu(late_a2, late_pre, TN).astype(bf16)
    norm_cols = jnp.stack([gain_grad_two, shift_grad_two], axis=1).astype(bf16)
    misc_grad = jnp.concatenate(
        [
            mxu(mixed, late_mid, TN).astype(bf16),
            grad_unpatch.astype(bf16),
            jnp.pad(norm_cols, ((0, 0), (0, 128 * seq_count - PP * TF - 2))),
        ],
        axis=1,
    )

    def over_scene(g):
        return lax.psum_scatter(g, "scene", scatter_dimension=0, tiled=True)

    def swap_scene(g):
        got = lax.all_to_all(g.reshape(scene_count, shard, -1), "scene", 0, 0, tiled=True)
        return jnp.sum(got.astype(f32), axis=0).astype(bf16)

    fc2_part = over_scene(fc2_grad)
    own_all, letters, fc2_part, fc1_grad, misc_grad = lax.optimization_barrier(
        (own_all, letters, fc2_part, fc1_grad, misc_grad)
    )
    fc1_part = over_scene(fc1_grad)
    misc_part = swap_scene(misc_grad)

    def sum_pieces(part):
        size = part.shape[1] // seq_count
        return [
            turn(piece(part, ahead(d), size, 1), d) if d else piece(part, rank, size, 1)
            for d in range(seq_count)
        ]

    def blocks_of(pieces):
        mine = sum(x.astype(f32) for x in pieces).astype(bf16)
        return [turn(mine, d) if d else mine for d in range(seq_count)]

    def side_by_side(blocks):
        size = blocks[0].shape[1]
        out = jnp.zeros((blocks[0].shape[0], size * seq_count), f32)
        for d, got in enumerate(blocks):
            out = lax.dynamic_update_slice_in_dim(out, got.astype(f32), behind(d) * size, 1)
        return out

    def exchange(mine):
        pieces = [piece(mine, (seq_count - d) % seq_count, tok_rows, 0) for d in range(seq_count)]
        return [turn(x, d) if d else x for d, x in enumerate(pieces)]

    fc2_pieces = sum_pieces(fc2_part)
    moved, head_grads = [], []
    dec_grads = (grad_w1, grad_b1, grad_w2)
    for p in range(pairs_dev):
        mine = attn_bwd(own_all, letters, bias, p, head_dim)
        if p == 0:
            own_all, mine, fc2_pieces = lax.optimization_barrier((own_all, mine, fc2_pieces))
            fc2_blocks = blocks_of(fc2_pieces)
        else:
            (mine, moved[-1], head_grads[-1], fc2_blocks, fc1_part, misc_part, dec_grads) = (
                lax.optimization_barrier(
                    (mine, moved[-1], head_grads[-1], fc2_blocks, fc1_part, misc_part, dec_grads)
                )
            )
        head_grads.append(mine)
        moved.append(exchange(mine))
    own_qkv = jnp.concatenate(
        [mxu(a1_all, part, TN).astype(bf16) for part in head_grads], axis=1
    )
    qkv_part = swap_scene(own_qkv)
    dec_grads = lax.psum(dec_grads, "scene")
    wide_part = jnp.concatenate([fc1_part, misc_part], axis=1)
    moved[-1], dec_grads, wide_part, qkv_part = lax.optimization_barrier(
        (moved[-1], dec_grads, wide_part, qkv_part)
    )
    row_grads = jnp.zeros((tok_rows, 3 * width), bf16)
    for p in range(pairs_dev):
        for d in range(seq_count):
            row_grads = lax.dynamic_update_slice_in_dim(
                row_grads, moved[p][d], behind(d) * 3 * cols + p * 3 * lanes, 1
            )

    grad_in = mxu(row_grads, qkv_w, NT)
    u_one, inv_one = normalize(inputs_f)
    back_one, gain_grad_one, shift_grad_one = norm_back(grad_in, u_one, inv_one, gain_one)
    grad_tokens = (grad_mid + back_one).astype(bf16)

    grad_fc2 = side_by_side(fc2_blocks)
    grad_wide = side_by_side(blocks_of(sum_pieces(wide_part)))
    hidden = w_fc1.shape[1]
    grad_fc1, grad_misc = grad_wide[:, :hidden], grad_wide[:, hidden:]
    grad_proj = grad_misc[:, :width]
    grad_unp = grad_misc[:, width : width + PP * TF]
    norm_two = grad_misc[:, width + PP * TF : width + PP * TF + 2]
    qkv_all = side_by_side([turn(qkv_part, d) if d else qkv_part for d in range(seq_count)])
    grad_qkv = qkv_all.reshape(shard, pairs, 3, lanes).transpose(0, 2, 1, 3).reshape(shard, 3 * width)

    norm_one = lax.psum(jnp.stack([gain_grad_one, shift_grad_one]), "scene")
    norm_one = lax.psum(lax.dynamic_slice_in_dim(norm_one, scene_rank * shard, shard, 1), "seq").T
    return (
        block_out,
        decoded,
        grad_tokens,
        norm_one,
        norm_two,
        grad_qkv,
        grad_proj,
        grad_fc1,
        grad_fc2,
        grad_unp,
        dec_grads[0],
        dec_grads[1],
        dec_grads[2],
    )


def solution(mesh):
    rows = P(("scene", "seq"), None)
    shard = P("scene", None)
    in_specs = (
        rows, P("scene"), shard, shard, shard, shard, shard, shard, P(), P(), P(), rows, rows
    )
    out_specs = (rows,) * 3 + (shard,) * 7 + (P(),) * 3
    return jax.shard_map(
        per_device, mesh=mesh, in_specs=in_specs, out_specs=out_specs, check_vma=False
    )
```

```python
import functools

import jax
import jax.numpy as jnp
from jax import lax
from jax.experimental import pallas as pl
from jax.experimental.pallas import tpu as pltpu
from jax.sharding import PartitionSpec as P

H = 16
TF = 32
PP = 4
OUT = 4
TG = 16
IMG_DEV = 576

EPS = 1e-05
NEG_FILL = -1e30
LOG2E = 1.4426950408889634
VMEM_BYTES = 60 * 2**20

NT = (((1,), (1,)), ((), ()))
NN = (((1,), (0,)), ((), ()))
TN = (((0,), (0,)), ((), ()))


def mxu(left, right, dims):
    return lax.dot_general(left, right, dims, preferred_element_type=jnp.float32)


def exact(left, right, dims):
    return lax.dot_general(
        left, right, dims, precision=lax.Precision.HIGHEST, preferred_element_type=jnp.float32
    )


def gelu_parts(v):
    a = jnp.abs(v) * 0.7071067811865476
    t = 1.0 / (1.0 + 0.3275911 * a)
    poly = t * (
        0.254829592
        + t * (-0.284496736 + t * (1.421413741 + t * (-1.453152027 + t * 1.061405429)))
    )
    e = jnp.exp(-a * a)
    tail = 0.5 * poly * e
    cdf = jnp.where(v >= 0.0, 1.0 - tail, tail)
    return v * cdf, cdf + v * (e * 0.3989422804014327)


def pair_keys(block, bias, head, half):
    lane = lax.broadcasted_iota(jnp.int32, block.shape, 1)
    mine = (lane < half) if head == 0 else (lane >= half)
    flag = half if head == 0 else 0
    zero = jnp.zeros_like(block)
    return jnp.where(mine, block, jnp.where(lane == flag, bias, zero))


def pair_queries(block, head, half):
    lane = lax.broadcasted_iota(jnp.int32, block.shape, 1)
    mine = (lane < half) if head == 0 else (lane >= half)
    flag = half if head == 0 else 0
    zero = jnp.zeros_like(block)
    return jnp.where(mine, block, jnp.where(lane == flag, jnp.ones_like(block), zero))


def pair_mask(block, head, half):
    lane = lax.broadcasted_iota(jnp.int32, block.shape, 1)
    mine = (lane < half) if head == 0 else (lane >= half)
    return jnp.where(mine, block, jnp.zeros_like(block))


def attn_fwd_kernel(*refs, first, last, sub, scale):
    q_ref, k_ref, v_ref, bias_ref = refs[:4]
    refs = refs[4:]
    if not first:
        acc_in, peak_in = refs[:2]
        refs = refs[2:]
    out_a, out_b, s_buf, k_buf, vt_buf, acc_buf = refs
    tq, lanes = q_ref.shape
    n = k_ref.shape[0] // sub
    half = lanes // 2
    q = q_ref[...]
    qs = [pair_queries(q, h, half) for h in range(2)]
    ones = jnp.ones((16, sub), jnp.bfloat16)
    for i in range(n):
        rows = slice(i * sub, i * sub + sub)
        kb, bias = k_ref[rows, :], bias_ref[rows, :]
        vt = v_ref[rows, :].T
        for h in range(2):
            k_buf[i, h] = pair_keys(kb, bias, h, half)
            vt_buf[i, h, :half] = vt[h * half : h * half + half]
            vt_buf[i, h, half:] = ones

    def score(j, peak):
        out = []
        for h in range(2):
            s = mxu(k_buf[j, h], qs[h], NT)
            s_buf[j % 2, h] = s
            out.append(jnp.maximum(peak[h], jnp.max(s, axis=0, keepdims=True)))
        return out

    def mix(j, before, peak):
        for h in range(2):
            p = jnp.exp2((s_buf[j % 2, h] - peak[h]) * scale).astype(jnp.bfloat16)
            part = mxu(vt_buf[j, h], p, NN)
            if first and j == 0:
                acc_buf[h] = part
            else:
                fade = jnp.exp2((before[h] - peak[h]) * scale)
                old = acc_in[h] if j == 0 else acc_buf[h]
                acc_buf[h] = old * fade + part

    if first:
        before = [jnp.full((1, tq), -3e38, jnp.float32)] * 2
    else:
        before = [peak_in[h : h + 1, :] for h in range(2)]
    peak = score(0, before)
    for j in range(1, n):
        fresh = score(j, peak)
        mix(j - 1, before, peak)
        before, peak = peak, fresh
    mix(n - 1, before, peak)
    if last:
        outs = []
        for h in range(2):
            acc = acc_buf[h]
            total = acc[half : half + 1]
            outs.append(acc[:half] / total)
            out_b[h : h + 1, :] = peak[h] * scale + jnp.log2(total)
        out_a[...] = jnp.concatenate(outs, axis=0).T.astype(jnp.bfloat16)
    else:
        for h in range(2):
            out_a[h] = acc_buf[h]
            out_b[h : h + 1, :] = peak[h]


def attn_fwd(q_rows, kv_rows, bias, state, last, head_dim):
    lanes = 2 * head_dim
    tq, tk = q_rows.shape[0], kv_rows.shape[0]
    pairs = kv_rows.shape[1] // (3 * lanes)
    width = pairs * lanes
    ext = head_dim + 16
    sub = 256
    first = state is None
    block = lambda rows, off: pl.BlockSpec((rows, lanes), lambda h: (0, 3 * h + off))
    stat = pl.BlockSpec((None, 2, tq), lambda h: (h, 0, 0))
    carry = pl.BlockSpec((None, 2, ext, tq), lambda h: (h, 0, 0, 0))
    stat_shape = jax.ShapeDtypeStruct((pairs, 2, tq), jnp.float32)
    if last:
        out_specs = (pl.BlockSpec((tq, lanes), lambda h: (0, h)), stat)
        out_shape = (jax.ShapeDtypeStruct((tq, width), jnp.bfloat16), stat_shape)
    else:
        out_specs = (carry, stat)
        out_shape = (jax.ShapeDtypeStruct((pairs, 2, ext, tq), jnp.float32), stat_shape)
    return pl.pallas_call(
        functools.partial(
            attn_fwd_kernel, first=first, last=last, sub=sub, scale=head_dim**-0.5 * LOG2E
        ),
        grid=(pairs,),
        in_specs=[block(tq, 0), block(tk, 1), block(tk, 2), pl.BlockSpec((tk, lanes), lambda h: (0, 0))]
        + ([] if first else [carry, stat]),
        out_specs=out_specs,
        out_shape=out_shape,
        scratch_shapes=[
            pltpu.VMEM((2, 2, sub, tq), jnp.float32),
            pltpu.VMEM((tk // sub, 2, sub, lanes), jnp.bfloat16),
            pltpu.VMEM((tk // sub, 2, ext, sub), jnp.bfloat16),
            pltpu.VMEM((2, ext, tq), jnp.float32),
        ],
        compiler_params=pltpu.CompilerParams(vmem_limit_bytes=VMEM_BYTES),
        cost_estimate=pl.CostEstimate(
            flops=16 * tq * tk * width, bytes_accessed=2 * width * (2 * tq + 2 * tk), transcendentals=0
        ),
        name="attn_fwd",
    )(q_rows, kv_rows, kv_rows, bias, *(() if first else state))


def attn_bwd_kernel(*refs, tk, tq, scale, post):
    q_ref, k_ref, v_ref, bias_ref = refs[:4]
    letters = refs[4:-14]
    out_ref = refs[-14]
    s_buf, dp_buf, lse_ref, del_ref, qm, km, dom, kt, qt, dot, dqa, dka, dva = refs[-13:]
    nq = q_ref.shape[0] // tq
    nk = k_ref.shape[0] // tk
    half = q_ref.shape[1] // 2
    for i in range(nk):
        rows = slice(i * tk, i * tk + tk)
        for h in range(2):
            km[h, rows] = pair_keys(k_ref[rows, :], bias_ref[...], h, half)
    for h in range(2):
        qm[h] = pair_queries(q_ref[...], h, half)
    kt[...] = k_ref[...].T
    qt[...] = q_ref[...].T
    per_row = tk // (2 * half)
    for i, letter in enumerate(letters):
        rows = slice(i * tk, i * tk + tk)
        do = letter[:tk, :]
        dot[:, rows] = do.T
        for h in range(2):
            dom[h, rows] = pair_mask(do, h, half)
        count = 4 * per_row
        stat = letter[tk : tk + 3 * count, :].astype(jnp.float32)
        stat = stat[:count] + stat[count : 2 * count] + stat[2 * count :]
        for kind, buf in enumerate((lse_ref, del_ref)):
            for h in range(2):
                at = (kind * 2 + h) * per_row
                buf[h : h + 1, rows] = jnp.concatenate(
                    [stat[at + j : at + j + 1] for j in range(per_row)], axis=1
                )
    for acc in (dqa, dka, dva):
        acc[...] = jnp.zeros(acc.shape, jnp.float32)

    def place(t):
        if isinstance(t, int):
            return t // nq * tk, t % nq * tq, t % 2
        return (
            pl.multiple_of(lax.div(t, nq) * tk, tk),
            pl.multiple_of(lax.rem(t, nq) * tq, tq),
            lax.rem(t, 2),
        )

    def score(t):
        k0, q0, slot = place(t)
        ks, qs = pl.ds(k0, tk), pl.ds(q0, tq)
        vv = v_ref[ks, :]
        for h in range(2):
            s_buf[slot, h] = mxu(km[h, ks, :], qm[h, qs, :], NT)
            dp_buf[slot, h] = mxu(vv, dom[h, qs, :], NT)

    def grads(t):
        k0, q0, slot = place(t)
        ks, qs = pl.ds(k0, tk), pl.ds(q0, tq)
        for h in range(2):
            p = jnp.exp2(s_buf[slot, h] * scale - lse_ref[h : h + 1, qs])
            ds = (p * (dp_buf[slot, h] - del_ref[h : h + 1, qs])).astype(jnp.bfloat16)
            pb = p.astype(jnp.bfloat16)
            r = slice(half * h, half * h + half)
            dqa[r, qs] += mxu(kt[r, ks], ds, NN)
            dva[r, ks] += mxu(dot[r, qs], pb, NT)
            dka[r, ks] += mxu(qt[r, qs], ds, NT)

    score(0)

    def body(t, carry):
        score(t)
        grads(t - 1)
        return carry

    lax.fori_loop(1, nq * nk, body, 0)
    grads(nq * nk - 1)
    lanes = 2 * half
    out_ref[:, :lanes] = (dqa[...] * post).T.astype(jnp.bfloat16)
    out_ref[:, lanes : 2 * lanes] = (dka[...] * post).T.astype(jnp.bfloat16)
    out_ref[:, 2 * lanes :] = dva[...].T.astype(jnp.bfloat16)


def attn_bwd(qkv, letters, bias, pair, head_dim):
    rows = qkv.shape[0]
    tk = bias.shape[0]
    lanes = 2 * head_dim
    block = lambda at: pl.BlockSpec((rows, lanes), lambda h: (0, at))
    return pl.pallas_call(
        functools.partial(
            attn_bwd_kernel, tk=tk, tq=tk, scale=head_dim**-0.5 * LOG2E, post=head_dim**-0.5
        ),
        grid=(1,),
        in_specs=[block(3 * pair), block(3 * pair + 1), block(3 * pair + 2)]
        + [pl.BlockSpec((tk, lanes), lambda h: (0, 0))]
        + [pl.BlockSpec((letters[0].shape[0], lanes), lambda h: (0, pair))] * len(letters),
        out_specs=pl.BlockSpec((rows, 3 * lanes), lambda h: (0, 0)),
        out_shape=jax.ShapeDtypeStruct((rows, 3 * lanes), jnp.bfloat16),
        scratch_shapes=[
            pltpu.VMEM((2, 2, tk, tk), jnp.float32),
            pltpu.VMEM((2, 2, tk, tk), jnp.float32),
            pltpu.VMEM((2, rows), jnp.float32),
            pltpu.VMEM((2, rows), jnp.float32),
            pltpu.VMEM((2, rows, lanes), jnp.bfloat16),
            pltpu.VMEM((2, rows, lanes), jnp.bfloat16),
            pltpu.VMEM((2, rows, lanes), jnp.bfloat16),
            pltpu.VMEM((lanes, rows), jnp.bfloat16),
            pltpu.VMEM((lanes, rows), jnp.bfloat16),
            pltpu.VMEM((lanes, rows), jnp.bfloat16),
            pltpu.VMEM((lanes, rows), jnp.float32),
            pltpu.VMEM((lanes, rows), jnp.float32),
            pltpu.VMEM((lanes, rows), jnp.float32),
        ],
        compiler_params=pltpu.CompilerParams(vmem_limit_bytes=VMEM_BYTES),
        cost_estimate=pl.CostEstimate(
            flops=40 * rows * rows * lanes, bytes_accessed=14 * rows * lanes, transcendentals=0
        ),
        name="attn_bwd",
    )(qkv, qkv, qkv, bias, *letters)


def fc1_kernel(x_ref, w_ref, act_ref, slope_ref):
    act, slope = gelu_parts(mxu(x_ref[...], w_ref[...], NN))
    act_ref[...] = act.astype(jnp.bfloat16)
    slope_ref[...] = slope.astype(jnp.bfloat16)


def fc1_gelu(x, w):
    rows, depth = x.shape
    cols = w.shape[1]
    tile = 512
    spec = pl.BlockSpec((rows, tile), lambda i: (0, i))
    return pl.pallas_call(
        fc1_kernel,
        grid=(cols // tile,),
        in_specs=[
            pl.BlockSpec((rows, depth), lambda i: (0, 0)),
            pl.BlockSpec((depth, tile), lambda i: (0, i)),
        ],
        out_specs=(spec, spec),
        out_shape=(jax.ShapeDtypeStruct((rows, cols), jnp.bfloat16),) * 2,
        compiler_params=pltpu.CompilerParams(vmem_limit_bytes=VMEM_BYTES),
        cost_estimate=pl.CostEstimate(
            flops=2 * rows * cols * depth,
            bytes_accessed=2 * (rows * depth + depth * cols + 2 * rows * cols),
            transcendentals=0,
        ),
        name="fc1_gelu",
    )(x, w)


def normalize(v):
    center = v - jnp.mean(v, axis=-1, keepdims=True)
    spread = jnp.mean(center * center, axis=-1, keepdims=True)
    inv = lax.rsqrt(spread + EPS)
    return center * inv, inv


def norm_back(g, u, inv, gain):
    q = g * gain
    back = inv * (
        q - jnp.mean(q, axis=-1, keepdims=True) - u * jnp.mean(q * u, axis=-1, keepdims=True)
    )
    return back, jnp.sum(g * u, axis=0), jnp.sum(g, axis=0)


def per_device(
    tokens,
    image_count,
    norm_params,
    w_qkv,
    w_proj,
    w_fc1,
    w_fc2,
    w_unpatch,
    w_dec1,
    b_dec1,
    w_dec2,
    cot_out,
    cot_dec,
):
    seq_count = lax.axis_size("seq")
    rank = lax.axis_index("seq")
    scene_rank = lax.axis_index("scene")
    tok_rows, width = tokens.shape
    head_dim = width // H
    cols = width // seq_count
    cells = TG * TG
    bf16, f32 = jnp.bfloat16, jnp.float32
    live_image = image_count[0] // seq_count
    pos = jnp.arange(tok_rows, dtype=jnp.int32)
    row_live = (pos >= IMG_DEV) | (pos < live_image)
    bias = jnp.broadcast_to(
        jnp.where(row_live, 0.0, NEG_FILL).astype(bf16)[:, None], (tok_rows, 2 * head_dim)
    )

    def hop(x, step):
        return lax.ppermute(
            x, "seq", [(i, i + step) for i in range(seq_count) if 0 <= i + step < seq_count]
        )

    def turn(x, step):
        return lax.ppermute(x, "seq", [(i, (i + step) % seq_count) for i in range(seq_count)])

    def ahead(d):
        return lax.rem(rank + d, seq_count)

    def behind(d):
        return lax.rem(rank - d + seq_count, seq_count)

    def piece(x, chunk, size, axis):
        return lax.dynamic_slice_in_dim(x, chunk * size, size, axis)

    cot_row = jnp.pad(cot_dec.reshape(1, -1), ((0, 15), (0, width - cot_dec.size)))
    parcel = jnp.concatenate([tokens, cot_row], axis=0)
    ups, downs = [parcel], [parcel]

    def move_on():
        ups.append(hop(ups[-1], 1))
        downs.append(hop(downs[-1], -1))

    move_on()
    move_on()

    def slot(d):
        pick = ups[d]
        for r in range(d):
            pick = jnp.where(rank == r, downs[d - r], pick)
        return pick

    lanes = 2 * head_dim
    pairs = width // lanes
    shard = w_qkv.shape[0]
    scene_count = width // shard

    def gather(w):
        return lax.all_gather(w.astype(bf16), "scene", axis=0, tiled=True)

    pair_order = w_qkv.astype(bf16).reshape(shard, 3, pairs, lanes).transpose(0, 2, 1, 3)
    first_w = lax.all_gather(
        jnp.concatenate(
            [
                pair_order.reshape(shard, 3 * width),
                w_unpatch.astype(bf16),
                jnp.pad(norm_params.astype(bf16), ((0, 0), (0, 124))),
            ],
            axis=1,
        ),
        "scene",
        axis=0,
        tiled=True,
    )
    qkv_w = first_w[:, : 3 * width]
    unpatch_w = first_w[:, 3 * width : 3 * width + PP * TF]
    norm_full = first_w[:, 3 * width + PP * TF : 3 * width + PP * TF + 4].astype(f32)
    gain_one, shift_one, gain_two, shift_two = (norm_full[:, i] for i in range(4))
    proj_w = gather(w_proj)
    fc1_w = gather(w_fc1)
    fc2_w = gather(w_fc2)

    slots, a1, qkv_rows = [], [], []
    state = None
    for d in range(seq_count):
        slots.append(slot(d))
        u, _ = normalize(slots[d][:tok_rows].astype(f32))
        a = (u * gain_one + shift_one).astype(bf16)
        qkv = mxu(a, qkv_w, NN).astype(bf16)
        a1.append(a)
        qkv_rows.append(qkv)
        if d == 0:
            q_rows = qkv
        state = attn_fwd(q_rows, qkv, bias, state, d == seq_count - 1, head_dim)
        if d + 2 < seq_count:
            ups[d + 2], downs[d + 2], state = lax.optimization_barrier(
                (ups[d + 2], downs[d + 2], state)
            )
            if d + 3 < seq_count:
                move_on()
    mixed, lse = state
    lse = lse.reshape(H, tok_rows)

    def in_turn(blocks):
        out = jnp.zeros((seq_count * tok_rows, blocks[0].shape[1]), blocks[0].dtype)
        for d, block in enumerate(blocks):
            at = jnp.where(rank >= d, d, rank - d + seq_count) * tok_rows
            out = lax.dynamic_update_slice_in_dim(out, block, at, 0)
        return out

    inputs_f = tokens.astype(f32)
    middle = inputs_f + mxu(mixed, proj_w, NN)
    u_two, inv_two = normalize(middle)
    a2 = (u_two * gain_two + shift_two).astype(bf16)
    act, slope = fc1_gelu(a2, fc1_w)
    triplane = (middle[IMG_DEV:] + mxu(act[IMG_DEV:], fc2_w, NN)).astype(bf16)
    tri_rows = tok_rows - IMG_DEV
    planes = mxu(triplane, unpatch_w, NN).astype(bf16)
    all_planes = jnp.zeros((seq_count * tri_rows, PP * TF), bf16)
    for d in range(seq_count):
        got = turn(planes, d) if d else planes
        all_planes = lax.dynamic_update_slice_in_dim(all_planes, got, behind(d) * tri_rows, 0)
    image_live = pos[:IMG_DEV] < live_image
    image_out = jnp.where(
        image_live[:, None], middle[:IMG_DEV] + mxu(act[:IMG_DEV], fc2_w, NN), 0.0
    ).astype(bf16)
    image_out, all_planes = lax.optimization_barrier((image_out, all_planes))
    block_out = jnp.concatenate([image_out, triplane], axis=0)

    cot_rows = jnp.zeros((seq_count, width), bf16)
    for d in range(seq_count):
        chunk = jnp.where(rank >= d, rank - d, d)
        cot_rows = lax.dynamic_update_slice_in_dim(
            cot_rows, slots[d][tok_rows : tok_rows + 1], chunk, 0
        )
    cot_cells = cot_rows[:, : cot_dec.size].reshape(cells, OUT * PP)
    planes_f = all_planes.astype(f32)
    feat = planes_f[:cells] + planes_f[cells : 2 * cells] + planes_f[2 * cells :]
    dh = w_dec1.shape[1]
    eye = jnp.eye(PP, dtype=f32)
    dec1 = jnp.einsum("fh,pq->pfqh", w_dec1, eye).reshape(PP * TF, PP * dh)
    dec2 = jnp.einsum("ho,pq->phoq", w_dec2, eye).reshape(PP * dh, OUT * PP)
    hidden_pre = exact(feat, dec1, NN) + jnp.tile(b_dec1, PP)
    zdec, zslope = gelu_parts(hidden_pre)
    decoded_all = exact(zdec, dec2, NN)
    cells_dev = cells // seq_count
    decoded = lax.dynamic_slice_in_dim(decoded_all, rank * cells_dev, cells_dev, 0)
    cot_f = cot_cells.astype(f32)
    grad_hidden = exact(cot_f, dec2, NT) * zslope
    gfeat = exact(grad_hidden, dec1, NT).astype(bf16)
    grad_w2 = jnp.einsum(
        "phop->ho", exact(zdec, cot_f, TN).reshape(PP, dh, OUT, PP)
    )
    grad_b1 = jnp.sum(jnp.sum(grad_hidden, axis=0).reshape(PP, dh), axis=0)
    grad_w1 = jnp.einsum(
        "pfph->fh", exact(feat, grad_hidden, TN).reshape(PP, TF, PP, dh)
    )
    plane_grad = lax.dynamic_slice_in_dim(
        jnp.concatenate([gfeat] * 4, axis=0), lax.rem(rank * tri_rows, cells), tri_rows, 0
    )
    grad_unpatch = mxu(triplane, plane_grad, TN)
    grad_tri = mxu(plane_grad, unpatch_w, NT)

    grad_result = jnp.where(row_live[:, None], cot_out.astype(f32), 0.0)
    grad_result = jnp.concatenate([grad_result[:IMG_DEV], grad_result[IMG_DEV:] + grad_tri], axis=0)
    branch = grad_result.astype(bf16)
    fc2_grad = mxu(act, branch, TN).astype(bf16)
    grad_pre = (mxu(branch, fc2_w, NT) * slope.astype(f32)).astype(bf16)
    back_two, gain_grad_two, shift_grad_two = norm_back(
        mxu(grad_pre, fc1_w, NT), u_two, inv_two, gain_two
    )
    grad_mid = grad_result + back_two
    mid_grad = grad_mid.astype(bf16)
    grad_mixed = mxu(mid_grad, proj_w, NT).astype(bf16)
    head_of = (jnp.arange(width) // head_dim)[None, :] == jnp.arange(H)[:, None]
    delta = exact(
        head_of.astype(f32), grad_mixed.astype(f32) * mixed.astype(f32), NT
    )
    pairs_dev = pairs // seq_count
    parts, rest = [], jnp.stack([lse, delta])
    for _ in range(3):
        top = lax.reduce_precision(rest, 8, 7)
        parts.append(top.astype(bf16))
        rest = rest - top
    stats = jnp.stack(parts).reshape(3, 2, pairs, 2, tok_rows // lanes, lanes)
    stats = stats.transpose(0, 1, 3, 4, 2, 5).reshape(-1, width)
    letter = jnp.concatenate(
        [grad_mixed, jnp.pad(stats, ((0, -stats.shape[0] % 16), (0, 0)))], axis=0
    )
    letter, late_a2, late_pre, late_mid, qkv_rows = lax.optimization_barrier(
        (letter, a2, grad_pre, mid_grad, qkv_rows)
    )
    letters = [piece(letter, ahead(d), cols, 1) for d in range(seq_count)]
    letters = [turn(x, d) if d else x for d, x in enumerate(letters)]
    own_all = in_turn([piece(x, rank, 3 * cols, 1) for x in qkv_rows])
    fc1_grad = mxu(late_a2, late_pre, TN).astype(bf16)
    norm_cols = jnp.stack([gain_grad_two, shift_grad_two], axis=1).astype(bf16)
    misc_grad = jnp.concatenate(
        [
            mxu(mixed, late_mid, TN).astype(bf16),
            grad_unpatch.astype(bf16),
            jnp.pad(norm_cols, ((0, 0), (0, 128 * seq_count - PP * TF - 2))),
        ],
        axis=1,
    )

    def over_scene(g):
        return lax.psum_scatter(g, "scene", scatter_dimension=0, tiled=True)

    fc2_part = over_scene(fc2_grad)
    dec_flat = jnp.concatenate([grad_w1.reshape(-1), grad_b1, grad_w2.reshape(-1)])
    dec_flat = jnp.pad(dec_flat, (0, -dec_flat.size % width)).reshape(-1, width)
    own_all, letters, fc2_part, fc1_grad, misc_grad, dec_flat = lax.optimization_barrier(
        (own_all, letters, fc2_part, fc1_grad, misc_grad, dec_flat)
    )
    fc1_part = over_scene(fc1_grad)
    misc_part = over_scene(misc_grad)

    def sum_pieces(*parts):
        def block(at):
            cut = [piece(part, at, part.shape[1] // seq_count, 1) for part in parts]
            return jnp.concatenate(cut, axis=1) if len(cut) > 1 else cut[0]

        return [turn(block(ahead(d)), d) if d else block(rank) for d in range(seq_count)]

    def blocks_of(pieces):
        mine = sum(x.astype(f32) for x in pieces).astype(bf16)
        return [turn(mine, d) if d else mine for d in range(seq_count)]

    def side_by_side(blocks):
        size = blocks[0].shape[1]
        out = jnp.zeros((blocks[0].shape[0], size * seq_count), f32)
        for d, got in enumerate(blocks):
            out = lax.dynamic_update_slice_in_dim(out, got.astype(f32), behind(d) * size, 1)
        return out

    def exchange(mine):
        pieces = [piece(mine, (seq_count - d) % seq_count, tok_rows, 0) for d in range(seq_count)]
        return [turn(x, d) if d else x for d, x in enumerate(pieces)]

    fc2_pieces = sum_pieces(fc2_part)
    moved, head_grads = [], []
    for p in range(pairs_dev):
        mine = attn_bwd(own_all, letters, bias, p, head_dim)
        if p == 0:
            own_all, mine, fc2_pieces = lax.optimization_barrier((own_all, mine, fc2_pieces))
            fc2_blocks = blocks_of(fc2_pieces)
        else:
            mine, moved[-1], head_grads[-1], a1, fc2_blocks, fc1_part, misc_part = (
                lax.optimization_barrier(
                    (mine, moved[-1], head_grads[-1], a1, fc2_blocks, fc1_part, misc_part)
                )
            )
        head_grads.append(mine)
        moved.append(exchange(mine))
    moved[-1][1], head_grads = lax.optimization_barrier((moved[-1][1], head_grads))
    a1_all = in_turn(a1)
    own_qkv = [mxu(a1_all, part, TN).astype(bf16) for part in head_grads]
    qkv_part = over_scene(jnp.concatenate(own_qkv, axis=1))
    grad_fc2 = side_by_side(fc2_blocks)

    def pair_weights(p):
        return jnp.concatenate(
            [
                lax.dynamic_slice_in_dim(
                    qkv_w, behind(d) * 3 * cols + p * 3 * lanes, 3 * lanes, 1
                )
                for d in range(seq_count)
            ],
            axis=1,
        )

    def pair_part(pieces, weights):
        return mxu(jnp.concatenate(pieces, axis=1), weights, NT)

    grad_in = sum(pair_part(moved[p], pair_weights(p)) for p in range(pairs_dev - 1))
    last_weights = pair_weights(pairs_dev - 1)
    moved[-1], grad_in, last_weights, grad_fc2, fc1_part, misc_part = lax.optimization_barrier(
        (moved[-1], grad_in, last_weights, grad_fc2, fc1_part, misc_part)
    )
    wide_pieces = sum_pieces(fc1_part, misc_part)
    grad_in = grad_in + pair_part(moved[-1], last_weights)
    u_one, inv_one = normalize(inputs_f)
    back_one, gain_grad_one, shift_grad_one = norm_back(grad_in, u_one, inv_one, gain_one)
    grad_tokens = (grad_mid + back_one).astype(bf16)

    sums = jnp.concatenate([jnp.stack([gain_grad_one, shift_grad_one]), dec_flat], axis=0)
    sums, wide_pieces = lax.optimization_barrier((sums, wide_pieces))
    wide_blocks = blocks_of(wide_pieces)
    cut = w_fc1.shape[1] // seq_count
    grad_fc1 = side_by_side([x[:, :cut] for x in wide_blocks])
    grad_misc = side_by_side([x[:, cut:] for x in wide_blocks])
    grad_proj = grad_misc[:, :width]
    grad_unp = grad_misc[:, width : width + PP * TF]
    norm_two = grad_misc[:, width + PP * TF : width + PP * TF + 2]
    qkv_all = side_by_side([turn(qkv_part, d) if d else qkv_part for d in range(seq_count)])
    grad_qkv = qkv_all.reshape(shard, pairs, 3, lanes).transpose(0, 2, 1, 3).reshape(shard, 3 * width)

    sums = lax.psum(sums, "scene")
    norm_one = lax.psum(lax.dynamic_slice_in_dim(sums[:2], scene_rank * shard, shard, 1), "seq").T
    dec_flat = sums[2:].reshape(-1)
    ends = (w_dec1.size, w_dec1.size + dh, w_dec1.size + dh + w_dec2.size)
    dec_grads = (
        dec_flat[: ends[0]].reshape(w_dec1.shape),
        dec_flat[ends[0] : ends[1]],
        dec_flat[ends[1] : ends[2]].reshape(w_dec2.shape),
    )
    return (
        block_out,
        decoded,
        grad_tokens,
        norm_one,
        norm_two,
        grad_qkv,
        grad_proj,
        grad_fc1,
        grad_fc2,
        grad_unp,
        dec_grads[0],
        dec_grads[1],
        dec_grads[2],
    )


def solution(mesh):
    rows = P(("scene", "seq"), None)
    shard = P("scene", None)
    in_specs = (
        rows, P("scene"), shard, shard, shard, shard, shard, shard, P(), P(), P(), rows, rows
    )
    out_specs = (rows,) * 3 + (shard,) * 7 + (P(),) * 3
    return jax.shard_map(
        per_device, mesh=mesh, in_specs=in_specs, out_specs=out_specs, check_vma=False
    )
```

```python
import functools

import jax
import jax.numpy as jnp
from jax import lax
from jax.experimental import pallas as pl
from jax.experimental.pallas import tpu as pltpu
from jax.sharding import PartitionSpec as P

H = 16
TF = 32
PP = 4
OUT = 4
TG = 16
IMG_DEV = 576

EPS = 1e-05
NEG_FILL = -1e30
LOG2E = 1.4426950408889634
VMEM_BYTES = 60 * 2**20

NT = (((1,), (1,)), ((), ()))
NN = (((1,), (0,)), ((), ()))
TN = (((0,), (0,)), ((), ()))


def mxu(left, right, dims):
    return lax.dot_general(left, right, dims, preferred_element_type=jnp.float32)


def exact(left, right, dims):
    return lax.dot_general(
        left, right, dims, precision=lax.Precision.HIGHEST, preferred_element_type=jnp.float32
    )


def gelu_parts(v):
    a = jnp.abs(v) * 0.7071067811865476
    t = 1.0 / (1.0 + 0.3275911 * a)
    poly = t * (
        0.254829592
        + t * (-0.284496736 + t * (1.421413741 + t * (-1.453152027 + t * 1.061405429)))
    )
    e = jnp.exp(-a * a)
    tail = 0.5 * poly * e
    cdf = jnp.where(v >= 0.0, 1.0 - tail, tail)
    return v * cdf, cdf + v * (e * 0.3989422804014327)


def pair_keys(block, bias, head, half):
    lane = lax.broadcasted_iota(jnp.int32, block.shape, 1)
    mine = (lane < half) if head == 0 else (lane >= half)
    flag = half if head == 0 else 0
    zero = jnp.zeros_like(block)
    return jnp.where(mine, block, jnp.where(lane == flag, bias, zero))


def pair_queries(block, head, half):
    lane = lax.broadcasted_iota(jnp.int32, block.shape, 1)
    mine = (lane < half) if head == 0 else (lane >= half)
    flag = half if head == 0 else 0
    zero = jnp.zeros_like(block)
    return jnp.where(mine, block, jnp.where(lane == flag, jnp.ones_like(block), zero))


def pair_mask(block, head, half):
    lane = lax.broadcasted_iota(jnp.int32, block.shape, 1)
    mine = (lane < half) if head == 0 else (lane >= half)
    return jnp.where(mine, block, jnp.zeros_like(block))


def attn_fwd_kernel(*refs, first, last, sub, scale):
    q_ref, k_ref, v_ref, bias_ref = refs[:4]
    refs = refs[4:]
    if not first:
        acc_in, peak_in = refs[:2]
        refs = refs[2:]
    out_a, out_b, s_buf, k_buf, vt_buf, acc_buf = refs
    tq, lanes = q_ref.shape
    n = k_ref.shape[0] // sub
    half = lanes // 2
    q = q_ref[...]
    qs = [pair_queries(q, h, half) for h in range(2)]
    ones = jnp.ones((16, sub), jnp.bfloat16)
    for i in range(n):
        rows = slice(i * sub, i * sub + sub)
        kb, bias = k_ref[rows, :], bias_ref[rows, :]
        vt = v_ref[rows, :].T
        for h in range(2):
            k_buf[i, h] = pair_keys(kb, bias, h, half)
            vt_buf[i, h, :half] = vt[h * half : h * half + half]
            vt_buf[i, h, half:] = ones

    def score(j, peak):
        out = []
        for h in range(2):
            s = mxu(k_buf[j, h], qs[h], NT)
            s_buf[j % 2, h] = s
            out.append(jnp.maximum(peak[h], jnp.max(s, axis=0, keepdims=True)))
        return out

    def mix(j, before, peak):
        for h in range(2):
            p = jnp.exp2((s_buf[j % 2, h] - peak[h]) * scale).astype(jnp.bfloat16)
            part = mxu(vt_buf[j, h], p, NN)
            if first and j == 0:
                acc_buf[h] = part
            else:
                fade = jnp.exp2((before[h] - peak[h]) * scale)
                old = acc_in[h] if j == 0 else acc_buf[h]
                acc_buf[h] = old * fade + part

    if first:
        before = [jnp.full((1, tq), -3e38, jnp.float32)] * 2
    else:
        before = [peak_in[h : h + 1, :] for h in range(2)]
    peak = score(0, before)
    for j in range(1, n):
        fresh = score(j, peak)
        mix(j - 1, before, peak)
        before, peak = peak, fresh
    mix(n - 1, before, peak)
    if last:
        outs = []
        for h in range(2):
            acc = acc_buf[h]
            total = acc[half : half + 1]
            outs.append(acc[:half] / total)
            out_b[h : h + 1, :] = peak[h] * scale + jnp.log2(total)
        out_a[...] = jnp.concatenate(outs, axis=0).T.astype(jnp.bfloat16)
    else:
        for h in range(2):
            out_a[h] = acc_buf[h]
            out_b[h : h + 1, :] = peak[h]


def attn_fwd(q_rows, kv_rows, bias, state, last, head_dim):
    lanes = 2 * head_dim
    tq, tk = q_rows.shape[0], kv_rows.shape[0]
    pairs = kv_rows.shape[1] // (3 * lanes)
    width = pairs * lanes
    ext = head_dim + 16
    sub = 256
    first = state is None
    block = lambda rows, off: pl.BlockSpec((rows, lanes), lambda h: (0, 3 * h + off))
    stat = pl.BlockSpec((None, 2, tq), lambda h: (h, 0, 0))
    carry = pl.BlockSpec((None, 2, ext, tq), lambda h: (h, 0, 0, 0))
    stat_shape = jax.ShapeDtypeStruct((pairs, 2, tq), jnp.float32)
    if last:
        out_specs = (pl.BlockSpec((tq, lanes), lambda h: (0, h)), stat)
        out_shape = (jax.ShapeDtypeStruct((tq, width), jnp.bfloat16), stat_shape)
    else:
        out_specs = (carry, stat)
        out_shape = (jax.ShapeDtypeStruct((pairs, 2, ext, tq), jnp.float32), stat_shape)
    return pl.pallas_call(
        functools.partial(
            attn_fwd_kernel, first=first, last=last, sub=sub, scale=head_dim**-0.5 * LOG2E
        ),
        grid=(pairs,),
        in_specs=[block(tq, 0), block(tk, 1), block(tk, 2), pl.BlockSpec((tk, lanes), lambda h: (0, 0))]
        + ([] if first else [carry, stat]),
        out_specs=out_specs,
        out_shape=out_shape,
        scratch_shapes=[
            pltpu.VMEM((2, 2, sub, tq), jnp.float32),
            pltpu.VMEM((tk // sub, 2, sub, lanes), jnp.bfloat16),
            pltpu.VMEM((tk // sub, 2, ext, sub), jnp.bfloat16),
            pltpu.VMEM((2, ext, tq), jnp.float32),
        ],
        compiler_params=pltpu.CompilerParams(vmem_limit_bytes=VMEM_BYTES),
        cost_estimate=pl.CostEstimate(
            flops=16 * tq * tk * width, bytes_accessed=2 * width * (2 * tq + 2 * tk), transcendentals=0
        ),
        name="attn_fwd",
    )(q_rows, kv_rows, kv_rows, bias, *(() if first else state))


def attn_bwd_kernel(*refs, tk, tq, scale, post):
    q_ref, k_ref, v_ref, bias_ref = refs[:4]
    letters = refs[4:-14]
    out_ref = refs[-14]
    s_buf, dp_buf, lse_ref, del_ref, qm, km, dom, kt, qt, dot, dqa, dka, dva = refs[-13:]
    nq = q_ref.shape[0] // tq
    nk = k_ref.shape[0] // tk
    half = q_ref.shape[1] // 2
    for i in range(nk):
        rows = slice(i * tk, i * tk + tk)
        for h in range(2):
            km[h, rows] = pair_keys(k_ref[rows, :], bias_ref[...], h, half)
    for h in range(2):
        qm[h] = pair_queries(q_ref[...], h, half)
    kt[...] = k_ref[...].T
    qt[...] = q_ref[...].T
    per_row = tk // (2 * half)
    for i, letter in enumerate(letters):
        rows = slice(i * tk, i * tk + tk)
        do = letter[:tk, :]
        dot[:, rows] = do.T
        for h in range(2):
            dom[h, rows] = pair_mask(do, h, half)
        count = 4 * per_row
        stat = letter[tk : tk + 3 * count, :].astype(jnp.float32)
        stat = stat[:count] + stat[count : 2 * count] + stat[2 * count :]
        for kind, buf in enumerate((lse_ref, del_ref)):
            for h in range(2):
                at = (kind * 2 + h) * per_row
                buf[h : h + 1, rows] = jnp.concatenate(
                    [stat[at + j : at + j + 1] for j in range(per_row)], axis=1
                )
    for acc in (dqa, dka, dva):
        acc[...] = jnp.zeros(acc.shape, jnp.float32)

    def place(t):
        if isinstance(t, int):
            return t // nq * tk, t % nq * tq, t % 2
        return (
            pl.multiple_of(lax.div(t, nq) * tk, tk),
            pl.multiple_of(lax.rem(t, nq) * tq, tq),
            lax.rem(t, 2),
        )

    def score(t):
        k0, q0, slot = place(t)
        ks, qs = pl.ds(k0, tk), pl.ds(q0, tq)
        vv = v_ref[ks, :]
        for h in range(2):
            s_buf[slot, h] = mxu(km[h, ks, :], qm[h, qs, :], NT)
            dp_buf[slot, h] = mxu(vv, dom[h, qs, :], NT)

    def grads(t):
        k0, q0, slot = place(t)
        ks, qs = pl.ds(k0, tk), pl.ds(q0, tq)
        for h in range(2):
            p = jnp.exp2(s_buf[slot, h] * scale - lse_ref[h : h + 1, qs])
            ds = (p * (dp_buf[slot, h] - del_ref[h : h + 1, qs])).astype(jnp.bfloat16)
            pb = p.astype(jnp.bfloat16)
            r = slice(half * h, half * h + half)
            dqa[r, qs] += mxu(kt[r, ks], ds, NN)
            dva[r, ks] += mxu(dot[r, qs], pb, NT)
            dka[r, ks] += mxu(qt[r, qs], ds, NT)

    score(0)

    def body(t, carry):
        score(t)
        grads(t - 1)
        return carry

    lax.fori_loop(1, nq * nk, body, 0)
    grads(nq * nk - 1)
    lanes = 2 * half
    out_ref[:, :lanes] = (dqa[...] * post).T.astype(jnp.bfloat16)
    out_ref[:, lanes : 2 * lanes] = (dka[...] * post).T.astype(jnp.bfloat16)
    out_ref[:, 2 * lanes :] = dva[...].T.astype(jnp.bfloat16)


def attn_bwd(qkv, letters, bias, pair, head_dim):
    rows = qkv.shape[0]
    tk = bias.shape[0]
    lanes = 2 * head_dim
    block = lambda at: pl.BlockSpec((rows, lanes), lambda h: (0, at))
    return pl.pallas_call(
        functools.partial(
            attn_bwd_kernel, tk=tk, tq=tk, scale=head_dim**-0.5 * LOG2E, post=head_dim**-0.5
        ),
        grid=(1,),
        in_specs=[block(3 * pair), block(3 * pair + 1), block(3 * pair + 2)]
        + [pl.BlockSpec((tk, lanes), lambda h: (0, 0))]
        + [pl.BlockSpec((letters[0].shape[0], lanes), lambda h: (0, pair))] * len(letters),
        out_specs=pl.BlockSpec((rows, 3 * lanes), lambda h: (0, 0)),
        out_shape=jax.ShapeDtypeStruct((rows, 3 * lanes), jnp.bfloat16),
        scratch_shapes=[
            pltpu.VMEM((2, 2, tk, tk), jnp.float32),
            pltpu.VMEM((2, 2, tk, tk), jnp.float32),
            pltpu.VMEM((2, rows), jnp.float32),
            pltpu.VMEM((2, rows), jnp.float32),
            pltpu.VMEM((2, rows, lanes), jnp.bfloat16),
            pltpu.VMEM((2, rows, lanes), jnp.bfloat16),
            pltpu.VMEM((2, rows, lanes), jnp.bfloat16),
            pltpu.VMEM((lanes, rows), jnp.bfloat16),
            pltpu.VMEM((lanes, rows), jnp.bfloat16),
            pltpu.VMEM((lanes, rows), jnp.bfloat16),
            pltpu.VMEM((lanes, rows), jnp.float32),
            pltpu.VMEM((lanes, rows), jnp.float32),
            pltpu.VMEM((lanes, rows), jnp.float32),
        ],
        compiler_params=pltpu.CompilerParams(vmem_limit_bytes=VMEM_BYTES),
        cost_estimate=pl.CostEstimate(
            flops=40 * rows * rows * lanes, bytes_accessed=14 * rows * lanes, transcendentals=0
        ),
        name="attn_bwd",
    )(qkv, qkv, qkv, bias, *letters)


def fc1_kernel(x_ref, w_ref, act_ref, slope_ref):
    act, slope = gelu_parts(mxu(x_ref[...], w_ref[...], NN))
    act_ref[...] = act.astype(jnp.bfloat16)
    slope_ref[...] = slope.astype(jnp.bfloat16)


def fc1_gelu(x, w):
    rows, depth = x.shape
    cols = w.shape[1]
    tile = 512
    spec = pl.BlockSpec((rows, tile), lambda i: (0, i))
    return pl.pallas_call(
        fc1_kernel,
        grid=(cols // tile,),
        in_specs=[
            pl.BlockSpec((rows, depth), lambda i: (0, 0)),
            pl.BlockSpec((depth, tile), lambda i: (0, i)),
        ],
        out_specs=(spec, spec),
        out_shape=(jax.ShapeDtypeStruct((rows, cols), jnp.bfloat16),) * 2,
        compiler_params=pltpu.CompilerParams(vmem_limit_bytes=VMEM_BYTES),
        cost_estimate=pl.CostEstimate(
            flops=2 * rows * cols * depth,
            bytes_accessed=2 * (rows * depth + depth * cols + 2 * rows * cols),
            transcendentals=0,
        ),
        name="fc1_gelu",
    )(x, w)


def normalize(v):
    center = v - jnp.mean(v, axis=-1, keepdims=True)
    spread = jnp.mean(center * center, axis=-1, keepdims=True)
    inv = lax.rsqrt(spread + EPS)
    return center * inv, inv


def norm_back(g, u, inv, gain):
    q = g * gain
    back = inv * (
        q - jnp.mean(q, axis=-1, keepdims=True) - u * jnp.mean(q * u, axis=-1, keepdims=True)
    )
    return back, jnp.sum(g * u, axis=0), jnp.sum(g, axis=0)


def per_device(
    tokens,
    image_count,
    norm_params,
    w_qkv,
    w_proj,
    w_fc1,
    w_fc2,
    w_unpatch,
    w_dec1,
    b_dec1,
    w_dec2,
    cot_out,
    cot_dec,
):
    seq_count = lax.axis_size("seq")
    rank = lax.axis_index("seq")
    scene_rank = lax.axis_index("scene")
    tok_rows, width = tokens.shape
    head_dim = width // H
    cols = width // seq_count
    cells = TG * TG
    bf16, f32 = jnp.bfloat16, jnp.float32
    live_image = image_count[0] // seq_count
    pos = jnp.arange(tok_rows, dtype=jnp.int32)
    row_live = (pos >= IMG_DEV) | (pos < live_image)
    bias = jnp.broadcast_to(
        jnp.where(row_live, 0.0, NEG_FILL).astype(bf16)[:, None], (tok_rows, 2 * head_dim)
    )

    def hop(x, step):
        return lax.ppermute(
            x, "seq", [(i, i + step) for i in range(seq_count) if 0 <= i + step < seq_count]
        )

    def turn(x, step):
        return lax.ppermute(x, "seq", [(i, (i + step) % seq_count) for i in range(seq_count)])

    def ahead(d):
        return lax.rem(rank + d, seq_count)

    def behind(d):
        return lax.rem(rank - d + seq_count, seq_count)

    def piece(x, chunk, size, axis):
        return lax.dynamic_slice_in_dim(x, chunk * size, size, axis)

    cot_row = jnp.pad(cot_dec.reshape(1, -1), ((0, 15), (0, width - cot_dec.size)))
    parcel = jnp.concatenate([tokens, cot_row], axis=0)
    ups, downs = [parcel], [parcel]

    def move_on():
        ups.append(hop(ups[-1], 1))
        downs.append(hop(downs[-1], -1))

    move_on()
    move_on()

    def slot(d):
        pick = ups[d]
        for r in range(d):
            pick = jnp.where(rank == r, downs[d - r], pick)
        return pick

    lanes = 2 * head_dim
    pairs = width // lanes
    shard = w_qkv.shape[0]
    scene_count = width // shard

    def gather(w):
        return lax.all_gather(w.astype(bf16), "scene", axis=0, tiled=True)

    pair_order = w_qkv.astype(bf16).reshape(shard, 3, pairs, lanes).transpose(0, 2, 1, 3)
    first_w = lax.all_gather(
        jnp.concatenate(
            [
                pair_order.reshape(shard, 3 * width),
                w_unpatch.astype(bf16),
                jnp.pad(norm_params.astype(bf16), ((0, 0), (0, 124))),
            ],
            axis=1,
        ),
        "scene",
        axis=0,
        tiled=True,
    )
    qkv_w = first_w[:, : 3 * width]
    unpatch_w = first_w[:, 3 * width : 3 * width + PP * TF]
    norm_full = first_w[:, 3 * width + PP * TF : 3 * width + PP * TF + 4].astype(f32)
    gain_one, shift_one, gain_two, shift_two = (norm_full[:, i] for i in range(4))
    proj_w = gather(w_proj)
    fc1_w = gather(w_fc1)
    fc2_w = gather(w_fc2)

    slots, a1, qkv_rows = [], [], []
    state = None
    for d in range(seq_count):
        slots.append(slot(d))
        u, _ = normalize(slots[d][:tok_rows].astype(f32))
        a = (u * gain_one + shift_one).astype(bf16)
        qkv = mxu(a, qkv_w, NN).astype(bf16)
        a1.append(a)
        qkv_rows.append(qkv)
        if d == 0:
            q_rows = qkv
        state = attn_fwd(q_rows, qkv, bias, state, d == seq_count - 1, head_dim)
        if d + 2 < seq_count:
            ups[d + 2], downs[d + 2], state = lax.optimization_barrier(
                (ups[d + 2], downs[d + 2], state)
            )
            if d + 3 < seq_count:
                move_on()
    mixed, lse = state
    lse = lse.reshape(H, tok_rows)

    def in_turn(blocks):
        out = jnp.zeros((seq_count * tok_rows, blocks[0].shape[1]), blocks[0].dtype)
        for d, block in enumerate(blocks):
            at = jnp.where(rank >= d, d, rank - d + seq_count) * tok_rows
            out = lax.dynamic_update_slice_in_dim(out, block, at, 0)
        return out

    inputs_f = tokens.astype(f32)
    middle = inputs_f + mxu(mixed, proj_w, NN)
    u_two, inv_two = normalize(middle)
    a2 = (u_two * gain_two + shift_two).astype(bf16)
    act, slope = fc1_gelu(a2, fc1_w)
    triplane = (middle[IMG_DEV:] + mxu(act[IMG_DEV:], fc2_w, NN)).astype(bf16)
    tri_rows = tok_rows - IMG_DEV
    planes = mxu(triplane, unpatch_w, NN).astype(bf16)
    all_planes = jnp.zeros((seq_count * tri_rows, PP * TF), bf16)
    for d in range(seq_count):
        got = turn(planes, d) if d else planes
        all_planes = lax.dynamic_update_slice_in_dim(all_planes, got, behind(d) * tri_rows, 0)
    image_live = pos[:IMG_DEV] < live_image
    image_out = jnp.where(
        image_live[:, None], middle[:IMG_DEV] + mxu(act[:IMG_DEV], fc2_w, NN), 0.0
    ).astype(bf16)
    image_out, all_planes = lax.optimization_barrier((image_out, all_planes))
    block_out = jnp.concatenate([image_out, triplane], axis=0)

    cot_rows = jnp.zeros((seq_count, width), bf16)
    for d in range(seq_count):
        chunk = jnp.where(rank >= d, rank - d, d)
        cot_rows = lax.dynamic_update_slice_in_dim(
            cot_rows, slots[d][tok_rows : tok_rows + 1], chunk, 0
        )
    cot_cells = cot_rows[:, : cot_dec.size].reshape(cells, OUT * PP)
    planes_f = all_planes.astype(f32)
    feat = planes_f[:cells] + planes_f[cells : 2 * cells] + planes_f[2 * cells :]
    dh = w_dec1.shape[1]
    def same(shape, row_of, col_of):
        row = lax.broadcasted_iota(jnp.int32, shape, 0)
        col = lax.broadcasted_iota(jnp.int32, shape, 1)
        return row_of(row) == col_of(col)

    diag_one = same((PP * TF, PP * dh), lambda r: r // TF, lambda c: c // dh)
    diag_two = same((PP * dh, OUT * PP), lambda r: r // dh, lambda c: c % PP)
    widen = same((OUT, OUT * PP), lambda r: r, lambda c: c // PP).astype(f32)
    dec1 = jnp.where(diag_one, jnp.tile(w_dec1, (PP, PP)), 0.0)
    dec2 = jnp.where(diag_two, jnp.tile(exact(w_dec2, widen, NN), (PP, 1)), 0.0)
    hidden_pre = exact(feat, dec1, NN) + jnp.tile(b_dec1, PP)
    zdec, zslope = gelu_parts(hidden_pre)
    decoded_all = exact(zdec, dec2, NN)
    cells_dev = cells // seq_count
    decoded = lax.dynamic_slice_in_dim(decoded_all, rank * cells_dev, cells_dev, 0)
    cot_f = cot_cells.astype(f32)
    grad_hidden = exact(cot_f, dec2, NT) * zslope
    gfeat = exact(grad_hidden, dec1, NT).astype(bf16)
    wide_w2 = jnp.where(diag_two, exact(zdec, cot_f, TN), 0.0)
    grad_w2 = exact(sum(wide_w2[p * dh : p * dh + dh] for p in range(PP)), widen, NT)
    wide_b1 = jnp.sum(grad_hidden, axis=0, keepdims=True)
    grad_b1 = sum(wide_b1[0, p * dh : p * dh + dh] for p in range(PP))
    wide_w1 = exact(feat, grad_hidden, TN)
    grad_w1 = sum(wide_w1[p * TF : p * TF + TF, p * dh : p * dh + dh] for p in range(PP))
    plane_grad = lax.dynamic_slice_in_dim(
        jnp.concatenate([gfeat] * 4, axis=0), lax.rem(rank * tri_rows, cells), tri_rows, 0
    )
    grad_unpatch = mxu(triplane, plane_grad, TN)
    grad_tri = mxu(plane_grad, unpatch_w, NT)

    grad_result = jnp.where(row_live[:, None], cot_out.astype(f32), 0.0)
    grad_result = jnp.concatenate([grad_result[:IMG_DEV], grad_result[IMG_DEV:] + grad_tri], axis=0)
    branch = grad_result.astype(bf16)
    fc2_grad = mxu(act, branch, TN).astype(bf16)
    grad_pre = (mxu(branch, fc2_w, NT) * slope.astype(f32)).astype(bf16)
    back_two, gain_grad_two, shift_grad_two = norm_back(
        mxu(grad_pre, fc1_w, NT), u_two, inv_two, gain_two
    )
    grad_mid = grad_result + back_two
    mid_grad = grad_mid.astype(bf16)
    grad_mixed = mxu(mid_grad, proj_w, NT).astype(bf16)
    head_of = (jnp.arange(width) // head_dim)[None, :] == jnp.arange(H)[:, None]
    delta = exact(
        head_of.astype(f32), grad_mixed.astype(f32) * mixed.astype(f32), NT
    )
    pairs_dev = pairs // seq_count
    parts, rest = [], jnp.stack([lse, delta])
    for _ in range(3):
        top = lax.reduce_precision(rest, 8, 7)
        parts.append(top.astype(bf16))
        rest = rest - top
    stats = jnp.stack(parts).reshape(3, 2, pairs, 2, tok_rows // lanes, lanes)
    stats = stats.transpose(0, 1, 3, 4, 2, 5).reshape(-1, width)
    letter = jnp.concatenate(
        [grad_mixed, jnp.pad(stats, ((0, -stats.shape[0] % 16), (0, 0)))], axis=0
    )
    letter, late_a2, late_pre, late_mid, qkv_rows = lax.optimization_barrier(
        (letter, a2, grad_pre, mid_grad, qkv_rows)
    )
    late_rows = qkv_rows
    letters = [piece(letter, ahead(d), cols, 1) for d in range(seq_count)]
    letters = [turn(x, d) if d else x for d, x in enumerate(letters)]
    fc1_grad = mxu(late_a2, late_pre, TN).astype(bf16)
    norm_cols = jnp.stack([gain_grad_two, shift_grad_two], axis=1).astype(bf16)
    misc_grad = jnp.concatenate(
        [
            mxu(mixed, late_mid, TN).astype(bf16),
            grad_unpatch.astype(bf16),
            jnp.pad(norm_cols, ((0, 0), (0, 128 * seq_count - PP * TF - 2))),
        ],
        axis=1,
    )

    def over_scene(g):
        return lax.psum_scatter(g, "scene", scatter_dimension=0, tiled=True)

    fc2_part = over_scene(fc2_grad)
    dec_flat = jnp.concatenate([grad_w1.reshape(-1), grad_b1, grad_w2.reshape(-1)])
    dec_flat = jnp.pad(dec_flat, (0, -dec_flat.size % width)).reshape(-1, width)
    letters, fc2_part, fc1_grad, misc_grad, dec_flat, late_rows = lax.optimization_barrier(
        (letters, fc2_part, fc1_grad, misc_grad, dec_flat, late_rows)
    )
    fc1_part = over_scene(fc1_grad)

    def send(pieces):
        return [turn(x, d) if d else x for d, x in enumerate(pieces)]

    def cut(part):
        size = part.shape[1] // seq_count
        return [piece(part, ahead(d), size, 1) for d in range(seq_count)]

    def sum_pieces(part):
        return send(cut(part))

    def blocks_of(pieces):
        mine = sum(x.astype(f32) for x in pieces).astype(bf16)
        return [turn(mine, d) if d else mine for d in range(seq_count)]

    def side_by_side(blocks):
        size = blocks[0].shape[1]
        out = jnp.zeros((blocks[0].shape[0], size * seq_count), f32)
        for d, got in enumerate(blocks):
            out = lax.dynamic_update_slice_in_dim(out, got.astype(f32), behind(d) * size, 1)
        return out

    def cut_rows(mine):
        return [piece(mine, (seq_count - d) % seq_count, tok_rows, 0) for d in range(seq_count)]

    fc2_cut, late_rows = lax.optimization_barrier((cut(fc2_part), late_rows))
    fc2_pieces = send(fc2_cut)
    own_all = in_turn([piece(x, rank, 3 * cols, 1) for x in late_rows])
    own_all, letters, fc2_pieces = lax.optimization_barrier((own_all, letters, fc2_pieces))
    fc2_blocks = blocks_of(fc2_pieces)
    moved, head_grads = [], []
    for p in range(pairs_dev):
        mine = attn_bwd(own_all, letters, bias, p, head_dim)
        if p == 0:
            mine, fc2_blocks, fc1_part, misc_grad = lax.optimization_barrier(
                (mine, fc2_blocks, fc1_part, misc_grad)
            )
            misc_part = over_scene(misc_grad)
            own_all, rows_cut, fc1_cut = lax.optimization_barrier(
                (own_all, cut_rows(mine), cut(fc1_part))
            )
            fc1_pieces = send(fc1_cut)
        else:
            held = (mine, moved[-1], head_grads[-1], a1, qkv_w, fc1_pieces[:-1], fc1_cut[-1], misc_part)
            mine, moved[-1], head_grads[-1], a1, late_w, fc1_pieces[:-1], fc1_cut[-1], misc_part = (
                lax.optimization_barrier(held)
            )
            fc1_pieces[-1] = turn(fc1_cut[-1], seq_count - 1)
        head_grads.append(mine)
        moved.append(send(cut_rows(mine) if p else rows_cut))
    moved[-1][1], head_grads = lax.optimization_barrier((moved[-1][1], head_grads))
    a1_all = in_turn(a1)
    own_qkv = [mxu(a1_all, part, TN).astype(bf16) for part in head_grads]
    qkv_part = over_scene(jnp.concatenate(own_qkv, axis=1))
    grad_fc2 = side_by_side(fc2_blocks)

    def pair_weights(p):
        return jnp.concatenate(
            [
                lax.dynamic_slice_in_dim(
                    late_w, behind(d) * 3 * cols + p * 3 * lanes, 3 * lanes, 1
                )
                for d in range(seq_count)
            ],
            axis=1,
        )

    def pair_part(pieces, weights):
        return mxu(jnp.concatenate(pieces, axis=1), weights, NT)

    grad_in = sum(pair_part(moved[p], pair_weights(p)) for p in range(pairs_dev - 1))
    last_weights = pair_weights(pairs_dev - 1)
    moved[-1], grad_in, last_weights, fc1_pieces, misc_part = lax.optimization_barrier(
        (moved[-1], grad_in, last_weights, fc1_pieces, misc_part)
    )
    fc1_blocks = blocks_of(fc1_pieces)
    misc_pieces = sum_pieces(misc_part)
    grad_in = grad_in + pair_part(moved[-1], last_weights)
    u_one, inv_one = normalize(inputs_f)
    back_one, gain_grad_one, shift_grad_one = norm_back(grad_in, u_one, inv_one, gain_one)
    grad_tokens = (grad_mid + back_one).astype(bf16)

    sums = jnp.concatenate([jnp.stack([gain_grad_one, shift_grad_one]), dec_flat], axis=0)
    sums, misc_pieces = lax.optimization_barrier((sums, misc_pieces))
    grad_fc1 = side_by_side(fc1_blocks)
    grad_misc = side_by_side(blocks_of(misc_pieces))
    grad_proj = grad_misc[:, :width]
    grad_unp = grad_misc[:, width : width + PP * TF]
    norm_two = grad_misc[:, width + PP * TF : width + PP * TF + 2]
    qkv_all = side_by_side([turn(qkv_part, d) if d else qkv_part for d in range(seq_count)])
    grad_qkv = qkv_all.reshape(shard, pairs, 3, lanes).transpose(0, 2, 1, 3).reshape(shard, 3 * width)

    sums = lax.psum(sums, "scene")
    norm_one = lax.psum(lax.dynamic_slice_in_dim(sums[:2], scene_rank * shard, shard, 1), "seq").T
    dec_flat = sums[2:].reshape(-1)
    ends = (w_dec1.size, w_dec1.size + dh, w_dec1.size + dh + w_dec2.size)
    dec_grads = (
        dec_flat[: ends[0]].reshape(w_dec1.shape),
        dec_flat[ends[0] : ends[1]],
        dec_flat[ends[1] : ends[2]].reshape(w_dec2.shape),
    )
    return (
        block_out,
        decoded,
        grad_tokens,
        norm_one,
        norm_two,
        grad_qkv,
        grad_proj,
        grad_fc1,
        grad_fc2,
        grad_unp,
        dec_grads[0],
        dec_grads[1],
        dec_grads[2],
    )


def solution(mesh):
    rows = P(("scene", "seq"), None)
    shard = P("scene", None)
    in_specs = (
        rows, P("scene"), shard, shard, shard, shard, shard, shard, P(), P(), P(), rows, rows
    )
    out_specs = (rows,) * 3 + (shard,) * 7 + (P(),) * 3
    return jax.shard_map(
        per_device, mesh=mesh, in_specs=in_specs, out_specs=out_specs, check_vma=False
    )
```

```python
import functools

import jax
import jax.numpy as jnp
from jax import lax
from jax.experimental import pallas as pl
from jax.experimental.pallas import tpu as pltpu
from jax.sharding import PartitionSpec as P

H = 16
TF = 32
PP = 4
OUT = 4
TG = 16
IMG_DEV = 576

EPS = 1e-05
NEG_FILL = -1e30
LOG2E = 1.4426950408889634
VMEM_BYTES = 60 * 2**20

NT = (((1,), (1,)), ((), ()))
NN = (((1,), (0,)), ((), ()))
TN = (((0,), (0,)), ((), ()))


def mxu(left, right, dims):
    return lax.dot_general(left, right, dims, preferred_element_type=jnp.float32)


def exact(left, right, dims):
    return lax.dot_general(
        left, right, dims, precision=lax.Precision.HIGHEST, preferred_element_type=jnp.float32
    )


def gelu_parts(v):
    a = jnp.abs(v) * 0.7071067811865476
    t = 1.0 / (1.0 + 0.3275911 * a)
    poly = t * (
        0.254829592
        + t * (-0.284496736 + t * (1.421413741 + t * (-1.453152027 + t * 1.061405429)))
    )
    e = jnp.exp(-a * a)
    tail = 0.5 * poly * e
    cdf = jnp.where(v >= 0.0, 1.0 - tail, tail)
    return v * cdf, cdf + v * (e * 0.3989422804014327)


def pair_keys(block, bias, head, half):
    lane = lax.broadcasted_iota(jnp.int32, block.shape, 1)
    mine = (lane < half) if head == 0 else (lane >= half)
    flag = half if head == 0 else 0
    zero = jnp.zeros_like(block)
    return jnp.where(mine, block, jnp.where(lane == flag, bias, zero))


def pair_queries(block, head, half):
    lane = lax.broadcasted_iota(jnp.int32, block.shape, 1)
    mine = (lane < half) if head == 0 else (lane >= half)
    flag = half if head == 0 else 0
    zero = jnp.zeros_like(block)
    return jnp.where(mine, block, jnp.where(lane == flag, jnp.ones_like(block), zero))


def pair_mask(block, head, half):
    lane = lax.broadcasted_iota(jnp.int32, block.shape, 1)
    mine = (lane < half) if head == 0 else (lane >= half)
    return jnp.where(mine, block, jnp.zeros_like(block))


def attn_fwd_kernel(*refs, first, last, sub, scale):
    q_ref, k_ref, v_ref, bias_ref = refs[:4]
    refs = refs[4:]
    if not first:
        acc_in, peak_in = refs[:2]
        refs = refs[2:]
    out_a, out_b, s_buf, k_buf, vt_buf, acc_buf = refs
    tq, lanes = q_ref.shape
    n = k_ref.shape[0] // sub
    half = lanes // 2
    q = q_ref[...]
    qs = [pair_queries(q, h, half) for h in range(2)]
    ones = jnp.ones((16, sub), jnp.bfloat16)
    for i in range(n):
        rows = slice(i * sub, i * sub + sub)
        kb, bias = k_ref[rows, :], bias_ref[rows, :]
        vt = v_ref[rows, :].T
        for h in range(2):
            k_buf[i, h] = pair_keys(kb, bias, h, half)
            vt_buf[i, h, :half] = vt[h * half : h * half + half]
            vt_buf[i, h, half:] = ones

    def score(j, peak):
        out = []
        for h in range(2):
            s = mxu(k_buf[j, h], qs[h], NT)
            s_buf[j % 2, h] = s
            out.append(jnp.maximum(peak[h], jnp.max(s, axis=0, keepdims=True)))
        return out

    def mix(j, before, peak):
        for h in range(2):
            p = jnp.exp2((s_buf[j % 2, h] - peak[h]) * scale).astype(jnp.bfloat16)
            part = mxu(vt_buf[j, h], p, NN)
            if first and j == 0:
                acc_buf[h] = part
            else:
                fade = jnp.exp2((before[h] - peak[h]) * scale)
                old = acc_in[h] if j == 0 else acc_buf[h]
                acc_buf[h] = old * fade + part

    if first:
        before = [jnp.full((1, tq), -3e38, jnp.float32)] * 2
    else:
        before = [peak_in[h : h + 1, :] for h in range(2)]
    peak = score(0, before)
    for j in range(1, n):
        fresh = score(j, peak)
        mix(j - 1, before, peak)
        before, peak = peak, fresh
    mix(n - 1, before, peak)
    if last:
        outs = []
        for h in range(2):
            acc = acc_buf[h]
            total = acc[half : half + 1]
            outs.append(acc[:half] / total)
            out_b[h : h + 1, :] = peak[h] * scale + jnp.log2(total)
        out_a[...] = jnp.concatenate(outs, axis=0).T.astype(jnp.bfloat16)
    else:
        for h in range(2):
            out_a[h] = acc_buf[h]
            out_b[h : h + 1, :] = peak[h]


def attn_fwd(q_rows, kv_rows, bias, state, last, head_dim):
    lanes = 2 * head_dim
    tq, tk = q_rows.shape[0], kv_rows.shape[0]
    pairs = kv_rows.shape[1] // (3 * lanes)
    width = pairs * lanes
    ext = head_dim + 16
    sub = 256
    first = state is None
    block = lambda rows, off: pl.BlockSpec((rows, lanes), lambda h: (0, 3 * h + off))
    stat = pl.BlockSpec((None, 2, tq), lambda h: (h, 0, 0))
    carry = pl.BlockSpec((None, 2, ext, tq), lambda h: (h, 0, 0, 0))
    stat_shape = jax.ShapeDtypeStruct((pairs, 2, tq), jnp.float32)
    if last:
        out_specs = (pl.BlockSpec((tq, lanes), lambda h: (0, h)), stat)
        out_shape = (jax.ShapeDtypeStruct((tq, width), jnp.bfloat16), stat_shape)
    else:
        out_specs = (carry, stat)
        out_shape = (jax.ShapeDtypeStruct((pairs, 2, ext, tq), jnp.float32), stat_shape)
    return pl.pallas_call(
        functools.partial(
            attn_fwd_kernel, first=first, last=last, sub=sub, scale=head_dim**-0.5 * LOG2E
        ),
        grid=(pairs,),
        in_specs=[block(tq, 0), block(tk, 1), block(tk, 2), pl.BlockSpec((tk, lanes), lambda h: (0, 0))]
        + ([] if first else [carry, stat]),
        out_specs=out_specs,
        out_shape=out_shape,
        scratch_shapes=[
            pltpu.VMEM((2, 2, sub, tq), jnp.float32),
            pltpu.VMEM((tk // sub, 2, sub, lanes), jnp.bfloat16),
            pltpu.VMEM((tk // sub, 2, ext, sub), jnp.bfloat16),
            pltpu.VMEM((2, ext, tq), jnp.float32),
        ],
        compiler_params=pltpu.CompilerParams(vmem_limit_bytes=VMEM_BYTES),
        cost_estimate=pl.CostEstimate(
            flops=16 * tq * tk * width, bytes_accessed=2 * width * (2 * tq + 2 * tk), transcendentals=0
        ),
        name="attn_fwd",
    )(q_rows, kv_rows, kv_rows, bias, *(() if first else state))


def attn_bwd_kernel(*refs, tk, tq, scale, post):
    q_ref, k_ref, v_ref, bias_ref = refs[:4]
    letters = refs[4:-14]
    out_ref = refs[-14]
    s_buf, dp_buf, lse_ref, del_ref, qm, km, dom, kt, qt, dot, dqa, dka, dva = refs[-13:]
    nq = q_ref.shape[0] // tq
    nk = k_ref.shape[0] // tk
    half = q_ref.shape[1] // 2
    for i in range(nk):
        rows = slice(i * tk, i * tk + tk)
        for h in range(2):
            km[h, rows] = pair_keys(k_ref[rows, :], bias_ref[...], h, half)
    for h in range(2):
        qm[h] = pair_queries(q_ref[...], h, half)
    kt[...] = k_ref[...].T
    qt[...] = q_ref[...].T
    per_row = tk // (2 * half)
    for i, letter in enumerate(letters):
        rows = slice(i * tk, i * tk + tk)
        do = letter[:tk, :]
        dot[:, rows] = do.T
        for h in range(2):
            dom[h, rows] = pair_mask(do, h, half)
        count = 4 * per_row
        stat = letter[tk : tk + 3 * count, :].astype(jnp.float32)
        stat = stat[:count] + stat[count : 2 * count] + stat[2 * count :]
        for kind, buf in enumerate((lse_ref, del_ref)):
            for h in range(2):
                at = (kind * 2 + h) * per_row
                buf[h : h + 1, rows] = jnp.concatenate(
                    [stat[at + j : at + j + 1] for j in range(per_row)], axis=1
                )
    for acc in (dqa, dka, dva):
        acc[...] = jnp.zeros(acc.shape, jnp.float32)

    def place(t):
        if isinstance(t, int):
            return t // nq * tk, t % nq * tq, t % 2
        return (
            pl.multiple_of(lax.div(t, nq) * tk, tk),
            pl.multiple_of(lax.rem(t, nq) * tq, tq),
            lax.rem(t, 2),
        )

    def score(t):
        k0, q0, slot = place(t)
        ks, qs = pl.ds(k0, tk), pl.ds(q0, tq)
        vv = v_ref[ks, :]
        for h in range(2):
            s_buf[slot, h] = mxu(km[h, ks, :], qm[h, qs, :], NT)
            dp_buf[slot, h] = mxu(vv, dom[h, qs, :], NT)

    def grads(t):
        k0, q0, slot = place(t)
        ks, qs = pl.ds(k0, tk), pl.ds(q0, tq)
        for h in range(2):
            p = jnp.exp2(s_buf[slot, h] * scale - lse_ref[h : h + 1, qs])
            ds = (p * (dp_buf[slot, h] - del_ref[h : h + 1, qs])).astype(jnp.bfloat16)
            pb = p.astype(jnp.bfloat16)
            r = slice(half * h, half * h + half)
            dqa[r, qs] += mxu(kt[r, ks], ds, NN)
            dva[r, ks] += mxu(dot[r, qs], pb, NT)
            dka[r, ks] += mxu(qt[r, qs], ds, NT)

    score(0)

    def body(t, carry):
        score(t)
        grads(t - 1)
        return carry

    lax.fori_loop(1, nq * nk, body, 0)
    grads(nq * nk - 1)
    lanes = 2 * half
    out_ref[:, :lanes] = (dqa[...] * post).T.astype(jnp.bfloat16)
    out_ref[:, lanes : 2 * lanes] = (dka[...] * post).T.astype(jnp.bfloat16)
    out_ref[:, 2 * lanes :] = dva[...].T.astype(jnp.bfloat16)


def attn_bwd(qkv, letters, bias, pair, head_dim):
    rows = qkv.shape[0]
    tk = bias.shape[0]
    lanes = 2 * head_dim
    block = lambda at: pl.BlockSpec((rows, lanes), lambda h: (0, at))
    return pl.pallas_call(
        functools.partial(
            attn_bwd_kernel, tk=tk, tq=tk, scale=head_dim**-0.5 * LOG2E, post=head_dim**-0.5
        ),
        grid=(1,),
        in_specs=[block(3 * pair), block(3 * pair + 1), block(3 * pair + 2)]
        + [pl.BlockSpec((tk, lanes), lambda h: (0, 0))]
        + [pl.BlockSpec((letters[0].shape[0], lanes), lambda h: (0, pair))] * len(letters),
        out_specs=pl.BlockSpec((rows, 3 * lanes), lambda h: (0, 0)),
        out_shape=jax.ShapeDtypeStruct((rows, 3 * lanes), jnp.bfloat16),
        scratch_shapes=[
            pltpu.VMEM((2, 2, tk, tk), jnp.float32),
            pltpu.VMEM((2, 2, tk, tk), jnp.float32),
            pltpu.VMEM((2, rows), jnp.float32),
            pltpu.VMEM((2, rows), jnp.float32),
            pltpu.VMEM((2, rows, lanes), jnp.bfloat16),
            pltpu.VMEM((2, rows, lanes), jnp.bfloat16),
            pltpu.VMEM((2, rows, lanes), jnp.bfloat16),
            pltpu.VMEM((lanes, rows), jnp.bfloat16),
            pltpu.VMEM((lanes, rows), jnp.bfloat16),
            pltpu.VMEM((lanes, rows), jnp.bfloat16),
            pltpu.VMEM((lanes, rows), jnp.float32),
            pltpu.VMEM((lanes, rows), jnp.float32),
            pltpu.VMEM((lanes, rows), jnp.float32),
        ],
        compiler_params=pltpu.CompilerParams(vmem_limit_bytes=VMEM_BYTES),
        cost_estimate=pl.CostEstimate(
            flops=40 * rows * rows * lanes, bytes_accessed=14 * rows * lanes, transcendentals=0
        ),
        name="attn_bwd",
    )(qkv, qkv, qkv, bias, *letters)


def fc1_kernel(x_ref, w_ref, act_ref, slope_ref):
    act, slope = gelu_parts(mxu(x_ref[...], w_ref[...], NN))
    act_ref[...] = act.astype(jnp.bfloat16)
    slope_ref[...] = slope.astype(jnp.bfloat16)


def fc1_gelu(x, w):
    rows, depth = x.shape
    cols = w.shape[1]
    tile = 512
    spec = pl.BlockSpec((rows, tile), lambda i: (0, i))
    return pl.pallas_call(
        fc1_kernel,
        grid=(cols // tile,),
        in_specs=[
            pl.BlockSpec((rows, depth), lambda i: (0, 0)),
            pl.BlockSpec((depth, tile), lambda i: (0, i)),
        ],
        out_specs=(spec, spec),
        out_shape=(jax.ShapeDtypeStruct((rows, cols), jnp.bfloat16),) * 2,
        compiler_params=pltpu.CompilerParams(vmem_limit_bytes=VMEM_BYTES),
        cost_estimate=pl.CostEstimate(
            flops=2 * rows * cols * depth,
            bytes_accessed=2 * (rows * depth + depth * cols + 2 * rows * cols),
            transcendentals=0,
        ),
        name="fc1_gelu",
    )(x, w)


def normalize(v):
    center = v - jnp.mean(v, axis=-1, keepdims=True)
    spread = jnp.mean(center * center, axis=-1, keepdims=True)
    inv = lax.rsqrt(spread + EPS)
    return center * inv, inv


def norm_back(g, u, inv, gain):
    q = g * gain
    back = inv * (
        q - jnp.mean(q, axis=-1, keepdims=True) - u * jnp.mean(q * u, axis=-1, keepdims=True)
    )
    return back, jnp.sum(g * u, axis=0), jnp.sum(g, axis=0)


def per_device(
    tokens,
    image_count,
    norm_params,
    w_qkv,
    w_proj,
    w_fc1,
    w_fc2,
    w_unpatch,
    w_dec1,
    b_dec1,
    w_dec2,
    cot_out,
    cot_dec,
):
    seq_count = lax.axis_size("seq")
    rank = lax.axis_index("seq")
    scene_rank = lax.axis_index("scene")
    tok_rows, width = tokens.shape
    head_dim = width // H
    cols = width // seq_count
    cells = TG * TG
    bf16, f32 = jnp.bfloat16, jnp.float32
    live_image = image_count[0] // seq_count
    pos = jnp.arange(tok_rows, dtype=jnp.int32)
    row_live = (pos >= IMG_DEV) | (pos < live_image)
    bias = jnp.broadcast_to(
        jnp.where(row_live, 0.0, NEG_FILL).astype(bf16)[:, None], (tok_rows, 2 * head_dim)
    )

    def hop(x, step):
        return lax.ppermute(
            x, "seq", [(i, i + step) for i in range(seq_count) if 0 <= i + step < seq_count]
        )

    def turn(x, step):
        return lax.ppermute(x, "seq", [(i, (i + step) % seq_count) for i in range(seq_count)])

    def ahead(d):
        return lax.rem(rank + d, seq_count)

    def behind(d):
        return lax.rem(rank - d + seq_count, seq_count)

    def piece(x, chunk, size, axis):
        return lax.dynamic_slice_in_dim(x, chunk * size, size, axis)

    cot_row = jnp.pad(cot_dec.reshape(1, -1), ((0, 15), (0, width - cot_dec.size)))
    parcel = jnp.concatenate([tokens, cot_row], axis=0)
    ups, downs = [parcel], [parcel]

    def move_on():
        ups.append(hop(ups[-1], 1))
        downs.append(hop(downs[-1], -1))

    move_on()
    move_on()

    def slot(d):
        pick = ups[d]
        for r in range(d):
            pick = jnp.where(rank == r, downs[d - r], pick)
        return pick

    lanes = 2 * head_dim
    pairs = width // lanes
    shard = w_qkv.shape[0]
    scene_count = width // shard

    def gather(w):
        return lax.all_gather(w.astype(bf16), "scene", axis=0, tiled=True)

    pair_order = w_qkv.astype(bf16).reshape(shard, 3, pairs, lanes).transpose(0, 2, 1, 3)
    first_w = lax.all_gather(
        jnp.concatenate(
            [
                pair_order.reshape(shard, 3 * width),
                w_unpatch.astype(bf16),
                jnp.pad(norm_params.astype(bf16), ((0, 0), (0, 124))),
            ],
            axis=1,
        ),
        "scene",
        axis=0,
        tiled=True,
    )
    qkv_w = first_w[:, : 3 * width]
    unpatch_w = first_w[:, 3 * width : 3 * width + PP * TF]
    norm_full = first_w[:, 3 * width + PP * TF : 3 * width + PP * TF + 4].astype(f32)
    gain_one, shift_one, gain_two, shift_two = (norm_full[:, i] for i in range(4))
    proj_w = gather(w_proj)
    fc1_w = gather(w_fc1)
    fc2_w = gather(w_fc2)

    slots, a1, qkv_rows = [], [], []
    state = None
    for d in range(seq_count):
        slots.append(slot(d))
        u, _ = normalize(slots[d][:tok_rows].astype(f32))
        a = (u * gain_one + shift_one).astype(bf16)
        qkv = mxu(a, qkv_w, NN).astype(bf16)
        a1.append(a)
        qkv_rows.append(qkv)
        if d == 0:
            q_rows = qkv
        state = attn_fwd(q_rows, qkv, bias, state, d == seq_count - 1, head_dim)
        if d + 2 < seq_count:
            ups[d + 2], downs[d + 2], state = lax.optimization_barrier(
                (ups[d + 2], downs[d + 2], state)
            )
            if d + 3 < seq_count:
                move_on()
    mixed, lse = state
    lse = lse.reshape(H, tok_rows)

    def in_turn(blocks):
        out = jnp.zeros((seq_count * tok_rows, blocks[0].shape[1]), blocks[0].dtype)
        for d, block in enumerate(blocks):
            at = jnp.where(rank >= d, d, rank - d + seq_count) * tok_rows
            out = lax.dynamic_update_slice_in_dim(out, block, at, 0)
        return out

    inputs_f = tokens.astype(f32)
    middle = inputs_f + mxu(mixed, proj_w, NN)
    u_two, inv_two = normalize(middle)
    a2 = (u_two * gain_two + shift_two).astype(bf16)
    act, slope = fc1_gelu(a2, fc1_w)
    triplane = (middle[IMG_DEV:] + mxu(act[IMG_DEV:], fc2_w, NN)).astype(bf16)
    tri_rows = tok_rows - IMG_DEV
    planes = mxu(triplane, unpatch_w, NN).astype(bf16)
    all_planes = jnp.zeros((seq_count * tri_rows, PP * TF), bf16)
    for d in range(seq_count):
        got = turn(planes, d) if d else planes
        all_planes = lax.dynamic_update_slice_in_dim(all_planes, got, behind(d) * tri_rows, 0)
    image_live = pos[:IMG_DEV] < live_image
    image_out = jnp.where(
        image_live[:, None], middle[:IMG_DEV] + mxu(act[:IMG_DEV], fc2_w, NN), 0.0
    ).astype(bf16)
    image_out, all_planes = lax.optimization_barrier((image_out, all_planes))
    block_out = jnp.concatenate([image_out, triplane], axis=0)

    cot_rows = jnp.zeros((seq_count, width), bf16)
    for d in range(seq_count):
        chunk = jnp.where(rank >= d, rank - d, d)
        cot_rows = lax.dynamic_update_slice_in_dim(
            cot_rows, slots[d][tok_rows : tok_rows + 1], chunk, 0
        )
    cot_cells = cot_rows[:, : cot_dec.size].reshape(cells, OUT * PP)
    planes_f = all_planes.astype(f32)
    feat = planes_f[:cells] + planes_f[cells : 2 * cells] + planes_f[2 * cells :]
    dh = w_dec1.shape[1]
    eye = jnp.eye(PP, dtype=f32)
    dec1 = jnp.einsum("fh,pq->pfqh", w_dec1, eye).reshape(PP * TF, PP * dh)
    dec2 = jnp.einsum("ho,pq->phoq", w_dec2, eye).reshape(PP * dh, OUT * PP)
    hidden_pre = exact(feat, dec1, NN) + jnp.tile(b_dec1, PP)
    zdec, zslope = gelu_parts(hidden_pre)
    decoded_all = exact(zdec, dec2, NN)
    cells_dev = cells // seq_count
    decoded = lax.dynamic_slice_in_dim(decoded_all, rank * cells_dev, cells_dev, 0)
    cot_f = cot_cells.astype(f32)
    grad_hidden = exact(cot_f, dec2, NT) * zslope
    gfeat = exact(grad_hidden, dec1, NT).astype(bf16)
    plane_grad = lax.dynamic_slice_in_dim(
        jnp.concatenate([gfeat] * 4, axis=0), lax.rem(rank * tri_rows, cells), tri_rows, 0
    )
    grad_unpatch = mxu(triplane, plane_grad, TN)
    grad_tri = mxu(plane_grad, unpatch_w, NT)

    grad_result = jnp.where(row_live[:, None], cot_out.astype(f32), 0.0)
    grad_result = jnp.concatenate([grad_result[:IMG_DEV], grad_result[IMG_DEV:] + grad_tri], axis=0)
    branch = grad_result.astype(bf16)
    fc2_grad = mxu(act, branch, TN).astype(bf16)
    grad_pre = (mxu(branch, fc2_w, NT) * slope.astype(f32)).astype(bf16)
    back_two, gain_grad_two, shift_grad_two = norm_back(
        mxu(grad_pre, fc1_w, NT), u_two, inv_two, gain_two
    )
    grad_mid = grad_result + back_two
    mid_grad = grad_mid.astype(bf16)
    grad_mixed = mxu(mid_grad, proj_w, NT).astype(bf16)
    head_of = (jnp.arange(width) // head_dim)[None, :] == jnp.arange(H)[:, None]
    delta = exact(
        head_of.astype(f32), grad_mixed.astype(f32) * mixed.astype(f32), NT
    )
    pairs_dev = pairs // seq_count
    parts, rest = [], jnp.stack([lse, delta])
    for _ in range(3):
        top = lax.reduce_precision(rest, 8, 7)
        parts.append(top.astype(bf16))
        rest = rest - top
    stats = jnp.stack(parts).reshape(3, 2, pairs, 2, tok_rows // lanes, lanes)
    stats = stats.transpose(0, 1, 3, 4, 2, 5).reshape(-1, width)
    letter = jnp.concatenate(
        [grad_mixed, jnp.pad(stats, ((0, -stats.shape[0] % 16), (0, 0)))], axis=0
    )
    letter, late_a2, late_pre, late_mid, qkv_rows = lax.optimization_barrier(
        (letter, a2, grad_pre, mid_grad, qkv_rows)
    )
    letters = [piece(letter, ahead(d), cols, 1) for d in range(seq_count)]
    letters = [turn(x, d) if d else x for d, x in enumerate(letters)]
    own_all = in_turn([piece(x, rank, 3 * cols, 1) for x in qkv_rows])
    fc1_grad = mxu(late_a2, late_pre, TN).astype(bf16)
    norm_cols = jnp.stack([gain_grad_two, shift_grad_two], axis=1).astype(bf16)
    misc_grad = jnp.concatenate(
        [
            mxu(mixed, late_mid, TN).astype(bf16),
            grad_unpatch.astype(bf16),
            jnp.pad(norm_cols, ((0, 0), (0, 128 * seq_count - PP * TF - 2))),
        ],
        axis=1,
    )

    def over_scene(g):
        return lax.psum_scatter(g, "scene", scatter_dimension=0, tiled=True)

    fc2_part = over_scene(fc2_grad)
    own_all, letters, fc2_part, fc1_grad, misc_grad = lax.optimization_barrier(
        (own_all, letters, fc2_part, fc1_grad, misc_grad)
    )
    fc1_part = over_scene(fc1_grad)
    misc_part = over_scene(misc_grad)

    def send(pieces):
        return [turn(x, d) if d else x for d, x in enumerate(pieces)]

    def cut(part):
        size = part.shape[1] // seq_count
        return [piece(part, ahead(d), size, 1) for d in range(seq_count)]

    def sum_pieces(part):
        return send(cut(part))

    def blocks_of(pieces):
        mine = sum(x.astype(f32) for x in pieces).astype(bf16)
        return [turn(mine, d) if d else mine for d in range(seq_count)]

    def side_by_side(blocks):
        size = blocks[0].shape[1]
        out = jnp.zeros((blocks[0].shape[0], size * seq_count), f32)
        for d, got in enumerate(blocks):
            out = lax.dynamic_update_slice_in_dim(out, got.astype(f32), behind(d) * size, 1)
        return out

    def exchange(mine):
        pieces = [piece(mine, (seq_count - d) % seq_count, tok_rows, 0) for d in range(seq_count)]
        return [turn(x, d) if d else x for d, x in enumerate(pieces)]

    fc2_pieces = sum_pieces(fc2_part)
    moved, head_grads = [], []
    for p in range(pairs_dev):
        mine = attn_bwd(own_all, letters, bias, p, head_dim)
        if p == 0:
            own_all, mine, fc2_pieces = lax.optimization_barrier((own_all, mine, fc2_pieces))
            fc2_blocks = blocks_of(fc2_pieces)
        else:
            decoder = (feat, zdec, cot_f, grad_hidden)
            mine, moved[-1], head_grads[-1], a1, fc2_blocks, fc1_part, misc_part, decoder = (
                lax.optimization_barrier(
                    (mine, moved[-1], head_grads[-1], a1, fc2_blocks, fc1_part, misc_part, decoder)
                )
            )
        head_grads.append(mine)
        moved.append(exchange(mine))
    moved[-1][1], head_grads = lax.optimization_barrier((moved[-1][1], head_grads))
    a1_all = in_turn(a1)
    own_qkv = [mxu(a1_all, part, TN).astype(bf16) for part in head_grads]
    qkv_sum = jnp.concatenate(own_qkv, axis=1)
    grad_fc2 = side_by_side(fc2_blocks)

    def pair_weights(p):
        return jnp.concatenate(
            [
                lax.dynamic_slice_in_dim(
                    qkv_w, behind(d) * 3 * cols + p * 3 * lanes, 3 * lanes, 1
                )
                for d in range(seq_count)
            ],
            axis=1,
        )

    def pair_part(pieces, weights):
        return mxu(jnp.concatenate(pieces, axis=1), weights, NT)

    grad_in = sum(pair_part(moved[p], pair_weights(p)) for p in range(pairs_dev - 1))
    last_weights = pair_weights(pairs_dev - 1)
    feat, zdec, cot_f, grad_hidden = decoder
    grad_w2 = jnp.einsum(
        "phop->ho", exact(zdec, cot_f, TN).reshape(PP, dh, OUT, PP)
    )
    grad_b1 = jnp.sum(jnp.sum(grad_hidden, axis=0).reshape(PP, dh), axis=0)
    grad_w1 = jnp.einsum(
        "pfph->fh", exact(feat, grad_hidden, TN).reshape(PP, TF, PP, dh)
    )
    dec_flat = jnp.concatenate([grad_w1.reshape(-1), grad_b1, grad_w2.reshape(-1)])
    dec_rows = jnp.pad(dec_flat, (0, -dec_flat.size % width)).reshape(-1, width)
    used = dec_rows.shape[0]
    dec_all = lax.all_gather(jnp.pad(dec_rows, ((0, 64 - used), (0, 0))), "scene")
    wide_cut = [
        jnp.concatenate([x, y], axis=1) for x, y in zip(cut(fc1_part), cut(misc_part))
    ]
    moved[-1], grad_in, last_weights, grad_fc2, wide_cut, dec_rows = lax.optimization_barrier(
        (moved[-1], grad_in, last_weights, grad_fc2, wide_cut, dec_rows)
    )
    grad_in = grad_in + pair_part(moved[-1], last_weights)
    u_one, inv_one = normalize(inputs_f)
    back_one, gain_grad_one, shift_grad_one = norm_back(grad_in, u_one, inv_one, gain_one)
    grad_tokens = (grad_mid + back_one).astype(bf16)

    sums = jnp.stack([gain_grad_one, shift_grad_one])
    sums, wide_cut, qkv_sum, dec_all = lax.optimization_barrier((sums, wide_cut, qkv_sum, dec_all))
    wide_blocks = blocks_of(send(wide_cut))
    edge = w_fc1.shape[1] // seq_count
    grad_fc1 = side_by_side([x[:, :edge] for x in wide_blocks])
    grad_misc = side_by_side([x[:, edge:] for x in wide_blocks])
    grad_proj = grad_misc[:, :width]
    grad_unp = grad_misc[:, width : width + PP * TF]
    norm_two = grad_misc[:, width + PP * TF : width + PP * TF + 2]
    qkv_part = over_scene(qkv_sum)
    qkv_all = side_by_side([turn(qkv_part, d) if d else qkv_part for d in range(seq_count)])
    grad_qkv = qkv_all.reshape(shard, pairs, 3, lanes).transpose(0, 2, 1, 3).reshape(shard, 3 * width)

    sums = lax.psum(sums, "scene")
    norm_one = lax.psum(lax.dynamic_slice_in_dim(sums, scene_rank * shard, shard, 1), "seq").T
    dec_flat = jnp.sum(dec_all[:, :used], axis=0).reshape(-1)
    ends = (w_dec1.size, w_dec1.size + dh, w_dec1.size + dh + w_dec2.size)
    dec_grads = (
        dec_flat[: ends[0]].reshape(w_dec1.shape),
        dec_flat[ends[0] : ends[1]],
        dec_flat[ends[1] : ends[2]].reshape(w_dec2.shape),
    )
    return (
        block_out,
        decoded,
        grad_tokens,
        norm_one,
        norm_two,
        grad_qkv,
        grad_proj,
        grad_fc1,
        grad_fc2,
        grad_unp,
        dec_grads[0],
        dec_grads[1],
        dec_grads[2],
    )


def solution(mesh):
    rows = P(("scene", "seq"), None)
    shard = P("scene", None)
    in_specs = (
        rows, P("scene"), shard, shard, shard, shard, shard, shard, P(), P(), P(), rows, rows
    )
    out_specs = (rows,) * 3 + (shard,) * 7 + (P(),) * 3
    return jax.shard_map(
        per_device, mesh=mesh, in_specs=in_specs, out_specs=out_specs, check_vma=False
    )
```

```python
import functools

import jax
import jax.numpy as jnp
from jax import lax
from jax.experimental import pallas as pl
from jax.experimental.pallas import tpu as pltpu
from jax.sharding import PartitionSpec as P

H = 16
TF = 32
PP = 4
OUT = 4
TG = 16
IMG_DEV = 576

EPS = 1e-05
NEG_FILL = -1e30
LOG2E = 1.4426950408889634
VMEM_BYTES = 60 * 2**20

NT = (((1,), (1,)), ((), ()))
NN = (((1,), (0,)), ((), ()))
TN = (((0,), (0,)), ((), ()))


def mxu(left, right, dims):
    return lax.dot_general(left, right, dims, preferred_element_type=jnp.float32)


def exact(left, right, dims):
    return lax.dot_general(
        left, right, dims, precision=lax.Precision.HIGHEST, preferred_element_type=jnp.float32
    )


def gelu_parts(v):
    a = jnp.abs(v) * 0.7071067811865476
    t = 1.0 / (1.0 + 0.3275911 * a)
    poly = t * (
        0.254829592
        + t * (-0.284496736 + t * (1.421413741 + t * (-1.453152027 + t * 1.061405429)))
    )
    e = jnp.exp(-a * a)
    tail = 0.5 * poly * e
    cdf = jnp.where(v >= 0.0, 1.0 - tail, tail)
    return v * cdf, cdf + v * (e * 0.3989422804014327)


def pair_keys(block, bias, head, half):
    lane = lax.broadcasted_iota(jnp.int32, block.shape, 1)
    mine = (lane < half) if head == 0 else (lane >= half)
    flag = half if head == 0 else 0
    zero = jnp.zeros_like(block)
    return jnp.where(mine, block, jnp.where(lane == flag, bias, zero))


def pair_queries(block, head, half):
    lane = lax.broadcasted_iota(jnp.int32, block.shape, 1)
    mine = (lane < half) if head == 0 else (lane >= half)
    flag = half if head == 0 else 0
    zero = jnp.zeros_like(block)
    return jnp.where(mine, block, jnp.where(lane == flag, jnp.ones_like(block), zero))


def pair_mask(block, head, half):
    lane = lax.broadcasted_iota(jnp.int32, block.shape, 1)
    mine = (lane < half) if head == 0 else (lane >= half)
    return jnp.where(mine, block, jnp.zeros_like(block))


def attn_fwd_kernel(*refs, first, last, sub, scale):
    q_ref, k_ref, v_ref, bias_ref = refs[:4]
    refs = refs[4:]
    if not first:
        acc_in, peak_in = refs[:2]
        refs = refs[2:]
    out_a, out_b, s_buf, k_buf, vt_buf, acc_buf = refs
    tq, lanes = q_ref.shape
    n = k_ref.shape[0] // sub
    half = lanes // 2
    q = q_ref[...]
    qs = [pair_queries(q, h, half) for h in range(2)]
    ones = jnp.ones((16, sub), jnp.bfloat16)
    for i in range(n):
        rows = slice(i * sub, i * sub + sub)
        kb, bias = k_ref[rows, :], bias_ref[rows, :]
        vt = v_ref[rows, :].T
        for h in range(2):
            k_buf[i, h] = pair_keys(kb, bias, h, half)
            vt_buf[i, h, :half] = vt[h * half : h * half + half]
            vt_buf[i, h, half:] = ones

    def score(j, peak):
        out = []
        for h in range(2):
            s = mxu(k_buf[j, h], qs[h], NT)
            s_buf[j % 2, h] = s
            out.append(jnp.maximum(peak[h], jnp.max(s, axis=0, keepdims=True)))
        return out

    def mix(j, before, peak):
        for h in range(2):
            p = jnp.exp2((s_buf[j % 2, h] - peak[h]) * scale).astype(jnp.bfloat16)
            part = mxu(vt_buf[j, h], p, NN)
            if first and j == 0:
                acc_buf[h] = part
            else:
                fade = jnp.exp2((before[h] - peak[h]) * scale)
                old = acc_in[h] if j == 0 else acc_buf[h]
                acc_buf[h] = old * fade + part

    if first:
        before = [jnp.full((1, tq), -3e38, jnp.float32)] * 2
    else:
        before = [peak_in[h : h + 1, :] for h in range(2)]
    peak = score(0, before)
    for j in range(1, n):
        fresh = score(j, peak)
        mix(j - 1, before, peak)
        before, peak = peak, fresh
    mix(n - 1, before, peak)
    if last:
        outs = []
        for h in range(2):
            acc = acc_buf[h]
            total = acc[half : half + 1]
            outs.append(acc[:half] / total)
            out_b[h : h + 1, :] = peak[h] * scale + jnp.log2(total)
        out_a[...] = jnp.concatenate(outs, axis=0).T.astype(jnp.bfloat16)
    else:
        for h in range(2):
            out_a[h] = acc_buf[h]
            out_b[h : h + 1, :] = peak[h]


def attn_fwd(q_rows, kv_rows, bias, state, last, head_dim):
    lanes = 2 * head_dim
    tq, tk = q_rows.shape[0], kv_rows.shape[0]
    pairs = kv_rows.shape[1] // (3 * lanes)
    width = pairs * lanes
    ext = head_dim + 16
    sub = 256
    first = state is None
    block = lambda rows, off: pl.BlockSpec((rows, lanes), lambda h: (0, 3 * h + off))
    stat = pl.BlockSpec((None, 2, tq), lambda h: (h, 0, 0))
    carry = pl.BlockSpec((None, 2, ext, tq), lambda h: (h, 0, 0, 0))
    stat_shape = jax.ShapeDtypeStruct((pairs, 2, tq), jnp.float32)
    if last:
        out_specs = (pl.BlockSpec((tq, lanes), lambda h: (0, h)), stat)
        out_shape = (jax.ShapeDtypeStruct((tq, width), jnp.bfloat16), stat_shape)
    else:
        out_specs = (carry, stat)
        out_shape = (jax.ShapeDtypeStruct((pairs, 2, ext, tq), jnp.float32), stat_shape)
    return pl.pallas_call(
        functools.partial(
            attn_fwd_kernel, first=first, last=last, sub=sub, scale=head_dim**-0.5 * LOG2E
        ),
        grid=(pairs,),
        in_specs=[block(tq, 0), block(tk, 1), block(tk, 2), pl.BlockSpec((tk, lanes), lambda h: (0, 0))]
        + ([] if first else [carry, stat]),
        out_specs=out_specs,
        out_shape=out_shape,
        scratch_shapes=[
            pltpu.VMEM((2, 2, sub, tq), jnp.float32),
            pltpu.VMEM((tk // sub, 2, sub, lanes), jnp.bfloat16),
            pltpu.VMEM((tk // sub, 2, ext, sub), jnp.bfloat16),
            pltpu.VMEM((2, ext, tq), jnp.float32),
        ],
        compiler_params=pltpu.CompilerParams(vmem_limit_bytes=VMEM_BYTES),
        cost_estimate=pl.CostEstimate(
            flops=16 * tq * tk * width, bytes_accessed=2 * width * (2 * tq + 2 * tk), transcendentals=0
        ),
        name="attn_fwd",
    )(q_rows, kv_rows, kv_rows, bias, *(() if first else state))


def attn_bwd_kernel(*refs, tk, tq, scale, post):
    q_ref, k_ref, v_ref, bias_ref = refs[:4]
    letters = refs[4:-14]
    out_ref = refs[-14]
    s_buf, dp_buf, lse_ref, del_ref, qm, km, dom, kt, qt, dot, dqa, dka, dva = refs[-13:]
    nq = q_ref.shape[0] // tq
    nk = k_ref.shape[0] // tk
    half = q_ref.shape[1] // 2
    for i in range(nk):
        rows = slice(i * tk, i * tk + tk)
        for h in range(2):
            km[h, rows] = pair_keys(k_ref[rows, :], bias_ref[...], h, half)
    for h in range(2):
        qm[h] = pair_queries(q_ref[...], h, half)
    kt[...] = k_ref[...].T
    qt[...] = q_ref[...].T
    per_row = tk // (2 * half)
    for i, letter in enumerate(letters):
        rows = slice(i * tk, i * tk + tk)
        do = letter[:tk, :]
        dot[:, rows] = do.T
        for h in range(2):
            dom[h, rows] = pair_mask(do, h, half)
        count = 4 * per_row
        stat = letter[tk : tk + 3 * count, :].astype(jnp.float32)
        stat = stat[:count] + stat[count : 2 * count] + stat[2 * count :]
        for kind, buf in enumerate((lse_ref, del_ref)):
            for h in range(2):
                at = (kind * 2 + h) * per_row
                buf[h : h + 1, rows] = jnp.concatenate(
                    [stat[at + j : at + j + 1] for j in range(per_row)], axis=1
                )
    for acc in (dqa, dka, dva):
        acc[...] = jnp.zeros(acc.shape, jnp.float32)

    def place(t):
        if isinstance(t, int):
            return t // nq * tk, t % nq * tq, t % 2
        return (
            pl.multiple_of(lax.div(t, nq) * tk, tk),
            pl.multiple_of(lax.rem(t, nq) * tq, tq),
            lax.rem(t, 2),
        )

    def score(t):
        k0, q0, slot = place(t)
        ks, qs = pl.ds(k0, tk), pl.ds(q0, tq)
        vv = v_ref[ks, :]
        for h in range(2):
            s_buf[slot, h] = mxu(km[h, ks, :], qm[h, qs, :], NT)
            dp_buf[slot, h] = mxu(vv, dom[h, qs, :], NT)

    def grads(t):
        k0, q0, slot = place(t)
        ks, qs = pl.ds(k0, tk), pl.ds(q0, tq)
        for h in range(2):
            p = jnp.exp2(s_buf[slot, h] * scale - lse_ref[h : h + 1, qs])
            ds = (p * (dp_buf[slot, h] - del_ref[h : h + 1, qs])).astype(jnp.bfloat16)
            pb = p.astype(jnp.bfloat16)
            r = slice(half * h, half * h + half)
            dqa[r, qs] += mxu(kt[r, ks], ds, NN)
            dva[r, ks] += mxu(dot[r, qs], pb, NT)
            dka[r, ks] += mxu(qt[r, qs], ds, NT)

    score(0)

    def body(t, carry):
        score(t)
        grads(t - 1)
        return carry

    lax.fori_loop(1, nq * nk, body, 0)
    grads(nq * nk - 1)
    lanes = 2 * half
    out_ref[:, :lanes] = (dqa[...] * post).T.astype(jnp.bfloat16)
    out_ref[:, lanes : 2 * lanes] = (dka[...] * post).T.astype(jnp.bfloat16)
    out_ref[:, 2 * lanes :] = dva[...].T.astype(jnp.bfloat16)


def attn_bwd(qkv, letters, bias, pair, head_dim):
    rows = qkv.shape[0]
    tk = bias.shape[0]
    lanes = 2 * head_dim
    block = lambda at: pl.BlockSpec((rows, lanes), lambda h: (0, at))
    return pl.pallas_call(
        functools.partial(
            attn_bwd_kernel, tk=tk, tq=tk, scale=head_dim**-0.5 * LOG2E, post=head_dim**-0.5
        ),
        grid=(1,),
        in_specs=[block(3 * pair), block(3 * pair + 1), block(3 * pair + 2)]
        + [pl.BlockSpec((tk, lanes), lambda h: (0, 0))]
        + [pl.BlockSpec((letters[0].shape[0], lanes), lambda h: (0, pair))] * len(letters),
        out_specs=pl.BlockSpec((rows, 3 * lanes), lambda h: (0, 0)),
        out_shape=jax.ShapeDtypeStruct((rows, 3 * lanes), jnp.bfloat16),
        scratch_shapes=[
            pltpu.VMEM((2, 2, tk, tk), jnp.float32),
            pltpu.VMEM((2, 2, tk, tk), jnp.float32),
            pltpu.VMEM((2, rows), jnp.float32),
            pltpu.VMEM((2, rows), jnp.float32),
            pltpu.VMEM((2, rows, lanes), jnp.bfloat16),
            pltpu.VMEM((2, rows, lanes), jnp.bfloat16),
            pltpu.VMEM((2, rows, lanes), jnp.bfloat16),
            pltpu.VMEM((lanes, rows), jnp.bfloat16),
            pltpu.VMEM((lanes, rows), jnp.bfloat16),
            pltpu.VMEM((lanes, rows), jnp.bfloat16),
            pltpu.VMEM((lanes, rows), jnp.float32),
            pltpu.VMEM((lanes, rows), jnp.float32),
            pltpu.VMEM((lanes, rows), jnp.float32),
        ],
        compiler_params=pltpu.CompilerParams(vmem_limit_bytes=VMEM_BYTES),
        cost_estimate=pl.CostEstimate(
            flops=40 * rows * rows * lanes, bytes_accessed=14 * rows * lanes, transcendentals=0
        ),
        name="attn_bwd",
    )(qkv, qkv, qkv, bias, *letters)


def fc1_kernel(x_ref, w_ref, act_ref, slope_ref):
    act, slope = gelu_parts(mxu(x_ref[...], w_ref[...], NN))
    act_ref[...] = act.astype(jnp.bfloat16)
    slope_ref[...] = slope.astype(jnp.bfloat16)


def fc1_gelu(x, w):
    rows, depth = x.shape
    cols = w.shape[1]
    tile = 512
    spec = pl.BlockSpec((rows, tile), lambda i: (0, i))
    return pl.pallas_call(
        fc1_kernel,
        grid=(cols // tile,),
        in_specs=[
            pl.BlockSpec((rows, depth), lambda i: (0, 0)),
            pl.BlockSpec((depth, tile), lambda i: (0, i)),
        ],
        out_specs=(spec, spec),
        out_shape=(jax.ShapeDtypeStruct((rows, cols), jnp.bfloat16),) * 2,
        compiler_params=pltpu.CompilerParams(vmem_limit_bytes=VMEM_BYTES),
        cost_estimate=pl.CostEstimate(
            flops=2 * rows * cols * depth,
            bytes_accessed=2 * (rows * depth + depth * cols + 2 * rows * cols),
            transcendentals=0,
        ),
        name="fc1_gelu",
    )(x, w)


def normalize(v):
    center = v - jnp.mean(v, axis=-1, keepdims=True)
    spread = jnp.mean(center * center, axis=-1, keepdims=True)
    inv = lax.rsqrt(spread + EPS)
    return center * inv, inv


def norm_back(g, u, inv, gain):
    q = g * gain
    back = inv * (
        q - jnp.mean(q, axis=-1, keepdims=True) - u * jnp.mean(q * u, axis=-1, keepdims=True)
    )
    return back, jnp.sum(g * u, axis=0), jnp.sum(g, axis=0)


def per_device(
    tokens,
    image_count,
    norm_params,
    w_qkv,
    w_proj,
    w_fc1,
    w_fc2,
    w_unpatch,
    w_dec1,
    b_dec1,
    w_dec2,
    cot_out,
    cot_dec,
):
    seq_count = lax.axis_size("seq")
    rank = lax.axis_index("seq")
    scene_rank = lax.axis_index("scene")
    tok_rows, width = tokens.shape
    head_dim = width // H
    cols = width // seq_count
    cells = TG * TG
    bf16, f32 = jnp.bfloat16, jnp.float32
    live_image = image_count[0] // seq_count
    pos = jnp.arange(tok_rows, dtype=jnp.int32)
    row_live = (pos >= IMG_DEV) | (pos < live_image)
    bias = jnp.broadcast_to(
        jnp.where(row_live, 0.0, NEG_FILL).astype(bf16)[:, None], (tok_rows, 2 * head_dim)
    )

    def hop(x, step):
        return lax.ppermute(
            x, "seq", [(i, i + step) for i in range(seq_count) if 0 <= i + step < seq_count]
        )

    def turn(x, step):
        return lax.ppermute(x, "seq", [(i, (i + step) % seq_count) for i in range(seq_count)])

    def ahead(d):
        return lax.rem(rank + d, seq_count)

    def behind(d):
        return lax.rem(rank - d + seq_count, seq_count)

    def piece(x, chunk, size, axis):
        return lax.dynamic_slice_in_dim(x, chunk * size, size, axis)

    cot_row = jnp.pad(cot_dec.reshape(1, -1), ((0, 15), (0, width - cot_dec.size)))
    parcel = jnp.concatenate([tokens, cot_row], axis=0)
    ups, downs = [parcel], [parcel]

    def move_on():
        ups.append(hop(ups[-1], 1))
        downs.append(hop(downs[-1], -1))

    move_on()
    move_on()

    def slot(d):
        pick = ups[d]
        for r in range(d):
            pick = jnp.where(rank == r, downs[d - r], pick)
        return pick

    lanes = 2 * head_dim
    pairs = width // lanes
    shard = w_qkv.shape[0]
    scene_count = width // shard

    def gather(w):
        return lax.all_gather(w.astype(bf16), "scene", axis=0, tiled=True)

    pair_order = w_qkv.astype(bf16).reshape(shard, 3, pairs, lanes).transpose(0, 2, 1, 3)
    first_w = lax.all_gather(
        jnp.concatenate(
            [
                pair_order.reshape(shard, 3 * width),
                w_unpatch.astype(bf16),
                jnp.pad(norm_params.astype(bf16), ((0, 0), (0, 124))),
            ],
            axis=1,
        ),
        "scene",
        axis=0,
        tiled=True,
    )
    qkv_w = first_w[:, : 3 * width]
    unpatch_w = first_w[:, 3 * width : 3 * width + PP * TF]
    norm_full = first_w[:, 3 * width + PP * TF : 3 * width + PP * TF + 4].astype(f32)
    gain_one, shift_one, gain_two, shift_two = (norm_full[:, i] for i in range(4))
    proj_w = gather(w_proj)
    fc1_w = gather(w_fc1)
    fc2_w = gather(w_fc2)

    slots, a1, qkv_rows = [], [], []
    state = None
    for d in range(seq_count):
        slots.append(slot(d))
        u, _ = normalize(slots[d][:tok_rows].astype(f32))
        a = (u * gain_one + shift_one).astype(bf16)
        qkv = mxu(a, qkv_w, NN).astype(bf16)
        a1.append(a)
        qkv_rows.append(qkv)
        if d == 0:
            q_rows = qkv
        state = attn_fwd(q_rows, qkv, bias, state, d == seq_count - 1, head_dim)
        if d + 2 < seq_count:
            ups[d + 2], downs[d + 2], state = lax.optimization_barrier(
                (ups[d + 2], downs[d + 2], state)
            )
            if d + 3 < seq_count:
                move_on()
    mixed, lse = state
    lse = lse.reshape(H, tok_rows)

    def in_turn(blocks):
        out = jnp.zeros((seq_count * tok_rows, blocks[0].shape[1]), blocks[0].dtype)
        for d, block in enumerate(blocks):
            at = jnp.where(rank >= d, d, rank - d + seq_count) * tok_rows
            out = lax.dynamic_update_slice_in_dim(out, block, at, 0)
        return out

    inputs_f = tokens.astype(f32)
    middle = inputs_f + mxu(mixed, proj_w, NN)
    u_two, inv_two = normalize(middle)
    a2 = (u_two * gain_two + shift_two).astype(bf16)
    act, slope = fc1_gelu(a2, fc1_w)
    triplane = (middle[IMG_DEV:] + mxu(act[IMG_DEV:], fc2_w, NN)).astype(bf16)
    tri_rows = tok_rows - IMG_DEV
    planes = mxu(triplane, unpatch_w, NN).astype(bf16)
    all_planes = jnp.zeros((seq_count * tri_rows, PP * TF), bf16)
    for d in range(seq_count):
        got = turn(planes, d) if d else planes
        all_planes = lax.dynamic_update_slice_in_dim(all_planes, got, behind(d) * tri_rows, 0)
    image_live = pos[:IMG_DEV] < live_image
    image_out = jnp.where(
        image_live[:, None], middle[:IMG_DEV] + mxu(act[:IMG_DEV], fc2_w, NN), 0.0
    ).astype(bf16)
    image_out, all_planes = lax.optimization_barrier((image_out, all_planes))

    cot_rows = jnp.zeros((seq_count, width), bf16)
    for d in range(seq_count):
        chunk = jnp.where(rank >= d, rank - d, d)
        cot_rows = lax.dynamic_update_slice_in_dim(
            cot_rows, slots[d][tok_rows : tok_rows + 1], chunk, 0
        )
    cot_cells = cot_rows[:, : cot_dec.size].reshape(cells, OUT * PP)
    planes_f = all_planes.astype(f32)
    feat = planes_f[:cells] + planes_f[cells : 2 * cells] + planes_f[2 * cells :]
    dh = w_dec1.shape[1]
    eye = jnp.eye(PP, dtype=f32)
    dec1 = jnp.einsum("fh,pq->pfqh", w_dec1, eye).reshape(PP * TF, PP * dh)
    dec2 = jnp.einsum("ho,pq->phoq", w_dec2, eye).reshape(PP * dh, OUT * PP)
    hidden_pre = exact(feat, dec1, NN) + jnp.tile(b_dec1, PP)
    zdec, zslope = gelu_parts(hidden_pre)
    decoded_all = exact(zdec, dec2, NN)
    cells_dev = cells // seq_count
    cot_f = cot_cells.astype(f32)
    grad_hidden = exact(cot_f, dec2, NT) * zslope
    gfeat = exact(grad_hidden, dec1, NT).astype(bf16)
    plane_grad = lax.dynamic_slice_in_dim(
        jnp.concatenate([gfeat] * 4, axis=0), lax.rem(rank * tri_rows, cells), tri_rows, 0
    )
    grad_unpatch = mxu(triplane, plane_grad, TN)
    grad_tri = mxu(plane_grad, unpatch_w, NT)

    grad_result = jnp.where(row_live[:, None], cot_out.astype(f32), 0.0)
    grad_result = jnp.concatenate([grad_result[:IMG_DEV], grad_result[IMG_DEV:] + grad_tri], axis=0)
    branch = grad_result.astype(bf16)
    fc2_grad = mxu(act, branch, TN).astype(bf16)
    grad_pre = (mxu(branch, fc2_w, NT) * slope.astype(f32)).astype(bf16)
    back_two, gain_grad_two, shift_grad_two = norm_back(
        mxu(grad_pre, fc1_w, NT), u_two, inv_two, gain_two
    )
    grad_mid = grad_result + back_two
    mid_grad = grad_mid.astype(bf16)
    grad_mixed = mxu(mid_grad, proj_w, NT).astype(bf16)
    head_of = (jnp.arange(width) // head_dim)[None, :] == jnp.arange(H)[:, None]
    delta = exact(
        head_of.astype(f32), grad_mixed.astype(f32) * mixed.astype(f32), NT
    )
    pairs_dev = pairs // seq_count
    parts, rest = [], jnp.stack([lse, delta])
    for _ in range(3):
        top = lax.reduce_precision(rest, 8, 7)
        parts.append(top.astype(bf16))
        rest = rest - top
    stats = jnp.stack(parts).reshape(3, 2, pairs, 2, tok_rows // lanes, lanes)
    stats = stats.transpose(0, 1, 3, 4, 2, 5).reshape(-1, width)
    letter = jnp.concatenate(
        [grad_mixed, jnp.pad(stats, ((0, -stats.shape[0] % 16), (0, 0)))], axis=0
    )
    letter, late_a2, late_pre, late_mid, qkv_rows = lax.optimization_barrier(
        (letter, a2, grad_pre, mid_grad, qkv_rows)
    )
    letters = [piece(letter, ahead(d), cols, 1) for d in range(seq_count)]
    letters = [turn(x, d) if d else x for d, x in enumerate(letters)]
    own_all = in_turn([piece(x, rank, 3 * cols, 1) for x in qkv_rows])
    fc1_grad = mxu(late_a2, late_pre, TN).astype(bf16)
    norm_cols = jnp.stack([gain_grad_two, shift_grad_two], axis=1).astype(bf16)
    misc_grad = jnp.concatenate(
        [
            mxu(mixed, late_mid, TN).astype(bf16),
            grad_unpatch.astype(bf16),
            jnp.pad(norm_cols, ((0, 0), (0, 128 * seq_count - PP * TF - 2))),
        ],
        axis=1,
    )

    def over_scene(g):
        return lax.psum_scatter(g, "scene", scatter_dimension=0, tiled=True)

    fc2_part = over_scene(fc2_grad)
    own_all, letters, fc2_part, fc1_grad, misc_grad = lax.optimization_barrier(
        (own_all, letters, fc2_part, fc1_grad, misc_grad)
    )
    fc1_part = over_scene(fc1_grad)
    misc_part = over_scene(misc_grad)

    def send(pieces):
        return [turn(x, d) if d else x for d, x in enumerate(pieces)]

    def cut(part):
        size = part.shape[1] // seq_count
        return [piece(part, ahead(d), size, 1) for d in range(seq_count)]

    def sum_pieces(part):
        return send(cut(part))

    def blocks_of(pieces):
        mine = sum(x.astype(f32) for x in pieces).astype(bf16)
        return [turn(mine, d) if d else mine for d in range(seq_count)]

    def side_by_side(blocks):
        size = blocks[0].shape[1]
        out = jnp.zeros((blocks[0].shape[0], size * seq_count), f32)
        for d, got in enumerate(blocks):
            out = lax.dynamic_update_slice_in_dim(out, got.astype(f32), behind(d) * size, 1)
        return out

    def cut_rows(mine):
        return [piece(mine, (seq_count - d) % seq_count, tok_rows, 0) for d in range(seq_count)]

    fc2_pieces = sum_pieces(fc2_part)
    moved, head_grads = [], []
    for p in range(pairs_dev):
        mine = attn_bwd(own_all, letters, bias, p, head_dim)
        if p == 0:
            own_all, mine, fc2_pieces = lax.optimization_barrier((own_all, mine, fc2_pieces))
            fc2_blocks = blocks_of(fc2_pieces)
        else:
            decoder = (feat, zdec, cot_f, grad_hidden, qkv_w)
            mine, moved[-1], head_grads[-1], a1, fc2_blocks, fc1_part, misc_part, decoder = (
                lax.optimization_barrier(
                    (mine, moved[-1], head_grads[-1], a1, fc2_blocks, fc1_part, misc_part, decoder)
                )
            )
        head_grads.append(mine)
        moved.append(send(cut_rows(mine)))
    moved[-1][1], head_grads, decoder = lax.optimization_barrier(
        (moved[-1][1], head_grads, decoder)
    )
    a1_all = in_turn(a1)
    own_qkv = [mxu(a1_all, part, TN).astype(bf16) for part in head_grads]
    qkv_sum = jnp.concatenate(own_qkv, axis=1)
    grad_fc2 = side_by_side(fc2_blocks)

    feat, zdec, cot_f, grad_hidden, late_w = decoder
    def pair_weights(p):
        return jnp.concatenate(
            [
                lax.dynamic_slice_in_dim(
                    late_w, behind(d) * 3 * cols + p * 3 * lanes, 3 * lanes, 1
                )
                for d in range(seq_count)
            ],
            axis=1,
        )

    def pair_part(pieces, weights):
        return mxu(jnp.concatenate(pieces, axis=1), weights, NT)

    grad_in = sum(pair_part(moved[p], pair_weights(p)) for p in range(pairs_dev - 1))
    last_weights = pair_weights(pairs_dev - 1)
    grad_w2 = jnp.einsum(
        "phop->ho", exact(zdec, cot_f, TN).reshape(PP, dh, OUT, PP)
    )
    grad_b1 = jnp.sum(jnp.sum(grad_hidden, axis=0).reshape(PP, dh), axis=0)
    grad_w1 = jnp.einsum(
        "pfph->fh", exact(feat, grad_hidden, TN).reshape(PP, TF, PP, dh)
    )
    dec_flat = jnp.concatenate([grad_w1.reshape(-1), grad_b1, grad_w2.reshape(-1)])
    dec_rows = jnp.pad(dec_flat, (0, -dec_flat.size % width)).reshape(-1, width)
    used = dec_rows.shape[0]
    wide_cut = [
        jnp.concatenate([x, y], axis=1) for x, y in zip(cut(fc1_part), cut(misc_part))
    ]
    qkv_part = over_scene(qkv_sum)
    moved[-1], grad_in, last_weights, grad_fc2, wide_cut, qkv_sum, dec_rows = (
        lax.optimization_barrier(
            (moved[-1], grad_in, last_weights, grad_fc2, wide_cut, qkv_sum, dec_rows)
        )
    )
    dec_all = lax.all_gather(jnp.pad(dec_rows, ((0, 64 - used), (0, 0))), "scene")
    grad_in = grad_in + pair_part(moved[-1], last_weights)
    u_one, inv_one = normalize(inputs_f)
    back_one, gain_grad_one, shift_grad_one = norm_back(grad_in, u_one, inv_one, gain_one)
    grad_tokens = (grad_mid + back_one).astype(bf16)

    sums = jnp.stack([gain_grad_one, shift_grad_one])
    sums, wide_cut = lax.optimization_barrier((sums, wide_cut))
    wide_pieces = send(wide_cut)
    sums = lax.psum(sums, "scene")
    sums, wide_pieces, qkv_part, image_out, triplane, decoded_all = lax.optimization_barrier(
        (sums, wide_pieces, qkv_part, image_out, triplane, decoded_all)
    )
    block_out = jnp.concatenate([image_out, triplane], axis=0)
    decoded = lax.dynamic_slice_in_dim(decoded_all, rank * cells_dev, cells_dev, 0)
    qkv_blocks = send([qkv_part] * seq_count)
    wide_blocks = blocks_of(wide_pieces)
    edge = w_fc1.shape[1] // seq_count
    grad_fc1 = side_by_side([x[:, :edge] for x in wide_blocks])
    grad_misc = side_by_side([x[:, edge:] for x in wide_blocks])
    grad_proj = grad_misc[:, :width]
    grad_unp = grad_misc[:, width : width + PP * TF]
    norm_two = grad_misc[:, width + PP * TF : width + PP * TF + 2]
    qkv_all = side_by_side(qkv_blocks)
    grad_qkv = qkv_all.reshape(shard, pairs, 3, lanes).transpose(0, 2, 1, 3).reshape(shard, 3 * width)

    norm_one = lax.psum(lax.dynamic_slice_in_dim(sums, scene_rank * shard, shard, 1), "seq").T
    dec_flat = jnp.sum(dec_all[:, :used], axis=0).reshape(-1)
    ends = (w_dec1.size, w_dec1.size + dh, w_dec1.size + dh + w_dec2.size)
    dec_grads = (
        dec_flat[: ends[0]].reshape(w_dec1.shape),
        dec_flat[ends[0] : ends[1]],
        dec_flat[ends[1] : ends[2]].reshape(w_dec2.shape),
    )
    return (
        block_out,
        decoded,
        grad_tokens,
        norm_one,
        norm_two,
        grad_qkv,
        grad_proj,
        grad_fc1,
        grad_fc2,
        grad_unp,
        dec_grads[0],
        dec_grads[1],
        dec_grads[2],
    )


def solution(mesh):
    rows = P(("scene", "seq"), None)
    shard = P("scene", None)
    in_specs = (
        rows, P("scene"), shard, shard, shard, shard, shard, shard, P(), P(), P(), rows, rows
    )
    out_specs = (rows,) * 3 + (shard,) * 7 + (P(),) * 3
    return jax.shard_map(
        per_device, mesh=mesh, in_specs=in_specs, out_specs=out_specs, check_vma=False
    )
```

```python
import functools

import jax
import jax.numpy as jnp
from jax import lax
from jax.experimental import pallas as pl
from jax.experimental.pallas import tpu as pltpu
from jax.sharding import PartitionSpec as P

H = 16
TF = 32
PP = 4
OUT = 4
TG = 16
IMG_DEV = 576

EPS = 1e-05
NEG_FILL = -1e30
LOG2E = 1.4426950408889634
VMEM_BYTES = 60 * 2**20

NT = (((1,), (1,)), ((), ()))
NN = (((1,), (0,)), ((), ()))
TN = (((0,), (0,)), ((), ()))


def mxu(left, right, dims):
    return lax.dot_general(left, right, dims, preferred_element_type=jnp.float32)


def exact(left, right, dims):
    return lax.dot_general(
        left, right, dims, precision=lax.Precision.HIGHEST, preferred_element_type=jnp.float32
    )


def gelu_parts(v):
    a = jnp.abs(v) * 0.7071067811865476
    t = 1.0 / (1.0 + 0.3275911 * a)
    poly = t * (
        0.254829592
        + t * (-0.284496736 + t * (1.421413741 + t * (-1.453152027 + t * 1.061405429)))
    )
    e = jnp.exp(-a * a)
    tail = 0.5 * poly * e
    cdf = jnp.where(v >= 0.0, 1.0 - tail, tail)
    return v * cdf, cdf + v * (e * 0.3989422804014327)


def pair_keys(block, bias, head, half):
    lane = lax.broadcasted_iota(jnp.int32, block.shape, 1)
    mine = (lane < half) if head == 0 else (lane >= half)
    flag = half if head == 0 else 0
    zero = jnp.zeros_like(block)
    return jnp.where(mine, block, jnp.where(lane == flag, bias, zero))


def pair_queries(block, head, half):
    lane = lax.broadcasted_iota(jnp.int32, block.shape, 1)
    mine = (lane < half) if head == 0 else (lane >= half)
    flag = half if head == 0 else 0
    zero = jnp.zeros_like(block)
    return jnp.where(mine, block, jnp.where(lane == flag, jnp.ones_like(block), zero))


def pair_mask(block, head, half):
    lane = lax.broadcasted_iota(jnp.int32, block.shape, 1)
    mine = (lane < half) if head == 0 else (lane >= half)
    return jnp.where(mine, block, jnp.zeros_like(block))


def attn_fwd_kernel(*refs, first, last, sub, scale):
    q_ref, k_ref, v_ref, bias_ref = refs[:4]
    refs = refs[4:]
    if not first:
        acc_in, peak_in = refs[:2]
        refs = refs[2:]
    out_a, out_b, s_buf, k_buf, vt_buf, acc_buf = refs
    tq, lanes = q_ref.shape
    n = k_ref.shape[0] // sub
    half = lanes // 2
    q = q_ref[...]
    qs = [pair_queries(q, h, half) for h in range(2)]
    ones = jnp.ones((16, sub), jnp.bfloat16)
    for i in range(n):
        rows = slice(i * sub, i * sub + sub)
        kb, bias = k_ref[rows, :], bias_ref[rows, :]
        vt = v_ref[rows, :].T
        for h in range(2):
            k_buf[i, h] = pair_keys(kb, bias, h, half)
            vt_buf[i, h, :half] = vt[h * half : h * half + half]
            vt_buf[i, h, half:] = ones

    def score(j, peak):
        out = []
        for h in range(2):
            s = mxu(k_buf[j, h], qs[h], NT)
            s_buf[j % 2, h] = s
            out.append(jnp.maximum(peak[h], jnp.max(s, axis=0, keepdims=True)))
        return out

    def mix(j, before, peak):
        for h in range(2):
            p = jnp.exp2((s_buf[j % 2, h] - peak[h]) * scale).astype(jnp.bfloat16)
            part = mxu(vt_buf[j, h], p, NN)
            if first and j == 0:
                acc_buf[h] = part
            else:
                fade = jnp.exp2((before[h] - peak[h]) * scale)
                old = acc_in[h] if j == 0 else acc_buf[h]
                acc_buf[h] = old * fade + part

    if first:
        before = [jnp.full((1, tq), -3e38, jnp.float32)] * 2
    else:
        before = [peak_in[h : h + 1, :] for h in range(2)]
    peak = score(0, before)
    for j in range(1, n):
        fresh = score(j, peak)
        mix(j - 1, before, peak)
        before, peak = peak, fresh
    mix(n - 1, before, peak)
    if last:
        outs = []
        for h in range(2):
            acc = acc_buf[h]
            total = acc[half : half + 1]
            outs.append(acc[:half] / total)
            out_b[h : h + 1, :] = peak[h] * scale + jnp.log2(total)
        out_a[...] = jnp.concatenate(outs, axis=0).T.astype(jnp.bfloat16)
    else:
        for h in range(2):
            out_a[h] = acc_buf[h]
            out_b[h : h + 1, :] = peak[h]


def attn_fwd(q_rows, kv_rows, bias, state, last, head_dim):
    lanes = 2 * head_dim
    tq, tk = q_rows.shape[0], kv_rows.shape[0]
    pairs = kv_rows.shape[1] // (3 * lanes)
    width = pairs * lanes
    ext = head_dim + 16
    sub = 256
    first = state is None
    block = lambda rows, off: pl.BlockSpec((rows, lanes), lambda h: (0, 3 * h + off))
    stat = pl.BlockSpec((None, 2, tq), lambda h: (h, 0, 0))
    carry = pl.BlockSpec((None, 2, ext, tq), lambda h: (h, 0, 0, 0))
    stat_shape = jax.ShapeDtypeStruct((pairs, 2, tq), jnp.float32)
    if last:
        out_specs = (pl.BlockSpec((tq, lanes), lambda h: (0, h)), stat)
        out_shape = (jax.ShapeDtypeStruct((tq, width), jnp.bfloat16), stat_shape)
    else:
        out_specs = (carry, stat)
        out_shape = (jax.ShapeDtypeStruct((pairs, 2, ext, tq), jnp.float32), stat_shape)
    return pl.pallas_call(
        functools.partial(
            attn_fwd_kernel, first=first, last=last, sub=sub, scale=head_dim**-0.5 * LOG2E
        ),
        grid=(pairs,),
        in_specs=[block(tq, 0), block(tk, 1), block(tk, 2), pl.BlockSpec((tk, lanes), lambda h: (0, 0))]
        + ([] if first else [carry, stat]),
        out_specs=out_specs,
        out_shape=out_shape,
        scratch_shapes=[
            pltpu.VMEM((2, 2, sub, tq), jnp.float32),
            pltpu.VMEM((tk // sub, 2, sub, lanes), jnp.bfloat16),
            pltpu.VMEM((tk // sub, 2, ext, sub), jnp.bfloat16),
            pltpu.VMEM((2, ext, tq), jnp.float32),
        ],
        compiler_params=pltpu.CompilerParams(vmem_limit_bytes=VMEM_BYTES),
        cost_estimate=pl.CostEstimate(
            flops=16 * tq * tk * width, bytes_accessed=2 * width * (2 * tq + 2 * tk), transcendentals=0
        ),
        name="attn_fwd",
    )(q_rows, kv_rows, kv_rows, bias, *(() if first else state))


def attn_bwd_kernel(*refs, tk, tq, scale, post):
    q_ref, k_ref, v_ref, bias_ref = refs[:4]
    letters = refs[4:-14]
    out_ref = refs[-14]
    s_buf, dp_buf, lse_ref, del_ref, qm, km, dom, kt, qt, dot, dqa, dka, dva = refs[-13:]
    nq = q_ref.shape[0] // tq
    nk = k_ref.shape[0] // tk
    half = q_ref.shape[1] // 2
    for i in range(nk):
        rows = slice(i * tk, i * tk + tk)
        for h in range(2):
            km[h, rows] = pair_keys(k_ref[rows, :], bias_ref[...], h, half)
    for h in range(2):
        qm[h] = pair_queries(q_ref[...], h, half)
    kt[...] = k_ref[...].T
    qt[...] = q_ref[...].T
    per_row = tk // (2 * half)
    for i, letter in enumerate(letters):
        rows = slice(i * tk, i * tk + tk)
        do = letter[:tk, :]
        dot[:, rows] = do.T
        for h in range(2):
            dom[h, rows] = pair_mask(do, h, half)
        count = 4 * per_row
        stat = letter[tk : tk + 3 * count, :].astype(jnp.float32)
        stat = stat[:count] + stat[count : 2 * count] + stat[2 * count :]
        for kind, buf in enumerate((lse_ref, del_ref)):
            for h in range(2):
                at = (kind * 2 + h) * per_row
                buf[h : h + 1, rows] = jnp.concatenate(
                    [stat[at + j : at + j + 1] for j in range(per_row)], axis=1
                )
    for acc in (dqa, dka, dva):
        acc[...] = jnp.zeros(acc.shape, jnp.float32)

    def place(t):
        if isinstance(t, int):
            return t // nq * tk, t % nq * tq, t % 2
        return (
            pl.multiple_of(lax.div(t, nq) * tk, tk),
            pl.multiple_of(lax.rem(t, nq) * tq, tq),
            lax.rem(t, 2),
        )

    def score(t):
        k0, q0, slot = place(t)
        ks, qs = pl.ds(k0, tk), pl.ds(q0, tq)
        vv = v_ref[ks, :]
        for h in range(2):
            s_buf[slot, h] = mxu(km[h, ks, :], qm[h, qs, :], NT)
            dp_buf[slot, h] = mxu(vv, dom[h, qs, :], NT)

    def grads(t):
        k0, q0, slot = place(t)
        ks, qs = pl.ds(k0, tk), pl.ds(q0, tq)
        for h in range(2):
            p = jnp.exp2(s_buf[slot, h] * scale - lse_ref[h : h + 1, qs])
            ds = (p * (dp_buf[slot, h] - del_ref[h : h + 1, qs])).astype(jnp.bfloat16)
            pb = p.astype(jnp.bfloat16)
            r = slice(half * h, half * h + half)
            dqa[r, qs] += mxu(kt[r, ks], ds, NN)
            dva[r, ks] += mxu(dot[r, qs], pb, NT)
            dka[r, ks] += mxu(qt[r, qs], ds, NT)

    score(0)

    def body(t, carry):
        score(t)
        grads(t - 1)
        return carry

    lax.fori_loop(1, nq * nk, body, 0)
    grads(nq * nk - 1)
    lanes = 2 * half
    out_ref[:, :lanes] = (dqa[...] * post).T.astype(jnp.bfloat16)
    out_ref[:, lanes : 2 * lanes] = (dka[...] * post).T.astype(jnp.bfloat16)
    out_ref[:, 2 * lanes :] = dva[...].T.astype(jnp.bfloat16)


def attn_bwd(qkv, letters, bias, pair, head_dim):
    rows = qkv.shape[0]
    tk = bias.shape[0]
    lanes = 2 * head_dim
    block = lambda at: pl.BlockSpec((rows, lanes), lambda h: (0, at))
    return pl.pallas_call(
        functools.partial(
            attn_bwd_kernel, tk=tk, tq=tk, scale=head_dim**-0.5 * LOG2E, post=head_dim**-0.5
        ),
        grid=(1,),
        in_specs=[block(3 * pair), block(3 * pair + 1), block(3 * pair + 2)]
        + [pl.BlockSpec((tk, lanes), lambda h: (0, 0))]
        + [pl.BlockSpec((letters[0].shape[0], lanes), lambda h: (0, pair))] * len(letters),
        out_specs=pl.BlockSpec((rows, 3 * lanes), lambda h: (0, 0)),
        out_shape=jax.ShapeDtypeStruct((rows, 3 * lanes), jnp.bfloat16),
        scratch_shapes=[
            pltpu.VMEM((2, 2, tk, tk), jnp.float32),
            pltpu.VMEM((2, 2, tk, tk), jnp.float32),
            pltpu.VMEM((2, rows), jnp.float32),
            pltpu.VMEM((2, rows), jnp.float32),
            pltpu.VMEM((2, rows, lanes), jnp.bfloat16),
            pltpu.VMEM((2, rows, lanes), jnp.bfloat16),
            pltpu.VMEM((2, rows, lanes), jnp.bfloat16),
            pltpu.VMEM((lanes, rows), jnp.bfloat16),
            pltpu.VMEM((lanes, rows), jnp.bfloat16),
            pltpu.VMEM((lanes, rows), jnp.bfloat16),
            pltpu.VMEM((lanes, rows), jnp.float32),
            pltpu.VMEM((lanes, rows), jnp.float32),
            pltpu.VMEM((lanes, rows), jnp.float32),
        ],
        compiler_params=pltpu.CompilerParams(vmem_limit_bytes=VMEM_BYTES),
        cost_estimate=pl.CostEstimate(
            flops=40 * rows * rows * lanes, bytes_accessed=14 * rows * lanes, transcendentals=0
        ),
        name="attn_bwd",
    )(qkv, qkv, qkv, bias, *letters)


def fc1_kernel(x_ref, w_ref, act_ref, slope_ref):
    act, slope = gelu_parts(mxu(x_ref[...], w_ref[...], NN))
    act_ref[...] = act.astype(jnp.bfloat16)
    slope_ref[...] = slope.astype(jnp.bfloat16)


def fc1_gelu(x, w):
    rows, depth = x.shape
    cols = w.shape[1]
    tile = 512
    spec = pl.BlockSpec((rows, tile), lambda i: (0, i))
    return pl.pallas_call(
        fc1_kernel,
        grid=(cols // tile,),
        in_specs=[
            pl.BlockSpec((rows, depth), lambda i: (0, 0)),
            pl.BlockSpec((depth, tile), lambda i: (0, i)),
        ],
        out_specs=(spec, spec),
        out_shape=(jax.ShapeDtypeStruct((rows, cols), jnp.bfloat16),) * 2,
        compiler_params=pltpu.CompilerParams(vmem_limit_bytes=VMEM_BYTES),
        cost_estimate=pl.CostEstimate(
            flops=2 * rows * cols * depth,
            bytes_accessed=2 * (rows * depth + depth * cols + 2 * rows * cols),
            transcendentals=0,
        ),
        name="fc1_gelu",
    )(x, w)


def normalize(v):
    center = v - jnp.mean(v, axis=-1, keepdims=True)
    spread = jnp.mean(center * center, axis=-1, keepdims=True)
    inv = lax.rsqrt(spread + EPS)
    return center * inv, inv


def norm_back(g, u, inv, gain):
    q = g * gain
    back = inv * (
        q - jnp.mean(q, axis=-1, keepdims=True) - u * jnp.mean(q * u, axis=-1, keepdims=True)
    )
    return back, jnp.sum(g * u, axis=0), jnp.sum(g, axis=0)


def per_device(
    tokens,
    image_count,
    norm_params,
    w_qkv,
    w_proj,
    w_fc1,
    w_fc2,
    w_unpatch,
    w_dec1,
    b_dec1,
    w_dec2,
    cot_out,
    cot_dec,
):
    seq_count = lax.axis_size("seq")
    rank = lax.axis_index("seq")
    scene_rank = lax.axis_index("scene")
    tok_rows, width = tokens.shape
    head_dim = width // H
    cols = width // seq_count
    cells = TG * TG
    bf16, f32 = jnp.bfloat16, jnp.float32
    live_image = image_count[0] // seq_count
    pos = jnp.arange(tok_rows, dtype=jnp.int32)
    row_live = (pos >= IMG_DEV) | (pos < live_image)
    bias = jnp.broadcast_to(
        jnp.where(row_live, 0.0, NEG_FILL).astype(bf16)[:, None], (tok_rows, 2 * head_dim)
    )

    def hop(x, step):
        return lax.ppermute(
            x, "seq", [(i, i + step) for i in range(seq_count) if 0 <= i + step < seq_count]
        )

    def turn(x, step):
        return lax.ppermute(x, "seq", [(i, (i + step) % seq_count) for i in range(seq_count)])

    def ahead(d):
        return lax.rem(rank + d, seq_count)

    def behind(d):
        return lax.rem(rank - d + seq_count, seq_count)

    def piece(x, chunk, size, axis):
        return lax.dynamic_slice_in_dim(x, chunk * size, size, axis)

    cot_row = jnp.pad(cot_dec.reshape(1, -1), ((0, 15), (0, width - cot_dec.size)))
    parcel = jnp.concatenate([tokens, cot_row], axis=0)
    ups, downs = [parcel], [parcel]

    def move_on():
        ups.append(hop(ups[-1], 1))
        downs.append(hop(downs[-1], -1))

    move_on()
    move_on()

    def slot(d):
        pick = ups[d]
        for r in range(d):
            pick = jnp.where(rank == r, downs[d - r], pick)
        return pick

    lanes = 2 * head_dim
    pairs = width // lanes
    shard = w_qkv.shape[0]
    scene_count = width // shard

    def gather(w):
        return lax.all_gather(w.astype(bf16), "scene", axis=0, tiled=True)

    pair_order = w_qkv.astype(bf16).reshape(shard, 3, pairs, lanes).transpose(0, 2, 1, 3)
    first_w = lax.all_gather(
        jnp.concatenate(
            [
                pair_order.reshape(shard, 3 * width),
                w_unpatch.astype(bf16),
                jnp.pad(norm_params.astype(bf16), ((0, 0), (0, 124))),
            ],
            axis=1,
        ),
        "scene",
        axis=0,
        tiled=True,
    )
    qkv_w = first_w[:, : 3 * width]
    unpatch_w = first_w[:, 3 * width : 3 * width + PP * TF]
    norm_full = first_w[:, 3 * width + PP * TF : 3 * width + PP * TF + 4].astype(f32)
    gain_one, shift_one, gain_two, shift_two = (norm_full[:, i] for i in range(4))
    proj_w = gather(w_proj)
    fc1_w = gather(w_fc1)
    fc2_w = gather(w_fc2)

    slots, a1, qkv_rows = [], [], []
    state = None
    for d in range(seq_count):
        slots.append(slot(d))
        u, _ = normalize(slots[d][:tok_rows].astype(f32))
        a = (u * gain_one + shift_one).astype(bf16)
        qkv = mxu(a, qkv_w, NN).astype(bf16)
        a1.append(a)
        qkv_rows.append(qkv)
        if d == 0:
            q_rows = qkv
        state = attn_fwd(q_rows, qkv, bias, state, d == seq_count - 1, head_dim)
        if d + 2 < seq_count:
            ups[d + 2], downs[d + 2], state = lax.optimization_barrier(
                (ups[d + 2], downs[d + 2], state)
            )
            if d + 3 < seq_count:
                move_on()
    mixed, lse = state
    lse = lse.reshape(H, tok_rows)

    def in_turn(blocks):
        out = jnp.zeros((seq_count * tok_rows, blocks[0].shape[1]), blocks[0].dtype)
        for d, block in enumerate(blocks):
            at = jnp.where(rank >= d, d, rank - d + seq_count) * tok_rows
            out = lax.dynamic_update_slice_in_dim(out, block, at, 0)
        return out

    inputs_f = tokens.astype(f32)
    middle = inputs_f + mxu(mixed, proj_w, NN)
    u_two, inv_two = normalize(middle)
    a2 = (u_two * gain_two + shift_two).astype(bf16)
    act, slope = fc1_gelu(a2, fc1_w)
    triplane = (middle[IMG_DEV:] + mxu(act[IMG_DEV:], fc2_w, NN)).astype(bf16)
    tri_rows = tok_rows - IMG_DEV
    planes = mxu(triplane, unpatch_w, NN).astype(bf16)
    all_planes = jnp.zeros((seq_count * tri_rows, PP * TF), bf16)
    for d in range(seq_count):
        got = turn(planes, d) if d else planes
        all_planes = lax.dynamic_update_slice_in_dim(all_planes, got, behind(d) * tri_rows, 0)
    image_live = pos[:IMG_DEV] < live_image
    image_out = jnp.where(
        image_live[:, None], middle[:IMG_DEV] + mxu(act[:IMG_DEV], fc2_w, NN), 0.0
    ).astype(bf16)
    image_out, all_planes = lax.optimization_barrier((image_out, all_planes))

    cot_rows = jnp.zeros((seq_count, width), bf16)
    for d in range(seq_count):
        chunk = jnp.where(rank >= d, rank - d, d)
        cot_rows = lax.dynamic_update_slice_in_dim(
            cot_rows, slots[d][tok_rows : tok_rows + 1], chunk, 0
        )
    cot_cells = cot_rows[:, : cot_dec.size].reshape(cells, OUT * PP)
    planes_f = all_planes.astype(f32)
    feat = planes_f[:cells] + planes_f[cells : 2 * cells] + planes_f[2 * cells :]
    dh = w_dec1.shape[1]
    eye = jnp.eye(PP, dtype=f32)
    dec1 = jnp.einsum("fh,pq->pfqh", w_dec1, eye).reshape(PP * TF, PP * dh)
    dec2 = jnp.einsum("ho,pq->phoq", w_dec2, eye).reshape(PP * dh, OUT * PP)
    hidden_pre = exact(feat, dec1, NN) + jnp.tile(b_dec1, PP)
    zdec, zslope = gelu_parts(hidden_pre)
    decoded_all = exact(zdec, dec2, NN)
    cells_dev = cells // seq_count
    cot_f = cot_cells.astype(f32)
    grad_hidden = exact(cot_f, dec2, NT) * zslope
    gfeat = exact(grad_hidden, dec1, NT).astype(bf16)
    plane_grad = lax.dynamic_slice_in_dim(
        jnp.concatenate([gfeat] * 4, axis=0), lax.rem(rank * tri_rows, cells), tri_rows, 0
    )
    grad_unpatch = mxu(triplane, plane_grad, TN)
    grad_tri = mxu(plane_grad, unpatch_w, NT)

    grad_result = jnp.where(row_live[:, None], cot_out.astype(f32), 0.0)
    grad_result = jnp.concatenate([grad_result[:IMG_DEV], grad_result[IMG_DEV:] + grad_tri], axis=0)
    branch = grad_result.astype(bf16)
    fc2_grad = mxu(act, branch, TN).astype(bf16)
    grad_pre = (mxu(branch, fc2_w, NT) * slope.astype(f32)).astype(bf16)
    back_two, gain_grad_two, shift_grad_two = norm_back(
        mxu(grad_pre, fc1_w, NT), u_two, inv_two, gain_two
    )
    grad_mid = grad_result + back_two
    mid_grad = grad_mid.astype(bf16)
    grad_mixed = mxu(mid_grad, proj_w, NT).astype(bf16)
    head_of = (jnp.arange(width) // head_dim)[None, :] == jnp.arange(H)[:, None]
    delta = exact(
        head_of.astype(f32), grad_mixed.astype(f32) * mixed.astype(f32), NT
    )
    pairs_dev = pairs // seq_count
    parts, rest = [], jnp.stack([lse, delta])
    for _ in range(3):
        top = lax.reduce_precision(rest, 8, 7)
        parts.append(top.astype(bf16))
        rest = rest - top
    stats = jnp.stack(parts).reshape(3, 2, pairs, 2, tok_rows // lanes, lanes)
    stats = stats.transpose(0, 1, 3, 4, 2, 5).reshape(-1, width)
    letter = jnp.concatenate(
        [grad_mixed, jnp.pad(stats, ((0, -stats.shape[0] % 16), (0, 0)))], axis=0
    )
    letter, late_a2, late_pre, late_mid, qkv_rows = lax.optimization_barrier(
        (letter, a2, grad_pre, mid_grad, qkv_rows)
    )
    letters = [piece(letter, ahead(d), cols, 1) for d in range(seq_count)]
    letters = [turn(x, d) if d else x for d, x in enumerate(letters)]
    own_all = in_turn([piece(x, rank, 3 * cols, 1) for x in qkv_rows])
    fc1_grad = mxu(late_a2, late_pre, TN).astype(bf16)
    norm_cols = jnp.stack([gain_grad_two, shift_grad_two], axis=1).astype(bf16)
    misc_grad = jnp.concatenate(
        [
            mxu(mixed, late_mid, TN).astype(bf16),
            grad_unpatch.astype(bf16),
            jnp.pad(norm_cols, ((0, 0), (0, 128 * seq_count - PP * TF - 2))),
        ],
        axis=1,
    )

    def over_scene(g):
        return lax.psum_scatter(g, "scene", scatter_dimension=0, tiled=True)

    fc2_part = over_scene(fc2_grad)
    own_all, letters, fc2_part, fc1_grad, misc_grad = lax.optimization_barrier(
        (own_all, letters, fc2_part, fc1_grad, misc_grad)
    )
    fc1_part = over_scene(fc1_grad)
    misc_part = over_scene(misc_grad)

    def send(pieces):
        return [turn(x, d) if d else x for d, x in enumerate(pieces)]

    def cut(part):
        size = part.shape[1] // seq_count
        return [piece(part, ahead(d), size, 1) for d in range(seq_count)]

    def sum_pieces(part):
        return send(cut(part))

    def blocks_of(pieces):
        mine = sum(x.astype(f32) for x in pieces).astype(bf16)
        return [turn(mine, d) if d else mine for d in range(seq_count)]

    def side_by_side(blocks):
        size = blocks[0].shape[1]
        out = jnp.zeros((blocks[0].shape[0], size * seq_count), f32)
        for d, got in enumerate(blocks):
            out = lax.dynamic_update_slice_in_dim(out, got.astype(f32), behind(d) * size, 1)
        return out

    def cut_rows(mine):
        return [piece(mine, (seq_count - d) % seq_count, tok_rows, 0) for d in range(seq_count)]

    fc2_pieces = sum_pieces(fc2_part)
    moved, head_grads = [], []
    for p in range(pairs_dev):
        mine = attn_bwd(own_all, letters, bias, p, head_dim)
        if p == 0:
            own_all, mine, fc2_pieces = lax.optimization_barrier((own_all, mine, fc2_pieces))
            fc2_blocks = blocks_of(fc2_pieces)
        else:
            decoder = (feat, zdec, cot_f, grad_hidden, qkv_w)
            mine, moved[-1], head_grads[-1], a1, fc2_blocks, fc1_part, misc_part, decoder = (
                lax.optimization_barrier(
                    (mine, moved[-1], head_grads[-1], a1, fc2_blocks, fc1_part, misc_part, decoder)
                )
            )
        head_grads.append(mine)
        moved.append(send(cut_rows(mine)))
    moved[-1][1], head_grads, decoder = lax.optimization_barrier(
        (moved[-1][1], head_grads, decoder)
    )
    a1_all = in_turn(a1)
    own_qkv = [mxu(a1_all, part, TN).astype(bf16) for part in head_grads]
    qkv_sum = jnp.concatenate(own_qkv, axis=1)
    grad_fc2 = side_by_side(fc2_blocks)

    feat, zdec, cot_f, grad_hidden, late_w = decoder
    def pair_weights(p):
        return jnp.concatenate(
            [
                lax.dynamic_slice_in_dim(
                    late_w, behind(d) * 3 * cols + p * 3 * lanes, 3 * lanes, 1
                )
                for d in range(seq_count)
            ],
            axis=1,
        )

    def pair_part(pieces, weights):
        return mxu(jnp.concatenate(pieces, axis=1), weights, NT)

    grad_in = sum(pair_part(moved[p], pair_weights(p)) for p in range(pairs_dev - 1))
    last_weights = pair_weights(pairs_dev - 1)
    grad_w2 = jnp.einsum(
        "phop->ho", exact(zdec, cot_f, TN).reshape(PP, dh, OUT, PP)
    )
    grad_b1 = jnp.sum(jnp.sum(grad_hidden, axis=0).reshape(PP, dh), axis=0)
    grad_w1 = jnp.einsum(
        "pfph->fh", exact(feat, grad_hidden, TN).reshape(PP, TF, PP, dh)
    )
    dec_flat = jnp.concatenate([grad_w1.reshape(-1), grad_b1, grad_w2.reshape(-1)])
    dec_rows = jnp.pad(dec_flat, (0, -dec_flat.size % width)).reshape(-1, width)
    used = dec_rows.shape[0]
    wide_cut = [
        jnp.concatenate([x, y], axis=1) for x, y in zip(cut(fc1_part), cut(misc_part))
    ]
    qkv_part = over_scene(qkv_sum)
    moved[-1], grad_in, last_weights, grad_fc2, wide_cut, qkv_sum, dec_rows = (
        lax.optimization_barrier(
            (moved[-1], grad_in, last_weights, grad_fc2, wide_cut, qkv_sum, dec_rows)
        )
    )
    dec_all = lax.all_gather(jnp.pad(dec_rows, ((0, 64 - used), (0, 0))), "scene")
    grad_in = grad_in + pair_part(moved[-1], last_weights)
    u_one, inv_one = normalize(inputs_f)
    back_one, gain_grad_one, shift_grad_one = norm_back(grad_in, u_one, inv_one, gain_one)
    grad_tokens = (grad_mid + back_one).astype(bf16)

    sums = jnp.stack([gain_grad_one, shift_grad_one])
    sums, wide_cut = lax.optimization_barrier((sums, wide_cut))
    wide_pieces = send(wide_cut)
    sums = lax.psum(sums, "scene")
    sums, wide_pieces, qkv_part, image_out, triplane, decoded_all = lax.optimization_barrier(
        (sums, wide_pieces, qkv_part, image_out, triplane, decoded_all)
    )
    block_out = jnp.concatenate([image_out, triplane], axis=0)
    decoded = lax.dynamic_slice_in_dim(decoded_all, rank * cells_dev, cells_dev, 0)
    qkv_blocks = send([qkv_part] * seq_count)
    norm_parts, rest = [], lax.dynamic_slice_in_dim(sums, scene_rank * shard, shard, 1).T
    for _ in range(3):
        top = lax.reduce_precision(rest, 8, 7)
        norm_parts.append(top.astype(bf16))
        rest = rest - top
    mine = jnp.concatenate(
        [
            sum(x.astype(f32) for x in wide_pieces).astype(bf16),
            jnp.pad(jnp.concatenate(norm_parts, axis=1), ((0, 0), (0, 122))),
        ],
        axis=1,
    )
    wide_blocks = send([mine] * seq_count)
    last = mine.shape[1] - 128
    norm_all = jnp.zeros((seq_count, shard, 6), f32)
    for d, got in enumerate(wide_blocks):
        norm_all = lax.dynamic_update_slice_in_dim(
            norm_all, got[None, :, last : last + 6].astype(f32), behind(d), 0
        )
    norm_all = jnp.sum(norm_all, axis=0)
    norm_one = norm_all[:, :2] + norm_all[:, 2:4] + norm_all[:, 4:]
    edge = w_fc1.shape[1] // seq_count
    grad_fc1 = side_by_side([x[:, :edge] for x in wide_blocks])
    grad_misc = side_by_side([x[:, edge:last] for x in wide_blocks])
    grad_proj = grad_misc[:, :width]
    grad_unp = grad_misc[:, width : width + PP * TF]
    norm_two = grad_misc[:, width + PP * TF : width + PP * TF + 2]
    qkv_all = side_by_side(qkv_blocks)
    grad_qkv = qkv_all.reshape(shard, pairs, 3, lanes).transpose(0, 2, 1, 3).reshape(shard, 3 * width)

    dec_flat = jnp.sum(dec_all[:, :used], axis=0).reshape(-1)
    ends = (w_dec1.size, w_dec1.size + dh, w_dec1.size + dh + w_dec2.size)
    dec_grads = (
        dec_flat[: ends[0]].reshape(w_dec1.shape),
        dec_flat[ends[0] : ends[1]],
        dec_flat[ends[1] : ends[2]].reshape(w_dec2.shape),
    )
    return (
        block_out,
        decoded,
        grad_tokens,
        norm_one,
        norm_two,
        grad_qkv,
        grad_proj,
        grad_fc1,
        grad_fc2,
        grad_unp,
        dec_grads[0],
        dec_grads[1],
        dec_grads[2],
    )


def solution(mesh):
    rows = P(("scene", "seq"), None)
    shard = P("scene", None)
    in_specs = (
        rows, P("scene"), shard, shard, shard, shard, shard, shard, P(), P(), P(), rows, rows
    )
    out_specs = (rows,) * 3 + (shard,) * 7 + (P(),) * 3
    return jax.shard_map(
        per_device, mesh=mesh, in_specs=in_specs, out_specs=out_specs, check_vma=False
    )
```
